256 devices in a mesh: dp: 2 (over z_lo), ctx: 32 (over z_hi, y, core), tensor: 4 (over x).
Axes of the slice: x: 4, y: 4, z: 8 (z_hi: 4, z_lo: 2; z = z_hi * 2 + z_lo), core: 2. Of those that a mesh axis runs over, the one named last changes fastest.
Arguments:
- queries: bfloat16 [8192, 3072], P(('dp', 'ctx'), 'tensor'), parts along dimension 0, may hold values from -6 to 6
- keys: bfloat16 [8192, 512], P(('dp', 'ctx'), 'tensor'), parts along dimension 0, may hold values from -6 to 6
- values: bfloat16 [8192, 512], P(('dp', 'ctx'), 'tensor'), parts along dimension 0, may hold values from -6 to 6
- cache_keys: bfloat16 [8192, 512], P(('dp', 'ctx'), 'tensor'), parts along dimension 0, may hold values from -6 to 6
- cache_values: bfloat16 [8192, 512], P(('dp', 'ctx'), 'tensor'), parts along dimension 0, may hold values from -6 to 6
- residual: bfloat16 [8192, 3072], P(('dp', 'ctx'), 'tensor'), parts along dimension 0, may hold values from -36 to 36
- norm_gain: float32 [3072], replicated, may hold values from 0.1 to 1.9
- w_gate: bfloat16 [3072, 65536], P(None, ('ctx', 'tensor')), may hold values from -0.109375 to 0.109375
- w_up: bfloat16 [3072, 65536], P(None, ('ctx', 'tensor')), may hold values from -0.109375 to 0.109375
- w_down: bfloat16 [65536, 3072], P(('ctx', 'tensor')), may hold values from -0.0625 to 0.0625
- expert_ids: int32 [8192, 2], P(('dp', 'ctx')), parts along dimension 0, may hold values from 0 to 7, all different within a row; in each aligned block of 128 rows (0 to 127, 128 to 255, ...) at most 36 rows name the same one
- gate_weights: float32 [8192, 2], P(('dp', 'ctx')), parts along dimension 0, may hold values from 0.1 to 0.9
Outputs:
- layer_out: bfloat16 [8192, 3072], P(('dp', 'ctx'), 'tensor'), parts along dimension 0
The draws below stay inside these ranges and needn't reach their ends.
There are 2 independent parts, one for each index of `dp`. The reference program is written for one: setup_inputs(seed, part) draws one part's arguments, and reference() takes and returns one part's arrays. A program takes and returns all parts, laid end to end along the dimension named above; an argument that names none is the same for every part. Nothing has to cross between parts.
Inputs may be any that keep to these rules, and one draw needn't show every extreme that they name: `expert_ids`: among the 128 rows of each index of ctx (aligned blocks of rows), no expert is named by more than 36 rows, a bound that some block reaches.
All inputs are finite; a program needn't handle non-finite values.
Results may differ from the reference program's by a relative error of at most 0.012.
Values may be sent and summed in bfloat16 or wider, within the bound.
No kernel may reach another device: no remote copies, remote signals or barrier semaphores. Data moves between devices by JAX's collectives and lax.ppermute only.
A program may use at most 192 MiB of HBM per device.

```python
import math
import jax
import jax.numpy as jnp
import numpy as np
from jax import lax

D = 3072
HEADS = 24
KV_HEADS = 4
HEAD_DIM = 128
FF = 8192
EXPERTS = 8
TOP = 2
TOK_DEV = 128
CAP = 36
TOKENS = 4096
N_CTX = 32


def draw_queries(key, part):
    drawn_key = jax.random.fold_in(key, 17)
    drawn_draw = jax.random.truncated_normal(drawn_key, -6.0, 6.0, (TOKENS, HEADS * HEAD_DIM), jnp.float32)
    return drawn_draw.astype(jnp.bfloat16)


def draw_keys(key, part):
    drawn_key = jax.random.fold_in(key, 29)
    drawn_draw = jax.random.truncated_normal(drawn_key, -6.0, 6.0, (TOKENS, KV_HEADS * HEAD_DIM), jnp.float32)
    return drawn_draw.astype(jnp.bfloat16)


def draw_residual(key, part):
    row_key, col_key, val_key = jax.random.split(jax.random.fold_in(key, 23), 3)
    row_scale = jnp.exp(jax.random.uniform(row_key, (TOKENS, 1), jnp.float32, math.log(0.3), math.log(3.0)))
    col_scale = jnp.exp(jax.random.uniform(col_key, (1, D), jnp.float32, math.log(0.3), math.log(3.0)))
    drawn_draw = jax.random.truncated_normal(val_key, -4.0, 4.0, (TOKENS, D), jnp.float32)
    return (drawn_draw * row_scale * col_scale).astype(jnp.bfloat16)


def shard_levels(own_key, extent, shards, smallest, high):
    gain = 1.0
    for dim, shards_of in shards:
        heights = jax.random.uniform(jax.random.fold_in(jax.random.fold_in(own_key, 6), dim), (shards_of,), jnp.float32, smallest / len(shards), high / len(shards))
        gain = gain * jnp.repeat(jnp.exp(heights), extent[dim] // shards_of).reshape((-1,) + (1,) * (len(extent) - 1 - dim))
    return gain


def routed_block(rng, own, number, rows, count, top, limit, lean):
    ranking = jax.random.permutation(rng, count)
    packed, common = shares(count, rows * top, limit, lean, True), shares(count, rows * top, limit, lean, False)
    places = jnp.arange(count)

    def named(lengths, offset_by):
        used = int((lengths > 0).sum())
        fixed = max(1, used // 4)
        moved = fixed + (places - fixed + offset_by * (used - fixed)) % max(1, count - fixed)
        return jnp.zeros((count,), jnp.int32).at[ranking[jnp.where(places < fixed, places, moved)]].set(jnp.asarray(lengths, jnp.int32))

    lengths = jnp.where(number % 4 == 0, named(packed, number // 4), named(common, number - number // 4 - 1))
    mixed = jax.random.permutation(jax.random.fold_in(own, 3), count)
    giver, sink = mixed[0:count // 2 * 2:2], mixed[1:count // 2 * 2:2]
    slack = jnp.minimum(lengths[giver] - 1, limit - lengths[sink]) // 2
    slack = jnp.where((giver == ranking[0]) | (sink == ranking[0]) | (lengths[sink] == 0), 0, jnp.maximum(slack, 0))
    moved = jax.random.randint(jax.random.fold_in(own, 4), (count // 2,), 0, 1 << 20) % (slack + 1)
    lengths = lengths.at[giver].add(-moved).at[sink].add(moved)
    items = jnp.searchsorted(jnp.cumsum(lengths), jnp.arange(rows * top), side="right").astype(jnp.int32)
    listing = items.reshape(top, rows).T
    listing = listing[jax.random.permutation(jax.random.fold_in(own, 1), rows)]
    offset_by = jax.random.randint(jax.random.fold_in(own, 2), (rows, 1), 0, top)
    return jnp.take_along_axis(listing, (jnp.arange(top)[None, :] + offset_by) % top, axis=1)


def shares(number_of, total, bound, slope, full):
    weights = [(1 << 20) // math.isqrt(standing ** slope) + 1 for standing in range(1, number_of + 1)]
    largest = bound if full else min(bound, max(-(-total // number_of), total * weights[0] // sum(weights)))
    least = 1 if total - largest >= number_of - 1 else 0
    counts, rest = [largest] + [least] * (number_of - 1), total - largest - least * (number_of - 1)
    while rest > 0:
        candidates = [i for i in range(1, number_of) if counts[i] < largest] or [i for i in range(1, number_of) if counts[i] < bound]
        pool, remaining = sum([weights[i] for i in candidates]), rest
        for i in candidates:
            extra = min(bound - counts[i], max(1, remaining * weights[i] // pool), rest)
            counts[i] = counts[i] + extra
            rest = rest - extra
    return np.array(counts)


def centred(rng, dims, deviation, most, pieces=(), kind=jnp.bfloat16):
    entries = deviation * jax.random.normal(rng, dims, jnp.float32)
    if pieces:
        entries = entries * shard_levels(rng, dims, pieces, -0.22, 0.18)
    return jnp.clip(entries, -most, most).astype(kind)


def setup_inputs(seed: int = 0, part: int = 0) -> dict:
    key_list = jax.random.split(jax.random.key(seed), 13)
    own_keys = jax.random.split(jax.random.fold_in(key_list[12], part), 13)
    queries = draw_queries(jax.random.fold_in(jax.random.fold_in(key_list[12], part), 71), part)
    keys = draw_keys(jax.random.fold_in(jax.random.fold_in(key_list[12], part), 71), part)
    values = centred(own_keys[2], (TOKENS, KV_HEADS * HEAD_DIM), 1.0, 6.0, ((0, 32), (1, 4)))
    cache_keys = centred(own_keys[3], (TOKENS, KV_HEADS * HEAD_DIM), 1.0, 6.0, ((0, 32), (1, 4)))
    cache_values = centred(own_keys[4], (TOKENS, KV_HEADS * HEAD_DIM), 1.0, 6.0, ((0, 32), (1, 4)))
    residual = draw_residual(jax.random.fold_in(jax.random.fold_in(key_list[12], part), 71), part)
    norm_gain = jnp.clip(1.0 + 0.18 * jax.random.normal(key_list[6], (D,), jnp.float32), 0.1, 1.9)
    w_gate = centred(key_list[7], (D, EXPERTS * FF), D ** -0.5, 0.109375, ((1, 128),))
    w_up = centred(key_list[8], (D, EXPERTS * FF), D ** -0.5, 0.109375, ((1, 128),))
    w_down = centred(key_list[9], (EXPERTS * FF, D), FF ** -0.5, 0.0625, ((0, 128),))
    expert_ids_keys = jax.random.split(jax.random.fold_in(own_keys[10], 1), TOKENS // TOK_DEV)
    expert_ids_turns = jax.random.permutation(jax.random.fold_in(own_keys[10], 3), TOKENS // TOK_DEV)
    expert_ids = jax.vmap(lambda own, number: routed_block(jax.random.fold_in(own_keys[10], 2), own, number, TOK_DEV, EXPERTS, TOP, CAP, 1))(expert_ids_keys, expert_ids_turns).reshape((TOKENS, TOP))
    gate_weights = jnp.clip(0.1 + 0.79999997 * jax.random.uniform(own_keys[11], (TOKENS, TOP), jnp.float32) ** shard_levels(own_keys[11], (TOKENS, TOP), ((0, 32),), -0.2, 0.2), 0.1, 0.9)
    return dict(queries=queries, keys=keys, values=values, cache_keys=cache_keys, cache_values=cache_values, residual=residual, norm_gain=norm_gain, w_gate=w_gate, w_up=w_up, w_down=w_down, expert_ids=expert_ids, gate_weights=gate_weights)


eps = 1e-05
neg_big = -1e+30

def reference(queries, keys, values, cache_keys, cache_values, residual, norm_gain, w_gate, w_up, w_down, expert_ids, gate_weights):
    window = TOKENS
    group_size = HEADS // KV_HEADS
    score_scale = 1.0 / math.sqrt(HEAD_DIM)
    all_keys = jnp.concatenate((cache_keys, keys), axis=0)
    all_values = jnp.concatenate((cache_values, values), axis=0)
    offsets = jnp.arange(TOKENS, dtype=jnp.int32)
    key_pos = jnp.concatenate((offsets - window, offsets))
    allowed = (key_pos[None, :] <= offsets[:, None]) & (key_pos[None, :] > offsets[:, None] - window)

    def one_head(head_index):
        kv_head = head_index // group_size
        head_query = lax.dynamic_slice_in_dim(queries, head_index * HEAD_DIM, HEAD_DIM, 1)
        head_keys = lax.dynamic_slice_in_dim(all_keys, kv_head * HEAD_DIM, HEAD_DIM, 1)
        head_values = lax.dynamic_slice_in_dim(all_values, kv_head * HEAD_DIM, HEAD_DIM, 1)
        scores = jnp.dot(head_query, head_keys.T, preferred_element_type=jnp.float32) * score_scale
        scores = jnp.where(allowed, scores, neg_big)
        row_max = lax.optimization_barrier(jnp.max(scores, axis=1, keepdims=True))
        weights = jnp.where(allowed, jnp.exp(scores - row_max), 0.0)
        row_total = lax.optimization_barrier(jnp.sum(weights, axis=1, keepdims=True))
        summed = jnp.dot(weights.astype(jnp.bfloat16), head_values, preferred_element_type=jnp.float32)
        return summed / row_total
    heads_out = lax.map(one_head, jnp.arange(HEADS, dtype=jnp.int32))
    attended = jnp.transpose(heads_out, (1, 0, 2)).reshape(TOKENS, HEADS * HEAD_DIM)
    hidden_state = (residual.astype(jnp.float32) + attended).astype(jnp.bfloat16)
    widened = hidden_state.astype(jnp.float32)
    inverse = lax.rsqrt(lax.optimization_barrier(jnp.mean(widened * widened, axis=1, keepdims=True)) + eps)
    normed = (widened * inverse * norm_gain).astype(jnp.bfloat16)
    row_limit = N_CTX * CAP

    def one_expert(mixture, expert):
        chosen = expert_ids == expert
        weight = lax.optimization_barrier(jnp.sum(jnp.where(chosen, gate_weights, 0.0), axis=1))
        routed = jnp.any(chosen, axis=1)
        row_ids = jnp.nonzero(routed, size=row_limit, fill_value=0)[0].astype(jnp.int32)
        filled = jnp.arange(row_limit, dtype=jnp.int32) < jnp.sum(routed.astype(jnp.int32))
        picked = jnp.take(normed, row_ids, axis=0)
        gate_proj = jnp.dot(picked, lax.dynamic_slice_in_dim(w_gate, expert * FF, FF, 1), preferred_element_type=jnp.float32)
        up_proj = jnp.dot(picked, lax.dynamic_slice_in_dim(w_up, expert * FF, FF, 1), preferred_element_type=jnp.float32)
        activated = (jax.nn.silu(gate_proj) * up_proj).astype(jnp.bfloat16)
        outcome = jnp.dot(activated, lax.dynamic_slice_in_dim(w_down, expert * FF, FF, 0), preferred_element_type=jnp.float32)
        scaled = outcome * jnp.where(filled, jnp.take(weight, row_ids), 0.0)[:, None]
        return (mixture.at[row_ids].add(scaled), None)
    mixture, _ = lax.scan(one_expert, jnp.zeros((TOKENS, D), jnp.float32), jnp.arange(EXPERTS, dtype=jnp.int32))
    return (widened + mixture).astype(jnp.bfloat16)
```

```python
import math

import jax
import jax.numpy as jnp
from jax import lax
from jax.experimental import pallas as pl
from jax.experimental.pallas import tpu as pltpu
from jax.sharding import Mesh, PartitionSpec as P

HEADS = 24
KV_HEADS = 4
HEAD_DIM = 128
EXPERTS = 8
TOP = 2
CAP = 36
EPS = 1e-05
NEG = -1e30
VMEM_LIMIT = 60 * 1024 * 1024

bf16 = jnp.bfloat16
f32 = jnp.float32


def pick_table(ids_ref):
    n = ids_ref.shape[1]
    first, second = ids_ref[0:1, :], ids_ref[1:2, :]
    expert = lax.broadcasted_iota(jnp.int32, (EXPERTS, n), 0)
    member = ((first == expert) | (second == expert)).astype(bf16)
    earlier = (
        lax.broadcasted_iota(jnp.int32, (n, n), 0) < lax.broadcasted_iota(jnp.int32, (n, n), 1)
    ).astype(bf16)
    rank = jnp.dot(member, earlier, preferred_element_type=f32).astype(jnp.int32)
    slot = lax.broadcasted_iota(jnp.int32, (EXPERTS * CAP, n), 0)
    place = jnp.full((EXPERTS * CAP, n), -1, jnp.int32)
    for e in range(EXPERTS):
        inside = (slot >= e * CAP) & (slot < (e + 1) * CAP)
        named = (first == e) | (second == e)
        place = jnp.where(inside & named, e * CAP + rank[e : e + 1, :], place)
    return place == slot, slot


def attend_kernel(where_ref, ids_ref, q_ref, res_ref, kv_ref, hid_ref, buf_ref, k_all, v_all, own, sems):
    n_w = kv_ref.shape[0]
    n_z = kv_ref.shape[1] - 1
    rows = q_ref.shape[0]
    mine, z = where_ref[0], where_ref[1]
    copies = []
    for w in range(n_w):
        src = lax.rem(mine + w, n_w)
        for s in range(n_z):
            if s == 0:
                slot = n_z if w == 0 else jnp.where(src < mine, n_z, z)
            else:
                slot = lax.rem(z + s, n_z)
            at = (w * n_z + s) * rows
            copies.append(
                pltpu.make_async_copy(kv_ref.at[src, slot, 0], k_all.at[pl.ds(at, rows)], sems.at[w])
            )
            copies.append(
                pltpu.make_async_copy(kv_ref.at[src, slot, 1], v_all.at[pl.ds(at, rows)], sems.at[w])
            )
    own_copy = pltpu.make_async_copy(kv_ref.at[mine, z], own, sems.at[n_w])
    for c in copies:
        c.start()
    own_copy.start()
    pick, _ = pick_table(ids_ref)
    for c in copies:
        c.wait()
    own_copy.wait()

    scale = math.log2(math.e) / math.sqrt(HEAD_DIM)
    group = q_ref.shape[1] // HEAD_DIM
    step = 1024
    row_at = lax.broadcasted_iota(jnp.int32, (rows, rows), 0)
    col_at = lax.broadcasted_iota(jnp.int32, (rows, rows), 1)
    tract = col_at <= row_at
    tdot = (((1,), (1,)), ((), ()))
    for h in range(group):
        cols = slice(h * HEAD_DIM, (h + 1) * HEAD_DIM)
        q = q_ref[:, cols]
        s_tract = lax.dot_general(q, k_all[0:rows], tdot, preferred_element_type=f32)
        s_cache = lax.dot_general(q, own[0], tdot, preferred_element_type=f32)
        s_own = jnp.where(tract, s_tract, s_cache) * scale
        m = jnp.max(s_own, axis=1, keepdims=True)
        p = jnp.exp2(s_own - m)
        l = jnp.sum(p, axis=1, keepdims=True)
        low = p.astype(bf16)
        zero = jnp.zeros_like(low)
        acc = jnp.dot(jnp.where(tract, low, zero), v_all[0:rows], preferred_element_type=f32)
        acc += jnp.dot(jnp.where(tract, zero, low), own[1], preferred_element_type=f32)
        for j in range(0, k_all.shape[0], step):
            lo = max(j, rows)
            k = k_all[lo : j + step]
            s = lax.dot_general(q, k, tdot, preferred_element_type=f32) * scale
            m_new = jnp.maximum(m, jnp.max(s, axis=1, keepdims=True))
            fade = jnp.exp2(m - m_new)
            p = jnp.exp2(s - m_new)
            l = l * fade + jnp.sum(p, axis=1, keepdims=True)
            acc = acc * fade + jnp.dot(p.astype(bf16), v_all[lo : j + step], preferred_element_type=f32)
            m = m_new
        hid_ref[:, cols] = (res_ref[:, cols].astype(f32) + acc / l).astype(bf16)
    buf_ref[...] = jnp.dot(pick.astype(bf16), hid_ref[...], preferred_element_type=f32).astype(bf16)


def attend(where, ids, queries, residual, kv):
    rows, width = queries.shape
    n_w, n_z = kv.shape[0], kv.shape[1] - 1
    keys = n_w * n_z * rows
    vm = pl.BlockSpec(memory_space=pltpu.VMEM)
    return pl.pallas_call(
        attend_kernel,
        out_shape=(
            jax.ShapeDtypeStruct((rows, width), bf16),
            jax.ShapeDtypeStruct((EXPERTS * CAP, width), bf16),
        ),
        in_specs=[pl.BlockSpec(memory_space=pltpu.SMEM), vm, vm, vm, pl.BlockSpec(memory_space=pl.ANY)],
        out_specs=(vm, vm),
        scratch_shapes=[
            pltpu.VMEM((keys, HEAD_DIM), bf16),
            pltpu.VMEM((keys, HEAD_DIM), bf16),
            pltpu.VMEM((2, rows, HEAD_DIM), bf16),
            pltpu.SemaphoreType.DMA((n_w + 1,)),
        ],
        compiler_params=pltpu.CompilerParams(vmem_limit_bytes=VMEM_LIMIT),
        name="attend",
    )(where, ids, queries, residual, kv)


def expert_kernel(
    x_ref, gain_ref, wg0, wu0, wd0, wg1, wu1, wd1, out_ref, x_v, g_v, u_v, d_v, normed, act, res, x_sem, w_sem, o_sem
):
    n_y, n_x, rows, width = x_ref.shape
    x_copies = [
        [pltpu.make_async_copy(x_ref.at[y, i], x_v.at[y, i], x_sem.at[y, i]) for i in range(n_x)]
        for y in range(n_y)
    ]
    w_copies = []
    for part, (g, u, d) in enumerate(((wg0, wu0, wd0), (wg1, wu1, wd1))):
        w_copies.append(
            (
                pltpu.make_async_copy(g, g_v.at[part], w_sem.at[part, 0]),
                pltpu.make_async_copy(u, u_v.at[part], w_sem.at[part, 1]),
                pltpu.make_async_copy(d, d_v.at[part], w_sem.at[part, 2]),
            )
        )
    for c in x_copies[0]:
        c.start()
    w_copies[0][0].start()
    w_copies[0][1].start()
    for c in x_copies[1]:
        c.start()
    w_copies[1][0].start()
    w_copies[1][1].start()
    w_copies[0][2].start()
    w_copies[1][2].start()
    total = n_x * width
    ff = g_v.shape[2]
    for y in range(n_y):
        for c in x_copies[y]:
            c.wait()
        sq = jnp.zeros((rows, 1), f32)
        for i in range(n_x):
            v = x_v[y, i].astype(f32)
            sq = sq + jnp.sum(v * v, axis=1, keepdims=True)
        inverse = lax.rsqrt(sq * (1.0 / total) + EPS)
        for i in range(n_x):
            gain = gain_ref[:, i * width : (i + 1) * width]
            normed[y, :, i * width : (i + 1) * width] = (
                x_v[y, i].astype(f32) * inverse * gain
            ).astype(bf16)
        for part in range(2):
            if y == 0:
                w_copies[part][0].wait()
                w_copies[part][1].wait()
            gate = jnp.dot(normed[y], g_v[part], preferred_element_type=f32)
            up = jnp.dot(normed[y], u_v[part], preferred_element_type=f32)
            act[y, :, part * ff : (part + 1) * ff] = (gate / (1.0 + jnp.exp(-gate)) * up).astype(bf16)
    w_copies[0][2].wait()
    w_copies[1][2].wait()
    outs = []
    for y in range(n_y):
        for i in range(n_x):
            cols = slice(i * width, (i + 1) * width)
            part = jnp.dot(act[y, :, :ff], d_v[0, :, cols], preferred_element_type=f32)
            part += jnp.dot(act[y, :, ff:], d_v[1, :, cols], preferred_element_type=f32)
            res[y, i] = part.astype(bf16)
            outs.append(pltpu.make_async_copy(res.at[y, i], out_ref.at[y, i], o_sem.at[y, i]))
            outs[-1].start()
    for c in outs:
        c.wait()


def experts(x, gain, own, other):
    n_y, n_x, rows, width = x.shape
    total, ff = own[0].shape
    hbm = pl.BlockSpec(memory_space=pl.ANY)
    vm = pl.BlockSpec(memory_space=pltpu.VMEM)
    return pl.pallas_call(
        expert_kernel,
        out_shape=jax.ShapeDtypeStruct(x.shape, bf16),
        in_specs=[hbm, vm] + [hbm] * 6,
        out_specs=hbm,
        scratch_shapes=[
            pltpu.VMEM(x.shape, bf16),
            pltpu.VMEM((2, total, ff), bf16),
            pltpu.VMEM((2, total, ff), bf16),
            pltpu.VMEM((2, ff, total), bf16),
            pltpu.VMEM((n_y, rows, total), bf16),
            pltpu.VMEM((n_y, rows, 2 * ff), bf16),
            pltpu.VMEM(x.shape, bf16),
            pltpu.SemaphoreType.DMA((n_y, n_x)),
            pltpu.SemaphoreType.DMA((2, 3)),
            pltpu.SemaphoreType.DMA((n_y, n_x)),
        ],
        compiler_params=pltpu.CompilerParams(vmem_limit_bytes=VMEM_LIMIT),
        name="experts",
    )(x, gain, *own, *other)


def mix_kernel(ids_ref, gates_ref, hid_ref, parts_ref, out_ref):
    pick, slot = pick_table(ids_ref)
    n = ids_ref.shape[1]
    weight = jnp.zeros((EXPERTS * CAP, n), f32)
    for e in range(EXPERTS):
        inside = (slot >= e * CAP) & (slot < (e + 1) * CAP)
        gate = jnp.where(ids_ref[0:1, :] == e, gates_ref[0:1, :], 0.0)
        gate = gate + jnp.where(ids_ref[1:2, :] == e, gates_ref[1:2, :], 0.0)
        weight = jnp.where(inside & pick, gate, weight)
    mixture = lax.dot_general(
        weight,
        parts_ref[...].astype(f32),
        (((0,), (0,)), ((), ())),
        precision=lax.Precision.HIGHEST,
        preferred_element_type=f32,
    )
    out_ref[...] = (hid_ref[...].astype(f32) + mixture).astype(bf16)


def mix(ids, gates, hidden, parts):
    vm = pl.BlockSpec(memory_space=pltpu.VMEM)
    return pl.pallas_call(
        mix_kernel,
        out_shape=jax.ShapeDtypeStruct(hidden.shape, bf16),
        in_specs=[vm] * 4,
        out_specs=vm,
        compiler_params=pltpu.CompilerParams(vmem_limit_bytes=VMEM_LIMIT),
        name="mix",
    )(ids, gates, hidden, parts)


def per_device(
    queries, keys, values, cache_keys, cache_values, residual, norm_gain, w_gate, w_up, w_down, expert_ids, gate_weights
):
    rows, width = queries.shape
    z = lax.axis_index("zh")
    n_z = lax.axis_size("zh")
    mine = lax.axis_index(("yh", "yl", "core"))
    ids, gates = expert_ids.T, gate_weights.T

    swap = [(0, 1), (1, 0)]
    own = (w_gate, w_up, w_down)
    other = tuple(lax.ppermute(w, "core", swap) for w in own)

    tract = jnp.stack((keys, values))
    cache = jnp.stack((cache_keys, cache_values))
    above = (jnp.arange(n_z) > z)[:, None, None, None]
    sent = jnp.where(above, tract[None], cache[None])
    from_z = lax.all_to_all(sent, "zh", split_axis=0, concat_axis=0, tiled=True)
    payload = jnp.concatenate((from_z, tract[None]))
    kv = lax.all_gather(payload, ("yh", "yl", "core"), axis=0, tiled=False)

    where = jnp.stack((mine, z)).astype(jnp.int32)
    hidden, buffer = attend(where, ids, queries, residual, kv)

    arrived = lax.all_to_all(
        buffer.reshape(EXPERTS, CAP, width), ("zh", "yh"), split_axis=0, concat_axis=0, tiled=True
    ).reshape(EXPERTS * CAP, width)
    gathered = lax.all_gather(arrived, ("yl", "x"), axis=0, tiled=False)
    n_x = lax.axis_size("x")
    partial = experts(
        gathered.reshape(-1, n_x, EXPERTS * CAP, width), norm_gain.reshape(1, -1), own, other
    )
    summed = lax.psum_scatter(
        partial.reshape(-1, width), ("yl", "x"), scatter_dimension=0, tiled=True
    )
    back = lax.all_to_all(
        summed.reshape(EXPERTS, CAP, width), ("zh", "yh"), split_axis=0, concat_axis=0, tiled=True
    ).reshape(EXPERTS * CAP, width)
    return mix(ids, gates, hidden, back)


def solution(mesh):
    fine = Mesh(mesh.devices.reshape(2, 4, 2, 2, 2, 4), ("dp", "zh", "yh", "yl", "core", "x"))
    ctx = ("zh", "yh", "yl", "core")
    tok = P(("dp",) + ctx, "x")
    in_specs = (
        tok, tok, tok, tok, tok, tok,
        P(),
        P(None, ctx + ("x",)),
        P(None, ctx + ("x",)),
        P(ctx + ("x",), None),
        P(("dp",) + ctx, None),
        P(("dp",) + ctx, None),
    )
    return jax.shard_map(per_device, mesh=fine, in_specs=in_specs, out_specs=tok, check_vma=False)
```

```python
import math

import jax
import jax.numpy as jnp
from jax import lax
from jax.experimental import pallas as pl
from jax.experimental.pallas import tpu as pltpu
from jax.sharding import Mesh, PartitionSpec as P

HEADS = 24
KV_HEADS = 4
HEAD_DIM = 128
EXPERTS = 8
TOP = 2
CAP = 36
PAD = 40
EPS = 1e-05
NZ, NY, NX, NC = 4, 4, 4, 2
SHIFTS = (1, 3, 2)
MB = 1024 * 1024

bf16 = jnp.bfloat16
f32 = jnp.float32
VM = pl.BlockSpec(memory_space=pltpu.VMEM)
SM = pl.BlockSpec(memory_space=pltpu.SMEM)
HBM = pl.BlockSpec(memory_space=pltpu.HBM)


def call(body, out_shape, args, name, scratch=(), limit=16, scalars=0, hbm=0):
    many = isinstance(out_shape, list)
    return pl.pallas_call(
        body,
        out_shape=out_shape,
        in_specs=[SM] * scalars + [VM] * (len(args) - scalars - hbm) + [HBM] * hbm,
        out_specs=[VM] * len(out_shape) if many else VM,
        scratch_shapes=list(scratch),
        compiler_params=pltpu.CompilerParams(vmem_limit_bytes=limit * MB),
        name=name,
    )(*args)


def pick_table(ids_ref):
    n = ids_ref.shape[1]
    first, second = ids_ref[0:1, :], ids_ref[1:2, :]
    line = lax.broadcasted_iota(jnp.int32, (EXPERTS, n), 0)
    named = (first == line) | (second == line)
    earlier = (
        lax.broadcasted_iota(jnp.int32, (n, n), 0) < lax.broadcasted_iota(jnp.int32, (n, n), 1)
    ).astype(bf16)
    rank = jnp.dot(named.astype(bf16), earlier, preferred_element_type=f32).astype(jnp.int32)
    rank = jnp.where(named, rank, -1)
    row = lax.broadcasted_iota(jnp.int32, (PAD, n), 0)
    return [rank[e : e + 1, :] == row for e in range(EXPERTS)]


def attend_kernel(where_ref, ids_ref, *refs):
    kv_refs = refs[: NY * NC]
    q_hbm, res_hbm, hid_ref, buf_ref, q_all, o_all, q_ref, res_ref, sems = refs[NY * NC :]
    q_load = pltpu.make_async_copy(q_hbm, q_ref, sems.at[0])
    res_load = pltpu.make_async_copy(res_hbm, res_ref, sems.at[1])
    q_load.start()
    res_load.start()
    rows, width = q_ref.shape
    q_load.wait()
    heads = width // HEAD_DIM
    y, core = where_ref[1], where_ref[2]
    mine = y * NC + core
    span = kv_refs[0].shape[1] - rows
    for h in range(heads):
        q_all[h * rows : (h + 1) * rows, :] = q_ref[:, h * HEAD_DIM : (h + 1) * HEAD_DIM]
    starts = [0]
    for i, shift in enumerate((0,) + SHIFTS):
        for c in range(NC):
            if i + c:
                src = lax.rem(y - shift + NY, NY) * NC + lax.rem(core + c, NC)
                starts.append(pl.multiple_of(jnp.where(src < mine, 0, rows), rows))

    scale = math.log2(math.e) / math.sqrt(HEAD_DIM)
    tile = 2 * rows
    row_at = lax.rem(lax.broadcasted_iota(jnp.int32, (tile, rows), 0), rows)
    col_at = lax.broadcasted_iota(jnp.int32, (tile, rows), 1)
    tract = col_at <= row_at
    tdot = (((1,), (1,)), ((), ()))

    def group(g, carry):
        at = pl.ds(pl.multiple_of(g * tile, tile), tile)
        q = q_all[at, :]
        s_tract = lax.dot_general(q, kv_refs[0][0, 0:rows], tdot, preferred_element_type=f32)
        s_cache = lax.dot_general(q, kv_refs[0][0, span:], tdot, preferred_element_type=f32)
        s = jnp.where(tract, s_tract, s_cache) * scale
        m = jnp.max(s, axis=1, keepdims=True)
        p = jnp.exp2(s - m)
        l = jnp.sum(p, axis=1, keepdims=True)
        low = p.astype(bf16)
        zero = jnp.zeros_like(low)
        acc = jnp.dot(jnp.where(tract, low, zero), kv_refs[0][1, 0:rows], preferred_element_type=f32)
        acc += jnp.dot(jnp.where(tract, zero, low), kv_refs[0][1, span:], preferred_element_type=f32)
        for i, (ref, start) in enumerate(zip(kv_refs, starts)):
            keys = pl.ds(start, span) if i else pl.ds(rows, span - rows)
            s = lax.dot_general(q, ref[0, keys], tdot, preferred_element_type=f32) * scale
            m_new = jnp.maximum(m, jnp.max(s, axis=1, keepdims=True))
            fade = jnp.exp2(m - m_new)
            p = jnp.exp2(s - m_new)
            l = l * fade + jnp.sum(p, axis=1, keepdims=True)
            acc = acc * fade + jnp.dot(p.astype(bf16), ref[1, keys], preferred_element_type=f32)
            m = m_new
        o_all[at, :] = acc / l
        return carry

    lax.fori_loop(0, heads * rows // tile, group, 0)
    res_load.wait()
    for h in range(heads):
        cols = slice(h * HEAD_DIM, (h + 1) * HEAD_DIM)
        attended = o_all[h * rows : (h + 1) * rows, :]
        hid_ref[:, cols] = (res_ref[:, cols].astype(f32) + attended).astype(bf16)
    table = jnp.concatenate([t.astype(f32) for t in pick_table(ids_ref)], axis=0).astype(bf16)
    routed = jnp.dot(table, hid_ref[...], preferred_element_type=f32).astype(bf16)
    for e in range(EXPERTS):
        buf_ref[e] = routed[e * PAD : e * PAD + CAP]


def attend(where, ids, queries, residual, kv):
    rows, width = queries.shape
    heads = width // HEAD_DIM
    return call(
        attend_kernel,
        [
            jax.ShapeDtypeStruct((rows, width), bf16),
            jax.ShapeDtypeStruct((EXPERTS, CAP, width), bf16),
        ],
        [where, ids, *kv, queries, residual],
        "attend",
        [
            pltpu.VMEM((heads * rows, HEAD_DIM), bf16),
            pltpu.VMEM((heads * rows, HEAD_DIM), f32),
            pltpu.VMEM((rows, width), bf16),
            pltpu.VMEM((rows, width), bf16),
            pltpu.SemaphoreType.DMA((2,)),
        ],
        limit=16,
        scalars=1,
        hbm=2,
    )


def expert_kernel(where_ref, gain_ref, *refs):
    a_own, a_far, b_all = refs[0:NX], refs[NX : 2 * NX], refs[2 * NX : 3 * NX]
    weights = refs[3 * NX : 3 * NX + 6]
    a_out = refs[3 * NX + 6 : 5 * NX + 6]
    b_out = refs[5 * NX + 6 : 6 * NX + 6]
    normed, act, *held, sems = refs[6 * NX + 6 :]
    rows, width = a_own[0].shape
    full = 2 * width
    total, ff = weights[0].shape
    loads = [pltpu.make_async_copy(w, v, sems.at[i]) for i, (w, v) in enumerate(zip(weights, held))]
    for i in (0, 1, 3, 4, 2, 5):
        loads[i].start()
    weights = held
    x = where_ref[3]
    order = (0,) + SHIFTS
    for r in range(2):
        a = a_own if r == 0 else a_far
        at = slice(r * rows, (r + 1) * rows)
        sq = jnp.zeros((rows, 1), f32)
        for i in range(NX):
            v = a[i][...].astype(f32)
            sq = sq + jnp.sum(v * v, axis=1, keepdims=True)
            v = b_all[i][r].astype(f32)
            sq = sq + jnp.sum(v * v, axis=1, keepdims=True)
        inverse = lax.rsqrt(sq * (1.0 / total) + EPS)
        for i, shift in enumerate(order):
            src = lax.rem(x - shift + NX, NX)
            gain = gain_ref[src]
            start = pl.multiple_of(src * full, full)
            v = a[i][...].astype(f32) * inverse * gain[:, :width]
            normed[at, pl.ds(start, width)] = v.astype(bf16)
            v = b_all[i][r].astype(f32) * inverse * gain[:, width:]
            normed[at, pl.ds(start + width, width)] = v.astype(bf16)
    for part in range(2):
        w_gate, w_up, _ = weights[3 * part : 3 * part + 3]
        loads[3 * part].wait()
        loads[3 * part + 1].wait()
        gate = jnp.dot(normed[...], w_gate[...], preferred_element_type=f32)
        up = jnp.dot(normed[...], w_up[...], preferred_element_type=f32)
        act[:, part * ff : (part + 1) * ff] = (gate / (1.0 + jnp.exp(-gate)) * up).astype(bf16)
    loads[2].wait()
    loads[5].wait()
    for i, shift in enumerate(order):
        cols = pl.ds(pl.multiple_of(lax.rem(x + shift, NX) * full, full), full)
        out = jnp.dot(act[:, :ff], weights[2][:, cols], preferred_element_type=f32)
        out += jnp.dot(act[:, ff:], weights[5][:, cols], preferred_element_type=f32)
        for r in range(2):
            at = slice(r * rows, (r + 1) * rows)
            a_out[r * NX + i][...] = out[at, :width].astype(bf16)
            b_out[i][r] = out[at, width:].astype(bf16)


def experts(where, gain, a_own, a_far, b_all, own, other):
    rows, width = a_own[0].shape
    total, ff = own[0].shape
    out = call(
        expert_kernel,
        [jax.ShapeDtypeStruct((rows, width), bf16)] * (2 * NX)
        + [jax.ShapeDtypeStruct((2, rows, width), bf16)] * NX,
        [where, gain, *a_own, *a_far, *b_all, *own, *other],
        "experts",
        [pltpu.VMEM((2 * rows, total), bf16), pltpu.VMEM((2 * rows, 2 * ff), bf16)]
        + [pltpu.VMEM(w.shape, bf16) for w in (*own, *other)]
        + [pltpu.SemaphoreType.DMA((6,))],
        limit=47,
        scalars=1,
        hbm=6,
    )
    return out[:NX], out[NX : 2 * NX], out[2 * NX :]


def mix_kernel(ids_ref, gates_ref, hid_ref, part_ref, out_ref, held):
    weight = []
    for e, pick in enumerate(pick_table(ids_ref)):
        gate = jnp.where(ids_ref[0:1, :] == e, gates_ref[0:1, :], 0.0)
        gate = gate + jnp.where(ids_ref[1:2, :] == e, gates_ref[1:2, :], 0.0)
        weight.append(jnp.where(pick, gate, 0.0))
    held[...] = jnp.zeros_like(held)
    for e in range(EXPERTS):
        held[e * PAD : e * PAD + CAP, :] = part_ref[e].astype(f32)
    mixture = lax.dot_general(
        jnp.concatenate(weight, axis=0),
        held[...],
        (((0,), (0,)), ((), ())),
        precision=lax.Precision.HIGHEST,
        preferred_element_type=f32,
    )
    out_ref[...] = (hid_ref[...].astype(f32) + mixture).astype(bf16)


def mix(ids, gates, hidden, parts):
    return call(
        mix_kernel,
        jax.ShapeDtypeStruct(hidden.shape, bf16),
        [ids, gates, hidden, parts],
        "mix",
        [pltpu.VMEM((EXPERTS * PAD, hidden.shape[1]), f32)],
    )


def pack_kv_kernel(*refs):
    from_z, near, out_ref, sems = refs[: NZ - 1], refs[NZ - 1 : NZ + 3], refs[-2], refs[-1]
    n = near[0].shape[0]
    loads = []
    for i, ref in enumerate(near):
        at = out_ref.at[i % 2, pl.ds((i // 2) * NZ * n, n)]
        loads.append(pltpu.make_async_copy(ref, at, sems.at[i]))
        loads[-1].start()
    for i, ref in enumerate(from_z):
        out_ref[:, (i + 1) * n : (i + 2) * n] = ref[...]
    for c in loads:
        c.wait()


def split_kernel(in_ref, a_ref, b_ref):
    width = a_ref.shape[1]
    for e in range(EXPERTS):
        a_ref[e * CAP : (e + 1) * CAP, :] = in_ref[e, :, :width]
        b_ref[e * CAP : (e + 1) * CAP, :] = in_ref[e, :, width:]


def first_sum_kernel(*refs):
    a_own, a_got = refs[0:3], refs[3:6]
    b_own, b_got = refs[6], refs[7:10]
    a_out, b_out = refs[10:13], refs[13:15]
    for own, got, out in zip(a_own, a_got, a_out):
        out[...] = (own[...].astype(f32) + got[...].astype(f32)).astype(bf16)
    for r in range(2):
        total = b_own[r].astype(f32)
        for got in b_got:
            total = total + got[r].astype(f32)
        b_out[r][...] = total.astype(bf16)


def last_sum_kernel(*refs):
    a_in, b_in, out_ref = refs[0:5], refs[5:7], refs[7]
    width = a_in[0].shape[1]
    a, b = a_in[0][...].astype(f32), b_in[0][...].astype(f32)
    for ref in a_in[1:]:
        a = a + ref[...].astype(f32)
    b = b + b_in[1][...].astype(f32)
    a, b = a.astype(bf16), b.astype(bf16)
    for e in range(EXPERTS):
        out_ref[e, :, :width] = a[e * CAP : (e + 1) * CAP]
        out_ref[e, :, width:] = b[e * CAP : (e + 1) * CAP]


SWAP = [(0, 1), (1, 0)]


def turn(v, axis, shift):
    n = 4
    return lax.ppermute(v, axis, [(i, (i + shift) % n) for i in range(n)])


def swap_y(v):
    return lax.ppermute(v, "yl", SWAP)


def swap_core(v):
    return lax.ppermute(v, "core", SWAP)


def gather_kv(z, keys, values, cache_keys, cache_values):
    tract = jnp.stack((keys, values))
    cache = jnp.stack((cache_keys, cache_values))
    sent = [jnp.where(z + s < NZ, tract, cache) for s in SHIFTS]
    from_z = lax.optimization_barrier([turn(v, "zh", s) for v, s in zip(sent, SHIFTS)])
    n = keys.shape[0]
    payload = call(
        pack_kv_kernel,
        jax.ShapeDtypeStruct((2, (NZ + 1) * n, HEAD_DIM), bf16),
        [*from_z, keys, values, cache_keys, cache_values],
        "pack_kv",
        [pltpu.SemaphoreType.DMA((4,))],
        hbm=4,
    )
    got = lax.optimization_barrier(
        [turn(payload, ("yh", "yl"), s) for s in SHIFTS] + [swap_core(payload)]
    )
    far = lax.optimization_barrier([swap_core(g) for g in got[:3]])
    return [payload, got[3], got[0], far[0], got[1], far[1], got[2], far[2]]


def per_device(
    queries, keys, values, cache_keys, cache_values, residual, norm_gain, w_gate, w_up, w_down, expert_ids, gate_weights
):
    rows, width = queries.shape
    half = width // 2
    z = lax.axis_index("zh")
    y = lax.axis_index(("yh", "yl"))
    where = jnp.stack((z, y, lax.axis_index("core"), lax.axis_index("x"))).astype(jnp.int32)
    ids, gates = expert_ids.T, gate_weights.T

    own = (w_gate, w_up, w_down)
    kv = gather_kv(z, keys, values, cache_keys, cache_values)
    held = lax.optimization_barrier((own, kv[-1]))[0]
    other = tuple(swap_core(w) for w in held)

    hidden, buffer = attend(where, ids, queries, residual, kv)
    buffer, other = lax.optimization_barrier((buffer, other))
    arrived = lax.all_to_all(buffer, ("zh", "yh"), split_axis=0, concat_axis=0, tiled=True)
    slots = EXPERTS * CAP
    piece = jax.ShapeDtypeStruct((slots, half), bf16)
    a, b = call(split_kernel, [piece] * 2, [arrived], "split")

    *a_turned, a_far, b_far = lax.optimization_barrier(
        [turn(a, "x", s) for s in SHIFTS] + [swap_y(a), swap_y(b)]
    )
    b_pair = jnp.stack((b, b_far))
    moved = lax.optimization_barrier(
        [turn(b_pair, "x", s) for s in SHIFTS] + [swap_y(v) for v in a_turned]
    )
    a_own, a_far = [a] + a_turned, [a_far] + moved[3:]
    b_all = [b_pair] + moved[:3]

    gain = norm_gain.reshape(NX, 1, width)
    a_own, a_far, b_all = experts(where, gain, a_own, a_far, b_all, own, other)
    moved = lax.optimization_barrier(
        [turn(v, "x", s) for v, s in zip(b_all[1:], SHIFTS)] + [swap_y(v) for v in a_far[1:]]
    )
    *a_sums, b_own, b_far = call(
        first_sum_kernel,
        [piece] * 5,
        [*a_own[1:], *moved[3:], b_all[0], *moved[:3]],
        "first_sum",
    )
    moved = lax.optimization_barrier(
        [turn(v, "x", s) for v, s in zip(a_sums, SHIFTS)] + [swap_y(a_far[0]), swap_y(b_far)]
    )
    result = call(
        last_sum_kernel,
        jax.ShapeDtypeStruct((EXPERTS, CAP, width), bf16),
        [a_own[0], *moved[:4], b_own, moved[4]],
        "last_sum",
    )
    back = lax.all_to_all(result, ("zh", "yh"), split_axis=0, concat_axis=0, tiled=True)
    return mix(ids, gates, hidden, back)


def solution(mesh):
    fine = Mesh(mesh.devices.reshape(2, 4, 2, 2, 2, 4), ("dp", "zh", "yh", "yl", "core", "x"))
    ctx = ("zh", "yh", "yl", "core")
    tok = P(("dp",) + ctx, "x")
    in_specs = (
        tok, tok, tok, tok, tok, tok,
        P(),
        P(None, ctx + ("x",)),
        P(None, ctx + ("x",)),
        P(ctx + ("x",), None),
        P(("dp",) + ctx, None),
        P(("dp",) + ctx, None),
    )
    return jax.shard_map(per_device, mesh=fine, in_specs=in_specs, out_specs=tok, check_vma=False)
```

```python
import math

import jax
import jax.numpy as jnp
from jax import lax
from jax.experimental import pallas as pl
from jax.experimental.pallas import tpu as pltpu
from jax.sharding import Mesh, PartitionSpec as P

HEADS = 24
KV_HEADS = 4
HEAD_DIM = 128
EXPERTS = 8
TOP = 2
CAP = 36
PAD = 40
EPS = 1e-05
NZ, NY, NX, NC = 4, 4, 4, 2
SHIFTS = (1, 3, 2)
MB = 1024 * 1024

bf16 = jnp.bfloat16
f32 = jnp.float32
VM = pl.BlockSpec(memory_space=pltpu.VMEM)
SM = pl.BlockSpec(memory_space=pltpu.SMEM)
HBM = pl.BlockSpec(memory_space=pltpu.HBM)


def call(body, out_shape, args, name, scratch=(), limit=16, scalars=0, hbm=0):
    many = isinstance(out_shape, list)
    return pl.pallas_call(
        body,
        out_shape=out_shape,
        in_specs=[SM] * scalars + [VM] * (len(args) - scalars - hbm) + [HBM] * hbm,
        out_specs=[VM] * len(out_shape) if many else VM,
        scratch_shapes=list(scratch),
        compiler_params=pltpu.CompilerParams(vmem_limit_bytes=limit * MB),
        name=name,
    )(*args)


def group_expert(z, yh, g):
    return lax.rem(z + g // 2, NZ) * 2 + lax.rem(yh + g % 2, 2)


def pick_table(z, yh, ids_ref):
    n = ids_ref.shape[1]
    first, second = ids_ref[0:1, :], ids_ref[1:2, :]
    line = lax.broadcasted_iota(jnp.int32, (EXPERTS, n), 0)
    expert = jnp.zeros((EXPERTS, n), jnp.int32)
    for g in range(EXPERTS):
        expert = jnp.where(line == g, group_expert(z, yh, g), expert)
    named = (first == expert) | (second == expert)
    earlier = (
        lax.broadcasted_iota(jnp.int32, (n, n), 0) < lax.broadcasted_iota(jnp.int32, (n, n), 1)
    ).astype(bf16)
    rank = jnp.dot(named.astype(bf16), earlier, preferred_element_type=f32).astype(jnp.int32)
    rank = jnp.where(named, rank, -1)
    row = lax.broadcasted_iota(jnp.int32, (PAD, n), 0)
    return [rank[g : g + 1, :] == row for g in range(EXPERTS)]


def prep_kernel(where_ref, ids_ref, q_ref, res_ref, k_ref, v_ref, ck_ref, cv_ref, *outs):
    q_all, res_out, tract, cache, table = outs
    rows = q_ref.shape[0]
    for h in range(q_ref.shape[1] // HEAD_DIM):
        q_all[h * rows : (h + 1) * rows, :] = q_ref[:, h * HEAD_DIM : (h + 1) * HEAD_DIM]
    res_out[...] = res_ref[...]
    tract[0], tract[1] = k_ref[...], v_ref[...]
    cache[0], cache[1] = ck_ref[...], cv_ref[...]
    picks = pick_table(where_ref[0], lax.div(where_ref[1], 2), ids_ref)
    table[...] = jnp.concatenate([t.astype(f32) for t in picks], axis=0).astype(bf16)


def pack_kv_kernel(where_ref, tract, cache, *refs):
    from_z, outs = refs[: NZ - 1], refs[NZ - 1 :]
    n = tract.shape[1]
    y, core = where_ref[1], where_ref[2]
    later = [y + s < NY for s in SHIFTS] + [core == 0]
    for out, is_later in zip(outs, later):
        out[:, 0:n] = jnp.where(is_later, tract[...], cache[...])
        for i, ref in enumerate(from_z):
            out[:, (i + 1) * n : (i + 2) * n] = ref[...]


def attend_kernel(q_all, res_ref, table, tract_ref, cache_ref, *refs):
    kv_refs = refs[: NY * NC]
    hid_ref, *z_refs, o_all = refs[NY * NC :]
    rows, width = res_ref.shape
    heads = width // HEAD_DIM
    span = kv_refs[0].shape[1]
    scale = math.log2(math.e) / math.sqrt(HEAD_DIM)
    tile = 2 * rows
    row_at = lax.rem(lax.broadcasted_iota(jnp.int32, (tile, rows), 0), rows)
    col_at = lax.broadcasted_iota(jnp.int32, (tile, rows), 1)
    tract = col_at <= row_at
    tdot = (((1,), (1,)), ((), ()))

    def group(g, carry):
        at = pl.ds(pl.multiple_of(g * tile, tile), tile)
        q = q_all[at, :]
        s_tract = lax.dot_general(q, tract_ref[0], tdot, preferred_element_type=f32)
        s_cache = lax.dot_general(q, cache_ref[0], tdot, preferred_element_type=f32)
        s = jnp.where(tract, s_tract, s_cache) * scale
        m = jnp.max(s, axis=1, keepdims=True)
        p = jnp.exp2(s - m)
        l = jnp.sum(p, axis=1, keepdims=True)
        low = p.astype(bf16)
        zero = jnp.zeros_like(low)
        acc = jnp.dot(jnp.where(tract, low, zero), tract_ref[1], preferred_element_type=f32)
        acc += jnp.dot(jnp.where(tract, zero, low), cache_ref[1], preferred_element_type=f32)
        for i, ref in enumerate(kv_refs):
            keys = pl.ds(0, span) if i else pl.ds(rows, span - rows)
            s = lax.dot_general(q, ref[0, keys], tdot, preferred_element_type=f32) * scale
            m_new = jnp.maximum(m, jnp.max(s, axis=1, keepdims=True))
            fade = jnp.exp2(m - m_new)
            p = jnp.exp2(s - m_new)
            l = l * fade + jnp.sum(p, axis=1, keepdims=True)
            acc = acc * fade + jnp.dot(p.astype(bf16), ref[1, keys], preferred_element_type=f32)
            m = m_new
        o_all[at, :] = acc / l
        return carry

    lax.fori_loop(0, heads * rows // tile, group, 0)
    for h in range(heads):
        cols = slice(h * HEAD_DIM, (h + 1) * HEAD_DIM)
        attended = o_all[h * rows : (h + 1) * rows, :]
        hid_ref[:, cols] = (res_ref[:, cols].astype(f32) + attended).astype(bf16)
    routed = jnp.dot(table[...], hid_ref[...], preferred_element_type=f32).astype(bf16)
    for g in range(EXPERTS):
        z_refs[g // 2][g % 2] = routed[g * PAD : g * PAD + CAP]


def merge_kernel(*refs):
    keep, away = refs[NZ:]
    for d, ref in enumerate(refs[:NZ]):
        keep[d * CAP : (d + 1) * CAP, :] = ref[0]
        away[d * CAP : (d + 1) * CAP, :] = ref[1]


def expert_kernel(where_ref, gain_ref, *refs):
    a_own, a_far, b_all = refs[0:NX], refs[NX : 2 * NX], refs[2 * NX : 3 * NX]
    weights = refs[3 * NX : 3 * NX + 6]
    a_own_out = refs[3 * NX + 6 : 4 * NX + 6]
    a_far_out = refs[4 * NX + 6 : 5 * NX + 6]
    b_out = refs[5 * NX + 6 : 6 * NX + 6]
    normed, act, *held, sems = refs[6 * NX + 6 :]
    rows, width = a_own[0].shape
    total, ff = weights[0].shape
    loads = [pltpu.make_async_copy(w, v, sems.at[i]) for i, (w, v) in enumerate(zip(weights, held))]
    for i in (0, 1, 3, 4, 2, 5):
        loads[i].start()
    weights = held
    x = where_ref[3]
    order = (0,) + SHIFTS
    parts = [
        lambda i: a_own[i][...],
        lambda i: a_far[i][...],
        lambda i: b_all[i][0],
        lambda i: b_all[i][1],
    ]
    for r, part in enumerate(parts):
        sq = jnp.zeros((rows, 1), f32)
        for i in range(NX):
            v = part(i).astype(f32)
            sq = sq + jnp.sum(v * v, axis=1, keepdims=True)
        inverse = lax.rsqrt(sq * (1.0 / total) + EPS)
        for i, shift in enumerate(order):
            src = lax.rem(x - shift + NX, NX)
            cols = pl.ds(pl.multiple_of(src * width, width), width)
            v = part(i).astype(f32) * inverse * gain_ref[src]
            normed[r * rows : (r + 1) * rows, cols] = v.astype(bf16)
    for half in range(2):
        loads[3 * half].wait()
        loads[3 * half + 1].wait()
        gate = jnp.dot(normed[...], weights[3 * half][...], preferred_element_type=f32)
        up = jnp.dot(normed[...], weights[3 * half + 1][...], preferred_element_type=f32)
        act[:, half * ff : (half + 1) * ff] = (gate / (1.0 + jnp.exp(-gate)) * up).astype(bf16)
    loads[2].wait()
    loads[5].wait()
    for i, shift in enumerate(order):
        cols = pl.ds(pl.multiple_of(lax.rem(x + shift, NX) * width, width), width)
        out = jnp.dot(act[:, :ff], weights[2][:, cols], preferred_element_type=f32)
        out += jnp.dot(act[:, ff:], weights[5][:, cols], preferred_element_type=f32)
        out = out.astype(bf16)
        a_own_out[i][...] = out[0:rows]
        a_far_out[i][...] = out[rows : 2 * rows]
        b_out[i][0] = out[2 * rows : 3 * rows]
        b_out[i][1] = out[3 * rows :]


def experts(where, gain, a_own, a_far, b_all, own, other):
    rows, width = a_own[0].shape
    total, ff = own[0].shape
    out = call(
        expert_kernel,
        [jax.ShapeDtypeStruct((rows, width), bf16)] * (2 * NX)
        + [jax.ShapeDtypeStruct((2, rows, width), bf16)] * NX,
        [where, gain, *a_own, *a_far, *b_all, *own, *other],
        "experts",
        [pltpu.VMEM((4 * rows, total), bf16), pltpu.VMEM((4 * rows, 2 * ff), bf16)]
        + [pltpu.VMEM(w.shape, bf16) for w in (*own, *other)]
        + [pltpu.SemaphoreType.DMA((6,))],
        limit=47,
        scalars=1,
        hbm=6,
    )
    return out[:NX], out[NX : 2 * NX], out[2 * NX :]


def first_sum_kernel(*refs):
    a_own, a_got = refs[0:NX], refs[NX : 2 * NX]
    b_own, b_got = refs[2 * NX], refs[2 * NX + 1 : 3 * NX]
    a_out, b_out = refs[3 * NX : 4 * NX], refs[4 * NX :]
    for own, got, out in zip(a_own, a_got, a_out):
        out[...] = (own[...].astype(f32) + got[...].astype(f32)).astype(bf16)
    for r in range(2):
        total = b_own[r].astype(f32)
        for got in b_got:
            total = total + got[r].astype(f32)
        b_out[r][...] = total.astype(bf16)


def last_sum_kernel(*refs):
    parts, back, outs = refs[:NX], refs[NX], refs[NX + 1 :]
    total = parts[0][...].astype(f32)
    for ref in parts[1:]:
        total = total + ref[...].astype(f32)
    total = total.astype(bf16)
    for d, out in enumerate(outs):
        out[0] = total[d * CAP : (d + 1) * CAP]
        out[1] = back[d * CAP : (d + 1) * CAP, :]


def mix_kernel(where_ref, ids_ref, gates_ref, hid_ref, *refs):
    part_refs, out_ref, held = refs[:NZ], refs[NZ], refs[NZ + 1]
    z, yh = where_ref[0], lax.div(where_ref[1], 2)
    weight = []
    for g, pick in enumerate(pick_table(z, yh, ids_ref)):
        e = group_expert(z, yh, g)
        gate = jnp.where(ids_ref[0:1, :] == e, gates_ref[0:1, :], 0.0)
        gate = gate + jnp.where(ids_ref[1:2, :] == e, gates_ref[1:2, :], 0.0)
        weight.append(jnp.where(pick, gate, 0.0))
    held[...] = jnp.zeros_like(held)
    for g in range(EXPERTS):
        held[g * PAD : g * PAD + CAP, :] = part_refs[g // 2][g % 2].astype(f32)
    mixture = lax.dot_general(
        jnp.concatenate(weight, axis=0),
        held[...],
        (((0,), (0,)), ((), ())),
        precision=lax.Precision.HIGHEST,
        preferred_element_type=f32,
    )
    out_ref[...] = (hid_ref[...].astype(f32) + mixture).astype(bf16)


SWAP = [(0, 1), (1, 0)]


def turn(v, axis, shift):
    n = 4
    return lax.ppermute(v, axis, [(i, (i + shift) % n) for i in range(n)])


def cross(v):
    return lax.ppermute(v, ("yh", "yl"), [(i, NY - 1 - i) for i in range(NY)])


def swap_y(v):
    return lax.ppermute(v, "yl", SWAP)


def swap_core(v):
    return lax.ppermute(v, "core", SWAP)


def per_device(
    queries, keys, values, cache_keys, cache_values, residual, norm_gain, w_gate, w_up, w_down, expert_ids, gate_weights
):
    rows, width = queries.shape
    heads = width // HEAD_DIM
    z = lax.axis_index("zh")
    y = lax.axis_index(("yh", "yl"))
    where = jnp.stack((z, y, lax.axis_index("core"), lax.axis_index("x"))).astype(jnp.int32)
    ids, gates = expert_ids.T, gate_weights.T
    shaped = lambda *dims: jax.ShapeDtypeStruct(dims, bf16)
    block = shaped(2, rows, HEAD_DIM)

    near, past = jnp.stack((keys, values)), jnp.stack((cache_keys, cache_values))
    *from_z, other_gate = lax.optimization_barrier(
        [turn(jnp.where(z + s < NZ, near, past), "zh", s) for s in SHIFTS] + [swap_core(w_gate)]
    )
    q_all, res, tract, cache, table = call(
        prep_kernel,
        [shaped(heads * rows, HEAD_DIM), shaped(rows, width), block, block, shaped(EXPERTS * PAD, rows)],
        [where, ids, queries, residual, keys, values, cache_keys, cache_values],
        "prep",
        scalars=1,
    )
    packed = call(
        pack_kv_kernel,
        [shaped(2, NZ * rows, HEAD_DIM)] * 4,
        [where, tract, cache, *from_z],
        "pack_kv",
        scalars=1,
    )
    held = lax.optimization_barrier((w_up, from_z[0]))[0]
    got = lax.optimization_barrier(
        [turn(v, ("yh", "yl"), s) for v, s in zip(packed, SHIFTS)]
        + [swap_core(packed[3]), swap_core(held)]
    )
    other_up = got[4]
    far = lax.optimization_barrier([swap_core(g) for g in got[:3]])
    held = lax.optimization_barrier((w_down, far[2]))[0]
    own, other = (w_gate, w_up, w_down), (other_gate, other_up, swap_core(held))

    hidden, *sent = call(
        attend_kernel,
        [shaped(rows, width)] + [shaped(2, CAP, width)] * NZ,
        [q_all, res, table, tract, cache, packed[3], got[3], *got[:3], *far],
        "attend",
        [pltpu.VMEM((heads * rows, HEAD_DIM), f32)],
    )

    sent, other = lax.optimization_barrier((sent, other))
    arrived = [sent[0]] + [turn(sent[s], "zh", s) for s in (1, 2, 3)]
    rows_a = shaped(NZ * CAP, width)
    a, away = call(merge_kernel, [rows_a] * 2, arrived, "merge")
    b = cross(away)
    a_far = [swap_y(a)]
    b_far = swap_y(b)
    *a_turned, b_far = lax.optimization_barrier([turn(a, "x", s) for s in SHIFTS] + [b_far])
    b_pair = jnp.stack((b, b_far))
    moved = lax.optimization_barrier(
        [turn(b_pair, "x", s) for s in SHIFTS] + [swap_y(v) for v in a_turned] + a_far
    )
    gain = norm_gain.reshape(NX, 1, width)
    a_own, a_far, b_all = experts(
        where, gain, [a] + a_turned, [moved[6]] + moved[3:6], [b_pair] + moved[:3], own, other
    )

    moved = lax.optimization_barrier(
        [turn(v, "x", s) for v, s in zip(b_all[1:], SHIFTS)] + [swap_y(v) for v in a_far]
    )
    *a_sums, b_own, b_far = call(
        first_sum_kernel, [rows_a] * (NX + 2), [*a_own, *moved[3:], b_all[0], *moved[:3]], "first_sum"
    )
    b_sum = (b_own.astype(f32) + swap_y(b_far).astype(f32)).astype(bf16)
    moved = lax.optimization_barrier(
        [turn(v, "x", s) for v, s in zip(a_sums[1:], SHIFTS)] + [cross(b_sum)]
    )
    result = call(
        last_sum_kernel,
        [shaped(2, CAP, width)] * NZ,
        [a_sums[0], *moved],
        "last_sum",
    )
    back = [result[0]] + [turn(result[s], "zh", NZ - s) for s in (1, 2, 3)]
    return call(
        mix_kernel,
        shaped(rows, width),
        [where, ids, gates, hidden, *back],
        "mix",
        [pltpu.VMEM((EXPERTS * PAD, width), f32)],
        scalars=1,
    )


def solution(mesh):
    fine = Mesh(mesh.devices.reshape(2, 4, 2, 2, 2, 4), ("dp", "zh", "yh", "yl", "core", "x"))
    ctx = ("zh", "yh", "yl", "core")
    tok = P(("dp",) + ctx, "x")
    in_specs = (
        tok, tok, tok, tok, tok, tok,
        P(),
        P(None, ctx + ("x",)),
        P(None, ctx + ("x",)),
        P(ctx + ("x",), None),
        P(("dp",) + ctx, None),
        P(("dp",) + ctx, None),
    )
    return jax.shard_map(per_device, mesh=fine, in_specs=in_specs, out_specs=tok, check_vma=False)
```

```python
import math

import jax
import jax.numpy as jnp
from jax import lax
from jax.experimental import pallas as pl
from jax.experimental.pallas import tpu as pltpu
from jax.sharding import Mesh, PartitionSpec as P

HEADS = 24
KV_HEADS = 4
HEAD_DIM = 128
EXPERTS = 8
TOP = 2
CAP = 36
PAD = 40
EPS = 1e-05
NZ, NY, NX, NC = 4, 4, 4, 2
SHIFTS = (1, 3, 2)
MB = 1024 * 1024

bf16 = jnp.bfloat16
f32 = jnp.float32
VM = pl.BlockSpec(memory_space=pltpu.VMEM)
SM = pl.BlockSpec(memory_space=pltpu.SMEM)
HBM = pl.BlockSpec(memory_space=pltpu.HBM)


def call(body, out_shape, args, name, scratch=(), limit=16, scalars=0, hbm=0):
    many = isinstance(out_shape, list)
    return pl.pallas_call(
        body,
        out_shape=out_shape,
        in_specs=[SM] * scalars + [VM] * (len(args) - scalars - hbm) + [HBM] * hbm,
        out_specs=[VM] * len(out_shape) if many else VM,
        scratch_shapes=list(scratch),
        compiler_params=pltpu.CompilerParams(vmem_limit_bytes=limit * MB),
        name=name,
    )(*args)


def group_expert(z, yh, g):
    return lax.rem(z + g // 2, NZ) * 2 + lax.rem(yh + g % 2, 2)


def pick_table(z, yh, ids_ref):
    n = ids_ref.shape[1]
    first, second = ids_ref[0:1, :], ids_ref[1:2, :]
    line = lax.broadcasted_iota(jnp.int32, (EXPERTS, n), 0)
    expert = jnp.zeros((EXPERTS, n), jnp.int32)
    for g in range(EXPERTS):
        expert = jnp.where(line == g, group_expert(z, yh, g), expert)
    named = (first == expert) | (second == expert)
    earlier = (
        lax.broadcasted_iota(jnp.int32, (n, n), 0) < lax.broadcasted_iota(jnp.int32, (n, n), 1)
    ).astype(bf16)
    rank = jnp.dot(named.astype(bf16), earlier, preferred_element_type=f32).astype(jnp.int32)
    rank = jnp.where(named, rank, -1)
    row = lax.broadcasted_iota(jnp.int32, (PAD, n), 0)
    return [rank[g : g + 1, :] == row for g in range(EXPERTS)]


def prep_kernel(where_ref, ids_ref, q_ref, res_ref, k_ref, v_ref, ck_ref, cv_ref, *outs):
    q_all, res_out, tract, cache, table = outs
    rows = q_ref.shape[0]
    for h in range(q_ref.shape[1] // HEAD_DIM):
        q_all[h * rows : (h + 1) * rows, :] = q_ref[:, h * HEAD_DIM : (h + 1) * HEAD_DIM]
    res_out[...] = res_ref[...]
    tract[0], tract[1] = k_ref[...], v_ref[...]
    cache[0], cache[1] = ck_ref[...], cv_ref[...]
    picks = pick_table(where_ref[0], lax.div(where_ref[1], 2), ids_ref)
    table[...] = jnp.concatenate([t.astype(f32) for t in picks], axis=0).astype(bf16)


def pack_kv_kernel(where_ref, tract, cache, *refs):
    from_z, outs = refs[: NZ - 1], refs[NZ - 1 :]
    n = tract.shape[1]
    y, core = where_ref[1], where_ref[2]
    later = [y + s < NY for s in SHIFTS] + [core == 0]
    for out, is_later in zip(outs, later):
        out[:, 0:n] = jnp.where(is_later, tract[...], cache[...])
        for i, ref in enumerate(from_z):
            out[:, (i + 1) * n : (i + 2) * n] = ref[...]


SCALE = math.log2(math.e) / math.sqrt(HEAD_DIM)
BY_ROWS = (((1,), (1,)), ((), ()))


def attend_piece(q, k, v, m, l, acc):
    s = lax.dot_general(q, k, BY_ROWS, preferred_element_type=f32) * SCALE
    m_new = jnp.maximum(m, jnp.max(s, axis=1, keepdims=True))
    fade = jnp.exp2(m - m_new)
    p = jnp.exp2(s - m_new)
    l = l * fade + jnp.sum(p, axis=1, keepdims=True)
    acc = acc * fade + jnp.dot(p.astype(bf16), v, preferred_element_type=f32)
    return m_new, l, acc


def attend_near_kernel(q_all, tract_ref, cache_ref, *refs):
    kv_refs, (m_ref, l_ref, acc_ref) = refs[:-3], refs[-3:]
    rows = tract_ref.shape[1]
    tile = 2 * rows
    row_at = lax.rem(lax.broadcasted_iota(jnp.int32, (tile, rows), 0), rows)
    col_at = lax.broadcasted_iota(jnp.int32, (tile, rows), 1)
    tract = col_at <= row_at

    def group(g, carry):
        at = pl.ds(pl.multiple_of(g * tile, tile), tile)
        q = q_all[at, :]
        s_tract = lax.dot_general(q, tract_ref[0], BY_ROWS, preferred_element_type=f32)
        s_cache = lax.dot_general(q, cache_ref[0], BY_ROWS, preferred_element_type=f32)
        s = jnp.where(tract, s_tract, s_cache) * SCALE
        m = jnp.max(s, axis=1, keepdims=True)
        p = jnp.exp2(s - m)
        l = jnp.sum(p, axis=1, keepdims=True)
        low = p.astype(bf16)
        zero = jnp.zeros_like(low)
        acc = jnp.dot(jnp.where(tract, low, zero), tract_ref[1], preferred_element_type=f32)
        acc += jnp.dot(jnp.where(tract, zero, low), cache_ref[1], preferred_element_type=f32)
        for i, ref in enumerate(kv_refs):
            keys = slice(0 if i else rows, ref.shape[1])
            m, l, acc = attend_piece(q, ref[0, keys], ref[1, keys], m, l, acc)
        m_ref[at, :] = jnp.broadcast_to(m, acc.shape)
        l_ref[at, :] = jnp.broadcast_to(l, acc.shape)
        acc_ref[at, :] = acc
        return carry

    lax.fori_loop(0, q_all.shape[0] // tile, group, 0)


def attend_kernel(q_all, res_ref, table, m_ref, l_ref, acc_ref, *refs):
    kv_refs, hid_ref, z_refs, o_all = refs[:NY], refs[NY], refs[NY + 1 : -1], refs[-1]
    rows, width = res_ref.shape
    heads = width // HEAD_DIM
    tile = 2 * rows

    def group(g, carry):
        at = pl.ds(pl.multiple_of(g * tile, tile), tile)
        q = q_all[at, :]
        m, l, acc = m_ref[at, :][:, :1], l_ref[at, :][:, :1], acc_ref[at, :]
        for ref in kv_refs:
            m, l, acc = attend_piece(q, ref[0], ref[1], m, l, acc)
        o_all[at, :] = acc / l
        return carry

    lax.fori_loop(0, heads * rows // tile, group, 0)
    for h in range(heads):
        cols = slice(h * HEAD_DIM, (h + 1) * HEAD_DIM)
        attended = o_all[h * rows : (h + 1) * rows, :]
        hid_ref[:, cols] = (res_ref[:, cols].astype(f32) + attended).astype(bf16)
    routed = jnp.dot(table[...], hid_ref[...], preferred_element_type=f32).astype(bf16)
    for g in range(EXPERTS):
        z_refs[g // 2][g % 2] = routed[g * PAD : g * PAD + CAP]


def merge_kernel(*refs):
    keep, away = refs[NZ:]
    for d, ref in enumerate(refs[:NZ]):
        keep[d * CAP : (d + 1) * CAP, :] = ref[0]
        away[d * CAP : (d + 1) * CAP, :] = ref[1]


def expert_kernel(where_ref, gain_ref, *refs):
    a_own, a_far, b_all = refs[0], refs[1], refs[2 : 2 + NX]
    weights = refs[2 + NX : 8 + NX]
    a_own_out, a_far_out = refs[8 + NX : 10 + NX]
    b_out = refs[10 + NX : 10 + 2 * NX]
    normed, act, gate_v, up_v, down_v, sems = refs[10 + 2 * NX :]
    rows, width = a_own.shape[1:]
    total, ff = weights[0].shape
    gate_loads, up_loads, down_loads = [
        [pltpu.make_async_copy(weights[3 * h + j], place(h), sems.at[h, j]) for h in range(2)]
        for j, place in enumerate(
            (
                lambda h: gate_v.at[h],
                lambda h: up_v.at[h],
                lambda h: down_v.at[pl.ds(h * ff, ff)],
            )
        )
    ]
    for c in (gate_loads[0], up_loads[0], gate_loads[1], up_loads[1], *down_loads):
        c.start()
    x = where_ref[3]
    order = (0,) + SHIFTS
    parts = [
        lambda i: a_own[i],
        lambda i: a_far[i],
        lambda i: b_all[i][0],
        lambda i: b_all[i][1],
    ]
    for r, part in enumerate(parts):
        sq = jnp.zeros((rows, 1), f32)
        for i in range(NX):
            v = part(i).astype(f32)
            sq = sq + jnp.sum(v * v, axis=1, keepdims=True)
        inverse = lax.rsqrt(sq * (1.0 / total) + EPS)
        for i, shift in enumerate(order):
            src = lax.rem(x - shift + NX, NX)
            cols = pl.ds(pl.multiple_of(src * width, width), width)
            v = part(i).astype(f32) * inverse * gain_ref[src]
            normed[r * rows : (r + 1) * rows, cols] = v.astype(bf16)

    def hidden_units(half, carry):
        for j, v in enumerate((gate_v, up_v)):
            pltpu.make_async_copy(v.at[half], v.at[half], sems.at[half, j]).wait()
        gate = jnp.dot(normed[...], gate_v[half], preferred_element_type=f32)
        up = jnp.dot(normed[...], up_v[half], preferred_element_type=f32)
        low = (gate / (1.0 + jnp.exp(-gate)) * up).astype(bf16)
        act[:, pl.ds(pl.multiple_of(half * ff, ff), ff)] = low
        return carry

    lax.fori_loop(0, 2, hidden_units, 0)
    for c in down_loads:
        c.wait()
    for i, shift in enumerate(order):
        cols = pl.ds(pl.multiple_of(lax.rem(x + shift, NX) * width, width), width)
        out = jnp.dot(act[...], down_v[:, cols], preferred_element_type=f32).astype(bf16)
        a_own_out[i] = out[0:rows]
        a_far_out[i] = out[rows : 2 * rows]
        b_out[i][0] = out[2 * rows : 3 * rows]
        b_out[i][1] = out[3 * rows :]


def experts(where, gain, a_own, a_far, b_all, own, other):
    rows, width = a_own.shape[1:]
    total, ff = own[0].shape
    out = call(
        expert_kernel,
        [jax.ShapeDtypeStruct((NX, rows, width), bf16)] * 2
        + [jax.ShapeDtypeStruct((2, rows, width), bf16)] * NX,
        [where, gain, a_own, a_far, *b_all, *own, *other],
        "experts",
        [pltpu.VMEM((4 * rows, total), bf16), pltpu.VMEM((4 * rows, 2 * ff), bf16)]
        + [pltpu.VMEM((2, total, ff), bf16)] * 2
        + [pltpu.VMEM((2 * ff, total), bf16), pltpu.SemaphoreType.DMA((2, 3))],
        limit=47,
        scalars=1,
        hbm=6,
    )
    return out[0], out[1], out[2:]


def first_sum_kernel(*refs):
    a_own, a_got, b_own, b_got = refs[0], refs[1], refs[2], refs[3 : 2 + NX]
    a_out, b_out = refs[2 + NX : 2 + 2 * NX], refs[2 + 2 * NX :]
    for i, out in enumerate(a_out):
        out[...] = (a_own[i].astype(f32) + a_got[i].astype(f32)).astype(bf16)
    for r in range(2):
        total = b_own[r].astype(f32)
        for got in b_got:
            total = total + got[r].astype(f32)
        b_out[r][...] = total.astype(bf16)


def last_sum_kernel(*refs):
    parts, back, outs = refs[:NX], refs[NX], refs[NX + 1 :]
    total = parts[0][...].astype(f32)
    for ref in parts[1:]:
        total = total + ref[...].astype(f32)
    total = total.astype(bf16)
    for d, out in enumerate(outs):
        out[0] = total[d * CAP : (d + 1) * CAP]
        out[1] = back[d * CAP : (d + 1) * CAP, :]


def mix_kernel(where_ref, ids_ref, gates_ref, hid_ref, *refs):
    part_refs, out_ref, held = refs[:NZ], refs[NZ], refs[NZ + 1]
    z, yh = where_ref[0], lax.div(where_ref[1], 2)
    weight = []
    for g, pick in enumerate(pick_table(z, yh, ids_ref)):
        e = group_expert(z, yh, g)
        gate = jnp.where(ids_ref[0:1, :] == e, gates_ref[0:1, :], 0.0)
        gate = gate + jnp.where(ids_ref[1:2, :] == e, gates_ref[1:2, :], 0.0)
        weight.append(jnp.where(pick, gate, 0.0))
    held[...] = jnp.zeros_like(held)
    for g in range(EXPERTS):
        held[g * PAD : g * PAD + CAP, :] = part_refs[g // 2][g % 2].astype(f32)
    mixture = lax.dot_general(
        jnp.concatenate(weight, axis=0),
        held[...],
        (((0,), (0,)), ((), ())),
        precision=lax.Precision.HIGHEST,
        preferred_element_type=f32,
    )
    out_ref[...] = (hid_ref[...].astype(f32) + mixture).astype(bf16)


SWAP = [(0, 1), (1, 0)]


def turn(v, axis, shift):
    n = 4
    return lax.ppermute(v, axis, [(i, (i + shift) % n) for i in range(n)])


def cross(v):
    return lax.ppermute(v, ("yh", "yl"), [(i, NY - 1 - i) for i in range(NY)])


def swap_y(v):
    return lax.ppermute(v, "yl", SWAP)


def swap_core(v):
    return lax.ppermute(v, "core", SWAP)


def per_device(
    queries, keys, values, cache_keys, cache_values, residual, norm_gain, w_gate, w_up, w_down, expert_ids, gate_weights
):
    rows, width = queries.shape
    heads = width // HEAD_DIM
    z = lax.axis_index("zh")
    y = lax.axis_index(("yh", "yl"))
    where = jnp.stack((z, y, lax.axis_index("core"), lax.axis_index("x"))).astype(jnp.int32)
    ids, gates = expert_ids.T, gate_weights.T
    shaped = lambda *dims: jax.ShapeDtypeStruct(dims, bf16)
    block = shaped(2, rows, HEAD_DIM)

    near, past = jnp.stack((keys, values)), jnp.stack((cache_keys, cache_values))
    from_z = [turn(jnp.where(z + s < NZ, near, past), "zh", s) for s in SHIFTS]
    q_all, res, tract, cache, table = call(
        prep_kernel,
        [shaped(heads * rows, HEAD_DIM), shaped(rows, width), block, block, shaped(EXPERTS * PAD, rows)],
        [where, ids, queries, residual, keys, values, cache_keys, cache_values],
        "prep",
        scalars=1,
    )
    packed = call(
        pack_kv_kernel,
        [shaped(2, NZ * rows, HEAD_DIM)] * 4,
        [where, tract, cache, *from_z],
        "pack_kv",
        scalars=1,
    )
    packed, other_gate = lax.optimization_barrier((packed, swap_core(w_gate)))
    held = lax.optimization_barrier((w_up, packed[0]))[0]
    y_1, y_3, partner = lax.optimization_barrier(
        [turn(packed[0], ("yh", "yl"), 1), turn(packed[1], ("yh", "yl"), 3), swap_core(packed[3])]
    )
    y_2 = turn(packed[2], ("yh", "yl"), 2)
    far_1, far_3 = swap_core(y_1), swap_core(y_3)
    state = [jax.ShapeDtypeStruct((heads * rows, HEAD_DIM), f32)] * 3
    carried = call(
        attend_near_kernel, state, [q_all, tract, cache, packed[3], partner, y_1, y_3], "attend_near"
    )
    carried, y_2, far_1, far_3, other_up = lax.optimization_barrier(
        (carried, y_2, far_1, far_3, swap_core(held))
    )
    far_2 = swap_core(y_2)
    held = lax.optimization_barrier((w_down, far_2))[0]
    own, other = (w_gate, w_up, w_down), (other_gate, other_up, swap_core(held))
    hidden, *sent = call(
        attend_kernel,
        [shaped(rows, width)] + [shaped(2, CAP, width)] * NZ,
        [q_all, res, table, *carried, y_2, far_1, far_3, far_2],
        "attend",
        [pltpu.VMEM((heads * rows, HEAD_DIM), f32)],
    )

    sent, other = lax.optimization_barrier((sent, other))
    arrived = [sent[0]] + [turn(sent[s], "zh", s) for s in (1, 2, 3)]
    rows_a = shaped(NZ * CAP, width)
    a, away = call(merge_kernel, [rows_a] * 2, arrived, "merge")
    b = cross(away)
    b_far = swap_y(b)
    *a_turned, b_far = lax.optimization_barrier([turn(a, "x", s) for s in SHIFTS] + [b_far])
    a_own = jnp.stack([a] + a_turned)
    b_pair = jnp.stack((b, b_far))
    *b_turned, a_far = lax.optimization_barrier(
        [turn(b_pair, "x", s) for s in SHIFTS] + [swap_y(a_own)]
    )
    gain = norm_gain.reshape(NX, 1, width)
    a_own, a_far, b_all = experts(where, gain, a_own, a_far, [b_pair] + b_turned, own, other)

    *b_turned, a_far = lax.optimization_barrier(
        [turn(v, "x", s) for v, s in zip(b_all[1:], SHIFTS)] + [swap_y(a_far)]
    )
    *a_sums, b_own, b_far = call(
        first_sum_kernel, [rows_a] * (NX + 2), [a_own, a_far, b_all[0], *b_turned], "first_sum"
    )
    b_sum = (b_own.astype(f32) + swap_y(b_far).astype(f32)).astype(bf16)
    moved = lax.optimization_barrier(
        [turn(v, "x", s) for v, s in zip(a_sums[1:], SHIFTS)] + [cross(b_sum)]
    )
    result = call(
        last_sum_kernel,
        [shaped(2, CAP, width)] * NZ,
        [a_sums[0], *moved],
        "last_sum",
    )
    back = [result[0]] + [turn(result[s], "zh", NZ - s) for s in (1, 2, 3)]
    return call(
        mix_kernel,
        shaped(rows, width),
        [where, ids, gates, hidden, *back],
        "mix",
        [pltpu.VMEM((EXPERTS * PAD, width), f32)],
        scalars=1,
    )


def solution(mesh):
    fine = Mesh(mesh.devices.reshape(2, 4, 2, 2, 2, 4), ("dp", "zh", "yh", "yl", "core", "x"))
    ctx = ("zh", "yh", "yl", "core")
    tok = P(("dp",) + ctx, "x")
    in_specs = (
        tok, tok, tok, tok, tok, tok,
        P(),
        P(None, ctx + ("x",)),
        P(None, ctx + ("x",)),
        P(ctx + ("x",), None),
        P(("dp",) + ctx, None),
        P(("dp",) + ctx, None),
    )
    return jax.shard_map(per_device, mesh=fine, in_specs=in_specs, out_specs=tok, check_vma=False)
```

```python
import math

import jax
import jax.numpy as jnp
from jax import lax
from jax.experimental import pallas as pl
from jax.experimental.pallas import tpu as pltpu
from jax.sharding import Mesh, PartitionSpec as P

HEADS = 24
KV_HEADS = 4
HEAD_DIM = 128
EXPERTS = 8
TOP = 2
CAP = 36
PAD = 40
EPS = 1e-05
NZ, NY, NX, NC = 4, 4, 4, 2
SHIFTS = (1, 3, 2)
MB = 1024 * 1024

bf16 = jnp.bfloat16
f32 = jnp.float32
VM = pl.BlockSpec(memory_space=pltpu.VMEM)
SM = pl.BlockSpec(memory_space=pltpu.SMEM)
HBM = pl.BlockSpec(memory_space=pltpu.HBM)


def call(body, out_shape, args, name, scratch=(), limit=16, scalars=0, hbm=0):
    many = isinstance(out_shape, list)
    return pl.pallas_call(
        body,
        out_shape=out_shape,
        in_specs=[SM] * scalars + [VM] * (len(args) - scalars - hbm) + [HBM] * hbm,
        out_specs=[VM] * len(out_shape) if many else VM,
        scratch_shapes=list(scratch),
        compiler_params=pltpu.CompilerParams(vmem_limit_bytes=limit * MB),
        name=name,
    )(*args)


def group_expert(z, yh, g):
    return lax.rem(z + g // 2, NZ) * 2 + lax.rem(yh + g % 2, 2)


def pick_table(z, yh, ids_ref):
    n = ids_ref.shape[1]
    first, second = ids_ref[0:1, :], ids_ref[1:2, :]
    line = lax.broadcasted_iota(jnp.int32, (EXPERTS, n), 0)
    expert = jnp.zeros((EXPERTS, n), jnp.int32)
    for g in range(EXPERTS):
        expert = jnp.where(line == g, group_expert(z, yh, g), expert)
    named = (first == expert) | (second == expert)
    earlier = (
        lax.broadcasted_iota(jnp.int32, (n, n), 0) < lax.broadcasted_iota(jnp.int32, (n, n), 1)
    ).astype(bf16)
    rank = jnp.dot(named.astype(bf16), earlier, preferred_element_type=f32).astype(jnp.int32)
    rank = jnp.where(named, rank, -1)
    row = lax.broadcasted_iota(jnp.int32, (PAD, n), 0)
    return [rank[g : g + 1, :] == row for g in range(EXPERTS)]


def prep_kernel(where_ref, ids_ref, q_ref, res_ref, q_all, res_out, table):
    rows = q_ref.shape[0]
    for h in range(q_ref.shape[1] // HEAD_DIM):
        q_all[h * rows : (h + 1) * rows, :] = q_ref[:, h * HEAD_DIM : (h + 1) * HEAD_DIM]
    res_out[...] = res_ref[...]
    picks = pick_table(where_ref[0], lax.div(where_ref[1], 2), ids_ref)
    table[...] = jnp.concatenate([t.astype(f32) for t in picks], axis=0).astype(bf16)


def pack_kv_kernel(where_ref, tract, cache, *refs):
    from_z, outs = refs[: NZ - 1], refs[NZ - 1 :]
    n = tract.shape[1]
    y, core = where_ref[1], where_ref[2]
    later = [y + s < NY for s in SHIFTS] + [core == 0]
    for out, is_later in zip(outs, later):
        out[:, 0:n] = jnp.where(is_later, tract[...], cache[...])
        for i, ref in enumerate(from_z):
            out[:, (i + 1) * n : (i + 2) * n] = ref[...]


SCALE = math.log2(math.e) / math.sqrt(HEAD_DIM)
BY_ROWS = (((1,), (1,)), ((), ()))


def attend_piece(q, k, v, m, l, acc):
    s = lax.dot_general(q, k, BY_ROWS, preferred_element_type=f32) * SCALE
    m_new = jnp.maximum(m, jnp.max(s, axis=1, keepdims=True))
    fade = jnp.exp2(m - m_new)
    p = jnp.exp2(s - m_new)
    l = l * fade + jnp.sum(p, axis=1, keepdims=True)
    acc = acc * fade + jnp.dot(p.astype(bf16), v, preferred_element_type=f32)
    return m_new, l, acc


def attend_own_kernel(q_all, tract_ref, cache_ref, *refs):
    kv_refs, (m_ref, l_ref, acc_ref) = refs[:-3], refs[-3:]
    rows = tract_ref.shape[1]
    tile = 2 * rows
    row_at = lax.rem(lax.broadcasted_iota(jnp.int32, (tile, rows), 0), rows)
    col_at = lax.broadcasted_iota(jnp.int32, (tile, rows), 1)
    tract = col_at <= row_at

    def group(g, carry):
        at = pl.ds(pl.multiple_of(g * tile, tile), tile)
        q = q_all[at, :]
        s_tract = lax.dot_general(q, tract_ref[0], BY_ROWS, preferred_element_type=f32)
        s_cache = lax.dot_general(q, cache_ref[0], BY_ROWS, preferred_element_type=f32)
        s = jnp.where(tract, s_tract, s_cache) * SCALE
        m = jnp.max(s, axis=1, keepdims=True)
        p = jnp.exp2(s - m)
        l = jnp.sum(p, axis=1, keepdims=True)
        low = p.astype(bf16)
        zero = jnp.zeros_like(low)
        acc = jnp.dot(jnp.where(tract, low, zero), tract_ref[1], preferred_element_type=f32)
        acc += jnp.dot(jnp.where(tract, zero, low), cache_ref[1], preferred_element_type=f32)
        for i, ref in enumerate(kv_refs):
            keys = slice(0 if i else rows, ref.shape[1])
            m, l, acc = attend_piece(q, ref[0, keys], ref[1, keys], m, l, acc)
        m_ref[at, :] = jnp.broadcast_to(m, acc.shape)
        l_ref[at, :] = jnp.broadcast_to(l, acc.shape)
        acc_ref[at, :] = acc
        return carry

    lax.fori_loop(0, q_all.shape[0] // tile, group, 0)


def attend_more_kernel(q_all, m_ref, l_ref, acc_ref, *refs):
    kv_refs, (m_out, l_out, acc_out) = refs[:-3], refs[-3:]
    tile = 256

    def group(g, carry):
        at = pl.ds(pl.multiple_of(g * tile, tile), tile)
        q = q_all[at, :]
        m, l, acc = m_ref[at, :][:, :1], l_ref[at, :][:, :1], acc_ref[at, :]
        for ref in kv_refs:
            m, l, acc = attend_piece(q, ref[0], ref[1], m, l, acc)
        m_out[at, :] = jnp.broadcast_to(m, acc.shape)
        l_out[at, :] = jnp.broadcast_to(l, acc.shape)
        acc_out[at, :] = acc
        return carry

    lax.fori_loop(0, q_all.shape[0] // tile, group, 0)


def attend_kernel(q_all, res_ref, table, m_ref, l_ref, acc_ref, *refs):
    kv_refs, hid_ref, z_refs, o_all = refs[:NC], refs[NC], refs[NC + 1 : -1], refs[-1]
    rows, width = res_ref.shape
    heads = width // HEAD_DIM
    tile = 2 * rows

    def group(g, carry):
        at = pl.ds(pl.multiple_of(g * tile, tile), tile)
        q = q_all[at, :]
        m, l, acc = m_ref[at, :][:, :1], l_ref[at, :][:, :1], acc_ref[at, :]
        for ref in kv_refs:
            m, l, acc = attend_piece(q, ref[0], ref[1], m, l, acc)
        o_all[at, :] = acc / l
        return carry

    lax.fori_loop(0, heads * rows // tile, group, 0)
    for h in range(heads):
        cols = slice(h * HEAD_DIM, (h + 1) * HEAD_DIM)
        attended = o_all[h * rows : (h + 1) * rows, :]
        hid_ref[:, cols] = (res_ref[:, cols].astype(f32) + attended).astype(bf16)
    routed = jnp.dot(table[...], hid_ref[...], preferred_element_type=f32).astype(bf16)
    for g in range(EXPERTS):
        z_refs[g // 2][(g % 2) * CAP : (g % 2 + 1) * CAP, :] = routed[g * PAD : g * PAD + CAP]


def merge_kernel(*refs):
    keep, away = refs[NZ:]
    for d, ref in enumerate(refs[:NZ]):
        keep[d * CAP : (d + 1) * CAP, :] = ref[:CAP]
        away[d * CAP : (d + 1) * CAP, :] = ref[CAP:]


def expert_kernel(where_ref, gain_ref, *refs):
    a_own, a_far, b_all = refs[0], refs[1], refs[2 : 2 + NX]
    weights = refs[2 + NX : 8 + NX]
    a_own_out, a_far_out = refs[8 + NX : 10 + NX]
    b_out = refs[10 + NX : 10 + 2 * NX]
    normed, act, gate_v, up_v, down_v, sems = refs[10 + 2 * NX :]
    rows, width = a_own.shape[1:]
    total, ff = weights[0].shape
    gate_loads, up_loads, down_loads = [
        [pltpu.make_async_copy(weights[3 * h + j], place(h), sems.at[h, j]) for h in range(2)]
        for j, place in enumerate(
            (
                lambda h: gate_v.at[h],
                lambda h: up_v.at[h],
                lambda h: down_v.at[pl.ds(h * ff, ff)],
            )
        )
    ]
    for c in (gate_loads[0], up_loads[0], gate_loads[1], up_loads[1], *down_loads):
        c.start()
    x = where_ref[3]
    order = (0,) + SHIFTS
    parts = [
        lambda i: a_own[i],
        lambda i: a_far[i],
        lambda i: b_all[i][0],
        lambda i: b_all[i][1],
    ]
    for r, part in enumerate(parts):
        sq = jnp.zeros((rows, 1), f32)
        for i in range(NX):
            v = part(i).astype(f32)
            sq = sq + jnp.sum(v * v, axis=1, keepdims=True)
        inverse = lax.rsqrt(sq * (1.0 / total) + EPS)
        for i, shift in enumerate(order):
            src = lax.rem(x - shift + NX, NX)
            cols = pl.ds(pl.multiple_of(src * width, width), width)
            v = part(i).astype(f32) * inverse * gain_ref[src]
            normed[r * rows : (r + 1) * rows, cols] = v.astype(bf16)

    def hidden_units(half, carry):
        for j, v in enumerate((gate_v, up_v)):
            pltpu.make_async_copy(v.at[half], v.at[half], sems.at[half, j]).wait()
        gate = jnp.dot(normed[...], gate_v[half], preferred_element_type=f32)
        up = jnp.dot(normed[...], up_v[half], preferred_element_type=f32)
        low = (gate / (1.0 + jnp.exp(-gate)) * up).astype(bf16)
        act[:, pl.ds(pl.multiple_of(half * ff, ff), ff)] = low
        return carry

    lax.fori_loop(0, 2, hidden_units, 0)
    for c in down_loads:
        c.wait()
    for i, shift in enumerate(order):
        cols = pl.ds(pl.multiple_of(lax.rem(x + shift, NX) * width, width), width)
        out = jnp.dot(act[...], down_v[:, cols], preferred_element_type=f32).astype(bf16)
        a_own_out[i] = out[0:rows]
        a_far_out[i] = out[rows : 2 * rows]
        b_out[i][0] = out[2 * rows : 3 * rows]
        b_out[i][1] = out[3 * rows :]


def experts(where, gain, a_own, a_far, b_all, own, other):
    rows, width = a_own.shape[1:]
    total, ff = own[0].shape
    out = call(
        expert_kernel,
        [jax.ShapeDtypeStruct((NX, rows, width), bf16)] * 2
        + [jax.ShapeDtypeStruct((2, rows, width), bf16)] * NX,
        [where, gain, a_own, a_far, *b_all, *own, *other],
        "experts",
        [pltpu.VMEM((4 * rows, total), bf16), pltpu.VMEM((4 * rows, 2 * ff), bf16)]
        + [pltpu.VMEM((2, total, ff), bf16)] * 2
        + [pltpu.VMEM((2 * ff, total), bf16), pltpu.SemaphoreType.DMA((2, 3))],
        limit=47,
        scalars=1,
        hbm=6,
    )
    return out[0], out[1], out[2:]


def first_sum_kernel(*refs):
    a_own, a_got, b_own, b_got = refs[0], refs[1], refs[2], refs[3 : 2 + NX]
    a_out, b_out = refs[2 + NX : 2 + 2 * NX], refs[2 + 2 * NX :]
    for i, out in enumerate(a_out):
        out[...] = (a_own[i].astype(f32) + a_got[i].astype(f32)).astype(bf16)
    for r in range(2):
        total = b_own[r].astype(f32)
        for got in b_got:
            total = total + got[r].astype(f32)
        b_out[r][...] = total.astype(bf16)


def last_sum_kernel(*refs):
    parts, back, outs = refs[:NX], refs[NX], refs[NX + 1 :]
    total = parts[0][...].astype(f32)
    for ref in parts[1:]:
        total = total + ref[...].astype(f32)
    total = total.astype(bf16)
    for d, out in enumerate(outs):
        out[:CAP] = total[d * CAP : (d + 1) * CAP]
        out[CAP:] = back[d * CAP : (d + 1) * CAP, :]


def mix_kernel(where_ref, ids_ref, gates_ref, hid_ref, *refs):
    part_refs, out_ref, held = refs[:NZ], refs[NZ], refs[NZ + 1]
    z, yh = where_ref[0], lax.div(where_ref[1], 2)
    weight = []
    for g, pick in enumerate(pick_table(z, yh, ids_ref)):
        e = group_expert(z, yh, g)
        gate = jnp.where(ids_ref[0:1, :] == e, gates_ref[0:1, :], 0.0)
        gate = gate + jnp.where(ids_ref[1:2, :] == e, gates_ref[1:2, :], 0.0)
        weight.append(jnp.where(pick, gate, 0.0))
    held[...] = jnp.zeros_like(held)
    for g in range(EXPERTS):
        part = part_refs[g // 2][(g % 2) * CAP : (g % 2 + 1) * CAP, :]
        held[g * PAD : g * PAD + CAP, :] = part.astype(f32)
    mixture = lax.dot_general(
        jnp.concatenate(weight, axis=0),
        held[...],
        (((0,), (0,)), ((), ())),
        precision=lax.Precision.HIGHEST,
        preferred_element_type=f32,
    )
    out_ref[...] = (hid_ref[...].astype(f32) + mixture).astype(bf16)


SWAP = [(0, 1), (1, 0)]


def turn(v, axis, shift):
    n = 4
    return lax.ppermute(v, axis, [(i, (i + shift) % n) for i in range(n)])


def cross(v):
    return lax.ppermute(v, ("yh", "yl"), [(i, NY - 1 - i) for i in range(NY)])


def swap_y(v):
    return lax.ppermute(v, "yl", SWAP)


def swap_core(v):
    return lax.ppermute(v, "core", SWAP)


def per_device(
    queries, keys, values, cache_keys, cache_values, residual, norm_gain, w_gate, w_up, w_down, expert_ids, gate_weights
):
    rows, width = queries.shape
    heads = width // HEAD_DIM
    z = lax.axis_index("zh")
    y = lax.axis_index(("yh", "yl"))
    where = jnp.stack((z, y, lax.axis_index("core"), lax.axis_index("x"))).astype(jnp.int32)
    ids, gates = expert_ids.T, gate_weights.T
    shaped = lambda *dims: jax.ShapeDtypeStruct(dims, bf16)

    near, past = jnp.stack((keys, values)), jnp.stack((cache_keys, cache_values))
    from_z = [turn(jnp.where(z + s < NZ, near, past), "zh", s) for s in SHIFTS]
    q_all, res, table = call(
        prep_kernel,
        [shaped(heads * rows, HEAD_DIM), shaped(rows, width), shaped(EXPERTS * PAD, rows)],
        [where, ids, queries, residual],
        "prep",
        scalars=1,
    )
    packed = call(
        pack_kv_kernel,
        [shaped(2, NZ * rows, HEAD_DIM)] * 4,
        [where, near, past, *from_z],
        "pack_kv",
        scalars=1,
    )
    packed, other_gate = lax.optimization_barrier((packed, swap_core(w_gate)))
    held = lax.optimization_barrier((w_up, packed[0]))[0]
    partner = swap_core(packed[3])
    y_1, y_3 = turn(packed[0], ("yh", "yl"), 1), turn(packed[1], ("yh", "yl"), 3)
    state = [jax.ShapeDtypeStruct((heads * rows, HEAD_DIM), f32)] * 3
    carried = call(attend_own_kernel, state, [q_all, near, past, packed[3], partner], "attend_own")
    carried, y_1, y_3, last, other_up = lax.optimization_barrier(
        (carried, y_1, y_3, packed[2], swap_core(held))
    )
    y_2 = turn(last, ("yh", "yl"), 2)
    far_1, far_3 = swap_core(y_1), swap_core(y_3)
    carried = call(attend_more_kernel, state, [q_all, *carried, y_1, y_3, far_1, far_3], "attend_more")
    carried, y_2 = lax.optimization_barrier((carried, y_2))
    far_2 = swap_core(y_2)
    held = lax.optimization_barrier((w_down, far_2))[0]
    own, other = (w_gate, w_up, w_down), (other_gate, other_up, swap_core(held))
    hidden, *sent = call(
        attend_kernel,
        [shaped(rows, width)] + [shaped(2 * CAP, width)] * NZ,
        [q_all, res, table, *carried, y_2, far_2],
        "attend",
        [pltpu.VMEM((heads * rows, HEAD_DIM), f32)],
    )

    arrived = [sent[0]] + [turn(sent[s], "zh", s) for s in (1, 2, 3)]
    arrived, other = lax.optimization_barrier((arrived, other))
    rows_a = shaped(NZ * CAP, width)
    a, away = call(merge_kernel, [rows_a] * 2, arrived, "merge")
    b = cross(away)
    b_far = swap_y(b)
    *a_turned, b_far = lax.optimization_barrier([turn(a, "x", s) for s in SHIFTS] + [b_far])
    a_own = jnp.stack([a] + a_turned)
    b_pair = jnp.stack((b, b_far))
    *b_turned, a_far = lax.optimization_barrier(
        [turn(b_pair, "x", s) for s in SHIFTS] + [swap_y(a_own)]
    )
    gain = norm_gain.reshape(NX, 1, width)
    a_own, a_far, b_all = experts(where, gain, a_own, a_far, [b_pair] + b_turned, own, other)

    *b_turned, a_far = lax.optimization_barrier(
        [turn(v, "x", s) for v, s in zip(b_all[1:], SHIFTS)] + [swap_y(a_far)]
    )
    *a_sums, b_own, b_far = call(
        first_sum_kernel, [rows_a] * (NX + 2), [a_own, a_far, b_all[0], *b_turned], "first_sum"
    )
    b_sum = (b_own.astype(f32) + swap_y(b_far).astype(f32)).astype(bf16)
    moved = lax.optimization_barrier(
        [turn(v, "x", s) for v, s in zip(a_sums[1:], SHIFTS)] + [cross(b_sum)]
    )
    result = call(
        last_sum_kernel,
        [shaped(2 * CAP, width)] * NZ,
        [a_sums[0], *moved],
        "last_sum",
    )
    back = [result[0]] + [turn(result[s], "zh", NZ - s) for s in (1, 2, 3)]
    return call(
        mix_kernel,
        shaped(rows, width),
        [where, ids, gates, hidden, *back],
        "mix",
        [pltpu.VMEM((EXPERTS * PAD, width), f32)],
        scalars=1,
    )


def solution(mesh):
    fine = Mesh(mesh.devices.reshape(2, 4, 2, 2, 2, 4), ("dp", "zh", "yh", "yl", "core", "x"))
    ctx = ("zh", "yh", "yl", "core")
    tok = P(("dp",) + ctx, "x")
    in_specs = (
        tok, tok, tok, tok, tok, tok,
        P(),
        P(None, ctx + ("x",)),
        P(None, ctx + ("x",)),
        P(ctx + ("x",), None),
        P(("dp",) + ctx, None),
        P(("dp",) + ctx, None),
    )
    return jax.shard_map(per_device, mesh=fine, in_specs=in_specs, out_specs=tok, check_vma=False)
```

```python
import math

import jax
import jax.numpy as jnp
from jax import lax
from jax.experimental import pallas as pl
from jax.experimental.pallas import tpu as pltpu
from jax.sharding import Mesh, PartitionSpec as P

HEADS = 24
KV_HEADS = 4
HEAD_DIM = 128
EXPERTS = 8
TOP = 2
CAP = 36
PAD = 40
EPS = 1e-05
NZ, NY, NX, NC = 4, 4, 4, 2
SHIFTS = (1, 3, 2)
KV_ORDER, Z_ORDER, X_ORDER = (0, 1, 2), (0, 1, 2), (2, 1, 0)
MB = 1024 * 1024

bf16 = jnp.bfloat16
f32 = jnp.float32
VM = pl.BlockSpec(memory_space=pltpu.VMEM)
SM = pl.BlockSpec(memory_space=pltpu.SMEM)
HBM = pl.BlockSpec(memory_space=pltpu.HBM)


def call(body, out_shape, args, name, scratch=(), limit=16, scalars=0, hbm=0):
    many = isinstance(out_shape, list)
    return pl.pallas_call(
        body,
        out_shape=out_shape,
        in_specs=[SM] * scalars + [VM] * (len(args) - scalars - hbm) + [HBM] * hbm,
        out_specs=[VM] * len(out_shape) if many else VM,
        scratch_shapes=list(scratch),
        compiler_params=pltpu.CompilerParams(vmem_limit_bytes=limit * MB),
        name=name,
    )(*args)


def group_expert(z, yh, g):
    return lax.rem(z + g // 2, NZ) * 2 + lax.rem(yh + g % 2, 2)


def pick_table(z, yh, ids_ref):
    n = ids_ref.shape[1]
    first, second = ids_ref[0:1, :], ids_ref[1:2, :]
    line = lax.broadcasted_iota(jnp.int32, (EXPERTS, n), 0)
    expert = jnp.zeros((EXPERTS, n), jnp.int32)
    for g in range(EXPERTS):
        expert = jnp.where(line == g, group_expert(z, yh, g), expert)
    named = (first == expert) | (second == expert)
    earlier = (
        lax.broadcasted_iota(jnp.int32, (n, n), 0) < lax.broadcasted_iota(jnp.int32, (n, n), 1)
    ).astype(bf16)
    rank = jnp.dot(named.astype(bf16), earlier, preferred_element_type=f32).astype(jnp.int32)
    rank = jnp.where(named, rank, -1)
    row = lax.broadcasted_iota(jnp.int32, (PAD, n), 0)
    return [rank[g : g + 1, :] == row for g in range(EXPERTS)]


def prep_kernel(where_ref, ids_ref, q_ref, res_ref, q_all, res_out, table):
    rows = q_ref.shape[0]
    for h in range(q_ref.shape[1] // HEAD_DIM):
        q_all[h * rows : (h + 1) * rows, :] = q_ref[:, h * HEAD_DIM : (h + 1) * HEAD_DIM]
    res_out[...] = res_ref[...]
    picks = pick_table(where_ref[0], lax.div(where_ref[1], 2), ids_ref)
    table[...] = jnp.concatenate([t.astype(f32) for t in picks], axis=0).astype(bf16)


def pack_kv_kernel(where_ref, tract, cache, *refs):
    from_z, outs = refs[: NZ - 1], refs[NZ - 1 :]
    n = tract.shape[1]
    y, core = where_ref[1], where_ref[2]
    later = [y + s < NY for s in SHIFTS] + [core == 0]
    for out, is_later in zip(outs, later):
        out[:, 0:n] = jnp.where(is_later, tract[...], cache[...])
        for i, ref in enumerate(from_z):
            out[:, (i + 1) * n : (i + 2) * n] = ref[...]


SCALE = math.log2(math.e) / math.sqrt(HEAD_DIM)
BY_ROWS = (((1,), (1,)), ((), ()))


def attend_piece(q, k, v, m, l, acc):
    s = lax.dot_general(q, k, BY_ROWS, preferred_element_type=f32) * SCALE
    m_new = jnp.maximum(m, jnp.max(s, axis=1, keepdims=True))
    fade = jnp.exp2(m - m_new)
    p = jnp.exp2(s - m_new)
    l = l * fade + jnp.sum(p, axis=1, keepdims=True)
    acc = acc * fade + jnp.dot(p.astype(bf16), v, preferred_element_type=f32)
    return m_new, l, acc


def attend_own_kernel(q_all, tract_ref, cache_ref, *refs):
    kv_refs, (m_ref, l_ref, acc_ref) = refs[:-3], refs[-3:]
    rows = tract_ref.shape[1]
    tile = 2 * rows
    row_at = lax.rem(lax.broadcasted_iota(jnp.int32, (tile, rows), 0), rows)
    col_at = lax.broadcasted_iota(jnp.int32, (tile, rows), 1)
    tract = col_at <= row_at

    def group(g, carry):
        at = pl.ds(pl.multiple_of(g * tile, tile), tile)
        q = q_all[at, :]
        s_tract = lax.dot_general(q, tract_ref[0], BY_ROWS, preferred_element_type=f32)
        s_cache = lax.dot_general(q, cache_ref[0], BY_ROWS, preferred_element_type=f32)
        s = jnp.where(tract, s_tract, s_cache) * SCALE
        m = jnp.max(s, axis=1, keepdims=True)
        p = jnp.exp2(s - m)
        l = jnp.sum(p, axis=1, keepdims=True)
        low = p.astype(bf16)
        zero = jnp.zeros_like(low)
        acc = jnp.dot(jnp.where(tract, low, zero), tract_ref[1], preferred_element_type=f32)
        acc += jnp.dot(jnp.where(tract, zero, low), cache_ref[1], preferred_element_type=f32)
        for i, ref in enumerate(kv_refs):
            keys = slice(0 if i else rows, ref.shape[1])
            m, l, acc = attend_piece(q, ref[0, keys], ref[1, keys], m, l, acc)
        m_ref[at, :] = jnp.broadcast_to(m, acc.shape)
        l_ref[at, :] = jnp.broadcast_to(l, acc.shape)
        acc_ref[at, :] = acc
        return carry

    lax.fori_loop(0, q_all.shape[0] // tile, group, 0)


def attend_more_kernel(q_all, m_ref, l_ref, acc_ref, *refs):
    kv_refs, (m_out, l_out, acc_out) = refs[:-3], refs[-3:]
    tile = 256

    def group(g, carry):
        at = pl.ds(pl.multiple_of(g * tile, tile), tile)
        q = q_all[at, :]
        m, l, acc = m_ref[at, :][:, :1], l_ref[at, :][:, :1], acc_ref[at, :]
        for ref in kv_refs:
            m, l, acc = attend_piece(q, ref[0], ref[1], m, l, acc)
        m_out[at, :] = jnp.broadcast_to(m, acc.shape)
        l_out[at, :] = jnp.broadcast_to(l, acc.shape)
        acc_out[at, :] = acc
        return carry

    lax.fori_loop(0, q_all.shape[0] // tile, group, 0)


def attend_kernel(q_all, res_ref, table, m_ref, l_ref, acc_ref, *refs):
    kv_refs, hid_ref, z_refs, o_all = refs[:NC], refs[NC], refs[NC + 1 : -1], refs[-1]
    rows, width = res_ref.shape
    heads = width // HEAD_DIM
    tile = 2 * rows

    def group(g, carry):
        at = pl.ds(pl.multiple_of(g * tile, tile), tile)
        q = q_all[at, :]
        m, l, acc = m_ref[at, :][:, :1], l_ref[at, :][:, :1], acc_ref[at, :]
        for ref in kv_refs:
            m, l, acc = attend_piece(q, ref[0], ref[1], m, l, acc)
        o_all[at, :] = acc / l
        return carry

    lax.fori_loop(0, heads * rows // tile, group, 0)
    for h in range(heads):
        cols = slice(h * HEAD_DIM, (h + 1) * HEAD_DIM)
        attended = o_all[h * rows : (h + 1) * rows, :]
        hid_ref[:, cols] = (res_ref[:, cols].astype(f32) + attended).astype(bf16)
    routed = jnp.dot(table[...], hid_ref[...], preferred_element_type=f32).astype(bf16)
    for g in range(EXPERTS):
        z_refs[g // 2][(g % 2) * CAP : (g % 2 + 1) * CAP, :] = routed[g * PAD : g * PAD + CAP]


def merge_kernel(*refs):
    keep, away = refs[NZ:]
    for d, ref in zip((0,) + SHIFTS, refs[:NZ]):
        keep[d * CAP : (d + 1) * CAP, :] = ref[:CAP]
        away[d * CAP : (d + 1) * CAP, :] = ref[CAP:]


def expert_kernel(where_ref, gain_ref, *refs):
    a_own, a_far, b_all = refs[0], refs[1], refs[2 : 2 + NX]
    weights = refs[2 + NX : 8 + NX]
    a_own_out, a_far_out = refs[8 + NX : 10 + NX]
    b_out = refs[10 + NX : 10 + 2 * NX]
    normed, act, gate_v, up_v, down_v, sems = refs[10 + 2 * NX :]
    rows, width = a_own.shape[1:]
    total, ff = weights[0].shape
    gate_loads, up_loads, down_loads = [
        [pltpu.make_async_copy(weights[3 * h + j], place(h), sems.at[h, j]) for h in range(2)]
        for j, place in enumerate(
            (
                lambda h: gate_v.at[h],
                lambda h: up_v.at[h],
                lambda h: down_v.at[pl.ds(h * ff, ff)],
            )
        )
    ]
    for c in (gate_loads[0], up_loads[0], gate_loads[1], up_loads[1], *down_loads):
        c.start()
    x = where_ref[3]
    order = (0,) + SHIFTS
    parts = [
        lambda i: a_own[i],
        lambda i: a_far[i],
        lambda i: b_all[i][0],
        lambda i: b_all[i][1],
    ]
    for r, part in enumerate(parts):
        sq = jnp.zeros((rows, 1), f32)
        for i in range(NX):
            v = part(i).astype(f32)
            sq = sq + jnp.sum(v * v, axis=1, keepdims=True)
        inverse = lax.rsqrt(sq * (1.0 / total) + EPS)
        for i, shift in enumerate(order):
            src = lax.rem(x - shift + NX, NX)
            cols = pl.ds(pl.multiple_of(src * width, width), width)
            v = part(i).astype(f32) * inverse * gain_ref[src]
            normed[r * rows : (r + 1) * rows, cols] = v.astype(bf16)

    def hidden_units(half, carry):
        for j, v in enumerate((gate_v, up_v)):
            pltpu.make_async_copy(v.at[half], v.at[half], sems.at[half, j]).wait()
        gate = jnp.dot(normed[...], gate_v[half], preferred_element_type=f32)
        up = jnp.dot(normed[...], up_v[half], preferred_element_type=f32)
        low = (gate / (1.0 + jnp.exp(-gate)) * up).astype(bf16)
        act[:, pl.ds(pl.multiple_of(half * ff, ff), ff)] = low
        return carry

    lax.fori_loop(0, 2, hidden_units, 0)
    for c in down_loads:
        c.wait()
    for i, shift in enumerate(order):
        cols = pl.ds(pl.multiple_of(lax.rem(x + shift, NX) * width, width), width)
        out = jnp.dot(act[...], down_v[:, cols], preferred_element_type=f32).astype(bf16)
        a_own_out[i] = out[0:rows]
        a_far_out[i] = out[rows : 2 * rows]
        b_out[i][0] = out[2 * rows : 3 * rows]
        b_out[i][1] = out[3 * rows :]


def experts(where, gain, a_own, a_far, b_all, own, other):
    rows, width = a_own.shape[1:]
    total, ff = own[0].shape
    out = call(
        expert_kernel,
        [jax.ShapeDtypeStruct((NX, rows, width), bf16)] * 2
        + [jax.ShapeDtypeStruct((2, rows, width), bf16)] * NX,
        [where, gain, a_own, a_far, *b_all, *own, *other],
        "experts",
        [pltpu.VMEM((4 * rows, total), bf16), pltpu.VMEM((4 * rows, 2 * ff), bf16)]
        + [pltpu.VMEM((2, total, ff), bf16)] * 2
        + [pltpu.VMEM((2 * ff, total), bf16), pltpu.SemaphoreType.DMA((2, 3))],
        limit=47,
        scalars=1,
        hbm=6,
    )
    return out[0], out[1], out[2:]


def first_sum_kernel(*refs):
    a_own, a_got, b_own, b_got = refs[0], refs[1], refs[2], refs[3 : 2 + NX]
    a_out, b_out = refs[2 + NX : 2 + 2 * NX], refs[2 + 2 * NX :]
    for i, out in enumerate(a_out):
        out[...] = (a_own[i].astype(f32) + a_got[i].astype(f32)).astype(bf16)
    for r in range(2):
        total = b_own[r].astype(f32)
        for got in b_got:
            total = total + got[r].astype(f32)
        b_out[r][...] = total.astype(bf16)


def last_sum_kernel(*refs):
    parts, back, outs = refs[:NX], refs[NX], refs[NX + 1 :]
    total = parts[0][...].astype(f32)
    for ref in parts[1:]:
        total = total + ref[...].astype(f32)
    total = total.astype(bf16)
    for d, out in enumerate(outs):
        out[:CAP] = total[d * CAP : (d + 1) * CAP]
        out[CAP:] = back[d * CAP : (d + 1) * CAP, :]


def mix_kernel(where_ref, ids_ref, gates_ref, hid_ref, *refs):
    part_refs, out_ref, held = refs[:NZ], refs[NZ], refs[NZ + 1]
    z, yh = where_ref[0], lax.div(where_ref[1], 2)
    weight = []
    for g, pick in enumerate(pick_table(z, yh, ids_ref)):
        e = group_expert(z, yh, g)
        gate = jnp.where(ids_ref[0:1, :] == e, gates_ref[0:1, :], 0.0)
        gate = gate + jnp.where(ids_ref[1:2, :] == e, gates_ref[1:2, :], 0.0)
        weight.append(jnp.where(pick, gate, 0.0))
    held[...] = jnp.zeros_like(held)
    for g in range(EXPERTS):
        part = part_refs[(0, 3, 1, 2).index(g // 2)][(g % 2) * CAP : (g % 2 + 1) * CAP, :]
        held[g * PAD : g * PAD + CAP, :] = part.astype(f32)
    mixture = lax.dot_general(
        jnp.concatenate(weight, axis=0),
        held[...],
        (((0,), (0,)), ((), ())),
        precision=lax.Precision.HIGHEST,
        preferred_element_type=f32,
    )
    out_ref[...] = (hid_ref[...].astype(f32) + mixture).astype(bf16)


SWAP = [(0, 1), (1, 0)]


def turn(v, axis, shift):
    n = 4
    return lax.ppermute(v, axis, [(i, (i + shift) % n) for i in range(n)])


def turned(parts, axis, order):
    got = {i: turn(parts[i], axis, SHIFTS[i]) for i in order}
    return [got[i] for i in range(len(parts))]


def together(parts, order):
    got = dict(zip(order, lax.optimization_barrier([parts[i] for i in order])))
    return [got[i] for i in range(len(parts))]


def cross(v):
    return lax.ppermute(v, ("yh", "yl"), [(i, NY - 1 - i) for i in range(NY)])


def swap_y(v):
    return lax.ppermute(v, "yl", SWAP)


def swap_core(v):
    return lax.ppermute(v, "core", SWAP)


def per_device(
    queries, keys, values, cache_keys, cache_values, residual, norm_gain, w_gate, w_up, w_down, expert_ids, gate_weights
):
    rows, width = queries.shape
    heads = width // HEAD_DIM
    z = lax.axis_index("zh")
    y = lax.axis_index(("yh", "yl"))
    where = jnp.stack((z, y, lax.axis_index("core"), lax.axis_index("x"))).astype(jnp.int32)
    ids, gates = expert_ids.T, gate_weights.T
    shaped = lambda *dims: jax.ShapeDtypeStruct(dims, bf16)

    near, past = jnp.stack((keys, values)), jnp.stack((cache_keys, cache_values))
    from_z = turned([jnp.where(z + s < NZ, near, past) for s in SHIFTS], "zh", KV_ORDER)
    q_all, res, table = call(
        prep_kernel,
        [shaped(heads * rows, HEAD_DIM), shaped(rows, width), shaped(EXPERTS * PAD, rows)],
        [where, ids, queries, residual],
        "prep",
        scalars=1,
    )
    packed = call(
        pack_kv_kernel,
        [shaped(2, NZ * rows, HEAD_DIM)] * 4,
        [where, near, past, *[from_z[i] for i in (1, 2, 0)]],
        "pack_kv",
        scalars=1,
    )
    packed, other_gate = lax.optimization_barrier((packed, swap_core(w_gate)))
    held = lax.optimization_barrier((w_up, packed[0]))[0]
    partner = swap_core(packed[3])
    y_1, y_3 = turn(packed[0], ("yh", "yl"), 1), turn(packed[1], ("yh", "yl"), 3)
    state = [jax.ShapeDtypeStruct((heads * rows, HEAD_DIM), f32)] * 3
    carried = call(attend_own_kernel, state, [q_all, near, past, packed[3], partner], "attend_own")
    carried, y_1, y_3, last, other_up = lax.optimization_barrier(
        (carried, y_1, y_3, packed[2], swap_core(held))
    )
    y_2 = turn(last, ("yh", "yl"), 2)
    far_1, far_3 = swap_core(y_1), swap_core(y_3)
    carried = call(attend_more_kernel, state, [q_all, *carried, y_1, y_3, far_1, far_3], "attend_more")
    carried, y_2 = lax.optimization_barrier((carried, y_2))
    far_2 = swap_core(y_2)
    held = lax.optimization_barrier((w_down, far_2))[0]
    own, other = (w_gate, w_up, w_down), (other_gate, other_up, swap_core(held))
    hidden, *sent = call(
        attend_kernel,
        [shaped(rows, width)] + [shaped(2 * CAP, width)] * NZ,
        [q_all, res, table, *carried, y_2, far_2],
        "attend",
        [pltpu.VMEM((heads * rows, HEAD_DIM), f32)],
    )

    arrived = [sent[0]] + turned([sent[s] for s in SHIFTS], "zh", Z_ORDER)
    arrived, other = lax.optimization_barrier((arrived, other))
    rows_a = shaped(NZ * CAP, width)
    a, away = call(merge_kernel, [rows_a] * 2, arrived, "merge")
    b = cross(away)
    b_far = swap_y(b)
    *a_turned, b_far = together(turned([a] * 3, "x", X_ORDER) + [b_far], (2, 1, 0, 3))
    a_own = jnp.stack([a] + a_turned)
    b_pair = jnp.stack((b, b_far))
    *b_turned, a_far = together(turned([b_pair] * 3, "x", X_ORDER) + [swap_y(a_own)], (2, 1, 0, 3))
    gain = norm_gain.reshape(NX, 1, width)
    a_own, a_far, b_all = experts(where, gain, a_own, a_far, [b_pair] + b_turned, own, other)

    *b_turned, a_far = lax.optimization_barrier(
        [turn(v, "x", s) for v, s in zip(b_all[1:], SHIFTS)] + [swap_y(a_far)]
    )
    *a_sums, b_own, b_far = call(
        first_sum_kernel, [rows_a] * (NX + 2), [a_own, a_far, b_all[0], *b_turned], "first_sum"
    )
    b_sum = (b_own.astype(f32) + swap_y(b_far).astype(f32)).astype(bf16)
    moved = lax.optimization_barrier(
        [turn(v, "x", s) for v, s in zip(a_sums[1:], SHIFTS)] + [cross(b_sum)]
    )
    result = call(
        last_sum_kernel,
        [shaped(2 * CAP, width)] * NZ,
        [a_sums[0], *moved],
        "last_sum",
    )
    back = turned([result[NZ - s] for s in SHIFTS], "zh", Z_ORDER)
    back = [result[0]] + back
    return call(
        mix_kernel,
        shaped(rows, width),
        [where, ids, gates, hidden, *back],
        "mix",
        [pltpu.VMEM((EXPERTS * PAD, width), f32)],
        scalars=1,
    )


def solution(mesh):
    fine = Mesh(mesh.devices.reshape(2, 4, 2, 2, 2, 4), ("dp", "zh", "yh", "yl", "core", "x"))
    ctx = ("zh", "yh", "yl", "core")
    tok = P(("dp",) + ctx, "x")
    in_specs = (
        tok, tok, tok, tok, tok, tok,
        P(),
        P(None, ctx + ("x",)),
        P(None, ctx + ("x",)),
        P(ctx + ("x",), None),
        P(("dp",) + ctx, None),
        P(("dp",) + ctx, None),
    )
    return jax.shard_map(per_device, mesh=fine, in_specs=in_specs, out_specs=tok, check_vma=False)
```

```python
import math

import jax
import jax.numpy as jnp
from jax import lax
from jax.experimental import pallas as pl
from jax.experimental.pallas import tpu as pltpu
from jax.sharding import Mesh, PartitionSpec as P

HEADS = 24
KV_HEADS = 4
HEAD_DIM = 128
EXPERTS = 8
TOP = 2
CAP = 36
PAD = 40
EPS = 1e-05
NZ, NY, NX, NC = 4, 4, 4, 2
SHIFTS = (1, 3, 2)
KV_ORDER, Z_ORDER, X_ORDER = (0, 1, 2), (0, 1, 2), (2, 1, 0)
MB = 1024 * 1024
LIMIT = 47

bf16 = jnp.bfloat16
f32 = jnp.float32
VM = pl.BlockSpec(memory_space=pltpu.VMEM)
SM = pl.BlockSpec(memory_space=pltpu.SMEM)
HBM = pl.BlockSpec(memory_space=pltpu.HBM)


def call(body, out_shape, args, name, scratch=(), limit=16, scalars=0, hbm=0):
    many = isinstance(out_shape, list)
    return pl.pallas_call(
        body,
        out_shape=out_shape,
        in_specs=[SM] * scalars + [VM] * (len(args) - scalars - hbm) + [HBM] * hbm,
        out_specs=[VM] * len(out_shape) if many else VM,
        scratch_shapes=list(scratch),
        compiler_params=pltpu.CompilerParams(vmem_limit_bytes=limit * MB),
        name=name,
    )(*args)


def group_expert(z, yh, g):
    return lax.rem(z + g // 2, NZ) * 2 + lax.rem(yh + g % 2, 2)


def pick_table(z, yh, ids_ref):
    n = ids_ref.shape[1]
    first, second = ids_ref[0:1, :], ids_ref[1:2, :]
    line = lax.broadcasted_iota(jnp.int32, (EXPERTS, n), 0)
    expert = jnp.zeros((EXPERTS, n), jnp.int32)
    for g in range(EXPERTS):
        expert = jnp.where(line == g, group_expert(z, yh, g), expert)
    named = (first == expert) | (second == expert)
    earlier = (
        lax.broadcasted_iota(jnp.int32, (n, n), 0) < lax.broadcasted_iota(jnp.int32, (n, n), 1)
    ).astype(bf16)
    rank = jnp.dot(named.astype(bf16), earlier, preferred_element_type=f32).astype(jnp.int32)
    rank = jnp.where(named, rank, -1)
    row = lax.broadcasted_iota(jnp.int32, (PAD, n), 0)
    return [rank[g : g + 1, :] == row for g in range(EXPERTS)]


def prep_kernel(where_ref, ids_ref, gates_ref, q_ref, res_ref, q_all, res_out, table, weight):
    rows = q_ref.shape[0]
    for h in range(q_ref.shape[1] // HEAD_DIM):
        q_all[h * rows : (h + 1) * rows, :] = q_ref[:, h * HEAD_DIM : (h + 1) * HEAD_DIM]
    res_out[...] = res_ref[...]
    z, yh = where_ref[0], lax.div(where_ref[1], 2)
    picks = pick_table(z, yh, ids_ref)
    table[...] = jnp.concatenate([t.astype(f32) for t in picks], axis=0).astype(bf16)
    for g, pick in enumerate(picks):
        e = group_expert(z, yh, g)
        gate = jnp.where(ids_ref[0:1, :] == e, gates_ref[0:1, :], 0.0)
        gate = gate + jnp.where(ids_ref[1:2, :] == e, gates_ref[1:2, :], 0.0)
        weight[g * PAD : (g + 1) * PAD, :] = jnp.where(pick, gate, 0.0)


def pack_kv_kernel(where_ref, tract, cache, *refs):
    from_z, outs = refs[: NZ - 1], refs[NZ - 1 :]
    n = tract.shape[1]
    y, core = where_ref[1], where_ref[2]
    later = [y + s < NY for s in SHIFTS] + [core == 0]
    for out, is_later in zip(outs, later):
        out[:, 0:n] = jnp.where(is_later, tract[...], cache[...])
        for i, ref in enumerate(from_z):
            out[:, (i + 1) * n : (i + 2) * n] = ref[...]


SCALE = math.log2(math.e) / math.sqrt(HEAD_DIM)
BY_ROWS = (((1,), (1,)), ((), ()))


def attend_piece(q, k, v, m, l, acc):
    s = lax.dot_general(q, k, BY_ROWS, preferred_element_type=f32) * SCALE
    m_new = jnp.maximum(m, jnp.max(s, axis=1, keepdims=True))
    fade = jnp.exp2(m - m_new)
    p = jnp.exp2(s - m_new)
    l = l * fade + jnp.sum(p, axis=1, keepdims=True)
    acc = acc * fade + jnp.dot(p.astype(bf16), v, preferred_element_type=f32)
    return m_new, l, acc


def attend_own_kernel(q_all, tract_ref, cache_ref, *refs):
    kv_refs, (m_ref, l_ref, acc_ref) = refs[:-3], refs[-3:]
    rows = tract_ref.shape[1]
    tile = 2 * rows
    row_at = lax.rem(lax.broadcasted_iota(jnp.int32, (tile, rows), 0), rows)
    col_at = lax.broadcasted_iota(jnp.int32, (tile, rows), 1)
    tract = col_at <= row_at

    def group(g, carry):
        at = pl.ds(pl.multiple_of(g * tile, tile), tile)
        q = q_all[at, :]
        s_tract = lax.dot_general(q, tract_ref[0], BY_ROWS, preferred_element_type=f32)
        s_cache = lax.dot_general(q, cache_ref[0], BY_ROWS, preferred_element_type=f32)
        s = jnp.where(tract, s_tract, s_cache) * SCALE
        m = jnp.max(s, axis=1, keepdims=True)
        p = jnp.exp2(s - m)
        l = jnp.sum(p, axis=1, keepdims=True)
        low = p.astype(bf16)
        zero = jnp.zeros_like(low)
        acc = jnp.dot(jnp.where(tract, low, zero), tract_ref[1], preferred_element_type=f32)
        acc += jnp.dot(jnp.where(tract, zero, low), cache_ref[1], preferred_element_type=f32)
        for i, ref in enumerate(kv_refs):
            keys = slice(0 if i else rows, ref.shape[1])
            m, l, acc = attend_piece(q, ref[0, keys], ref[1, keys], m, l, acc)
        m_ref[at, :] = jnp.broadcast_to(m, acc.shape)
        l_ref[at, :] = jnp.broadcast_to(l, acc.shape)
        acc_ref[at, :] = acc
        return carry

    lax.fori_loop(0, q_all.shape[0] // tile, group, 0)


def attend_more_kernel(q_all, m_ref, l_ref, acc_ref, *refs):
    kv_refs, (m_out, l_out, acc_out) = refs[:-3], refs[-3:]
    tile = 256

    def group(g, carry):
        at = pl.ds(pl.multiple_of(g * tile, tile), tile)
        q = q_all[at, :]
        m, l, acc = m_ref[at, :][:, :1], l_ref[at, :][:, :1], acc_ref[at, :]
        for ref in kv_refs:
            m, l, acc = attend_piece(q, ref[0], ref[1], m, l, acc)
        m_out[at, :] = jnp.broadcast_to(m, acc.shape)
        l_out[at, :] = jnp.broadcast_to(l, acc.shape)
        acc_out[at, :] = acc
        return carry

    lax.fori_loop(0, q_all.shape[0] // tile, group, 0)


def attend_kernel(q_all, res_ref, table, m_ref, l_ref, acc_ref, *refs):
    kv_refs, hid_ref, z_refs, o_all = refs[:NC], refs[NC], refs[NC + 1 : -1], refs[-1]
    rows, width = res_ref.shape
    heads = width // HEAD_DIM
    tile = 2 * rows

    def group(g, carry):
        at = pl.ds(pl.multiple_of(g * tile, tile), tile)
        q = q_all[at, :]
        m, l, acc = m_ref[at, :][:, :1], l_ref[at, :][:, :1], acc_ref[at, :]
        for ref in kv_refs:
            m, l, acc = attend_piece(q, ref[0], ref[1], m, l, acc)
        o_all[at, :] = acc / l
        return carry

    lax.fori_loop(0, heads * rows // tile, group, 0)
    for h in range(heads):
        cols = slice(h * HEAD_DIM, (h + 1) * HEAD_DIM)
        attended = o_all[h * rows : (h + 1) * rows, :]
        hid_ref[:, cols] = (res_ref[:, cols].astype(f32) + attended).astype(bf16)
    routed = jnp.dot(table[...], hid_ref[...], preferred_element_type=f32).astype(bf16)
    for g in range(EXPERTS):
        z_refs[g // 2][(g % 2) * CAP : (g % 2 + 1) * CAP, :] = routed[g * PAD : g * PAD + CAP]


def merge_kernel(*refs):
    keep, away = refs[NZ:]
    for d, ref in zip((0,) + SHIFTS, refs[:NZ]):
        keep[d * CAP : (d + 1) * CAP, :] = ref[:CAP]
        away[d * CAP : (d + 1) * CAP, :] = ref[CAP:]


def expert_kernel(stacks, pairs, where_ref, gain_ref, *refs):
    refs = list(refs)
    take = lambda n: [refs.pop(0) for _ in range(n)]
    stack_in, pair_in = take(stacks), take(NX * pairs)
    weights = take(6)
    stack_out, pair_out = take(stacks), take(NX * pairs)
    normed, act, gate_v, up_v, down_v, sems = refs
    total, ff = weights[0].shape
    width = total // NX
    rows = normed.shape[0] // (stacks + 2 * pairs)
    gate_loads, up_loads, down_loads = [
        [pltpu.make_async_copy(weights[3 * h + j], place(h), sems.at[h, j]) for h in range(2)]
        for j, place in enumerate(
            (
                lambda h: gate_v.at[h],
                lambda h: up_v.at[h],
                lambda h: down_v.at[pl.ds(h * ff, ff)],
            )
        )
    ]
    for c in (gate_loads[0], up_loads[0], gate_loads[1], up_loads[1], *down_loads):
        c.start()
    x = where_ref[3]
    order = (0,) + SHIFTS

    def place(r, shift, v, inverse):
        src = lax.rem(x - shift + NX, NX)
        cols = pl.ds(pl.multiple_of(src * width, width), width)
        v = v.astype(f32) * inverse * gain_ref[src]
        normed[r * rows : (r + 1) * rows, cols] = v.astype(bf16)

    def square(v, sq):
        v = v.astype(f32)
        return sq + jnp.sum(v * v, axis=1, keepdims=True)

    for r, ref in enumerate(stack_in):
        sq = lax.fori_loop(0, NX, lambda i, sq: square(ref[i], sq), jnp.zeros((rows, 1), f32))
        inverse = lax.rsqrt(sq * (1.0 / total) + EPS)

        def put(i, carry):
            place(r, i ^ (i >> 1), ref[i], inverse)
            return carry

        lax.fori_loop(0, NX, put, 0)
    for r in range(2 * pairs):
        sq = jnp.zeros((rows, 1), f32)
        for ref in pair_in:
            sq = square(ref[r], sq)
        inverse = lax.rsqrt(sq * (1.0 / total) + EPS)
        for shift, ref in zip(order, pair_in):
            place(stacks + r, shift, ref[r], inverse)

    def hidden_units(half, carry):
        for j, v in enumerate((gate_v, up_v)):
            pltpu.make_async_copy(v.at[half], v.at[half], sems.at[half, j]).wait()
        gate = jnp.dot(normed[...], gate_v[half], preferred_element_type=f32)
        up = jnp.dot(normed[...], up_v[half], preferred_element_type=f32)
        low = (gate / (1.0 + jnp.exp(-gate)) * up).astype(bf16)
        act[:, pl.ds(pl.multiple_of(half * ff, ff), ff)] = low
        return carry

    lax.fori_loop(0, 2, hidden_units, 0)
    for c in down_loads:
        c.wait()
    for i, shift in enumerate(order):
        cols = pl.ds(pl.multiple_of(lax.rem(x + shift, NX) * width, width), width)
        out = jnp.dot(act[...], down_v[:, cols], preferred_element_type=f32).astype(bf16)
        for r, ref in enumerate(stack_out):
            ref[i] = out[r * rows : (r + 1) * rows]
        for r in range(2 * pairs):
            at = (stacks + r) * rows
            pair_out[i][r] = out[at : at + rows]


def experts(where, gain, stacks, pairs, own, other, name):
    rows, width = stacks[0].shape[1:]
    total, ff = own[0].shape
    groups = 1 if pairs else 0
    n = rows * (len(stacks) + 2 * groups)

    def body(*refs):
        expert_kernel(len(stacks), groups, *refs)

    return call(
        body,
        [jax.ShapeDtypeStruct(v.shape, bf16) for v in (*stacks, *pairs)],
        [where, gain, *stacks, *pairs, *own, *other],
        name,
        [pltpu.VMEM((n, total), bf16), pltpu.VMEM((n, 2 * ff), bf16)]
        + [pltpu.VMEM((2, total, ff), bf16)] * 2
        + [pltpu.VMEM((2 * ff, total), bf16), pltpu.SemaphoreType.DMA((2, 3))],
        limit=LIMIT,
        scalars=1,
        hbm=6,
    )


def first_sum_kernel(*refs):
    a_own, a_got, b_own, b_got = refs[0], refs[1], refs[2], refs[3 : 2 + NX]
    a_out, b_out = refs[2 + NX : 2 + 2 * NX], refs[2 + 2 * NX :]
    for i, out in enumerate(a_out):
        out[...] = (a_own[i].astype(f32) + a_got[i].astype(f32)).astype(bf16)
    for r in range(2):
        total = b_own[r].astype(f32)
        for got in b_got:
            total = total + got[r].astype(f32)
        b_out[r][...] = total.astype(bf16)


def last_sum_kernel(*refs):
    parts, back, outs = refs[:NX], refs[NX], refs[NX + 1 :]
    total = parts[0][...].astype(f32)
    for ref in parts[1:]:
        total = total + ref[...].astype(f32)
    total = total.astype(bf16)
    for d, out in enumerate(outs):
        out[:CAP] = total[d * CAP : (d + 1) * CAP]
        out[CAP:] = back[d * CAP : (d + 1) * CAP, :]


def mix_kernel(weight_ref, hid_ref, *refs):
    part_refs, out_ref, held = refs[:NZ], refs[NZ], refs[NZ + 1]
    held[...] = jnp.zeros_like(held)
    for g in range(EXPERTS):
        part = part_refs[(0, 3, 1, 2).index(g // 2)][(g % 2) * CAP : (g % 2 + 1) * CAP, :]
        held[g * PAD : g * PAD + CAP, :] = part.astype(f32)
    mixture = lax.dot_general(
        weight_ref[...],
        held[...],
        (((0,), (0,)), ((), ())),
        precision=lax.Precision.HIGHEST,
        preferred_element_type=f32,
    )
    out_ref[...] = (hid_ref[...].astype(f32) + mixture).astype(bf16)


SWAP = [(0, 1), (1, 0)]


def turn(v, axis, shift):
    n = 4
    return lax.ppermute(v, axis, [(i, (i + shift) % n) for i in range(n)])


def turned(parts, axis, order):
    got = {i: turn(parts[i], axis, SHIFTS[i]) for i in order}
    return [got[i] for i in range(len(parts))]


def together(parts, order):
    got = dict(zip(order, lax.optimization_barrier([parts[i] for i in order])))
    return [got[i] for i in range(len(parts))]


def cross(v):
    return lax.ppermute(v, ("yh", "yl"), [(i, NY - 1 - i) for i in range(NY)])


def swap_y(v):
    return lax.ppermute(v, "yl", SWAP)


def swap_core(v):
    return lax.ppermute(v, "core", SWAP)


def per_device(
    queries, keys, values, cache_keys, cache_values, residual, norm_gain, w_gate, w_up, w_down, expert_ids, gate_weights
):
    rows, width = queries.shape
    heads = width // HEAD_DIM
    z = lax.axis_index("zh")
    y = lax.axis_index(("yh", "yl"))
    where = jnp.stack((z, y, lax.axis_index("core"), lax.axis_index("x"))).astype(jnp.int32)
    ids, gates = expert_ids.T, gate_weights.T
    shaped = lambda *dims: jax.ShapeDtypeStruct(dims, bf16)

    near, past = jnp.stack((keys, values)), jnp.stack((cache_keys, cache_values))
    from_z = turned([jnp.where(z + s < NZ, near, past) for s in SHIFTS], "zh", KV_ORDER)
    slots = EXPERTS * PAD
    q_all, res, table, weight = call(
        prep_kernel,
        [
            shaped(heads * rows, HEAD_DIM),
            shaped(rows, width),
            shaped(slots, rows),
            jax.ShapeDtypeStruct((slots, rows), f32),
        ],
        [where, ids, gates, queries, residual],
        "prep",
        scalars=1,
    )
    packed = call(
        pack_kv_kernel,
        [shaped(2, NZ * rows, HEAD_DIM)] * 4,
        [where, near, past, *[from_z[i] for i in (1, 2, 0)]],
        "pack_kv",
        scalars=1,
    )
    packed, other_gate = lax.optimization_barrier((packed, swap_core(w_gate)))
    held = lax.optimization_barrier((w_up, packed[0]))[0]
    partner = swap_core(packed[3])
    y_1, y_3 = turn(packed[0], ("yh", "yl"), 1), turn(packed[1], ("yh", "yl"), 3)
    state = [jax.ShapeDtypeStruct((heads * rows, HEAD_DIM), f32)] * 3
    carried = call(attend_own_kernel, state, [q_all, near, past, packed[3], partner], "attend_own")
    carried, y_1, y_3, last, other_up = lax.optimization_barrier(
        (carried, y_1, y_3, packed[2], swap_core(held))
    )
    y_2 = turn(last, ("yh", "yl"), 2)
    far_1, far_3 = swap_core(y_1), swap_core(y_3)
    carried = call(attend_more_kernel, state, [q_all, *carried, y_1, y_3, far_1, far_3], "attend_more")
    carried, y_2 = lax.optimization_barrier((carried, y_2))
    far_2 = swap_core(y_2)
    held = lax.optimization_barrier((w_down, far_2))[0]
    own, other = (w_gate, w_up, w_down), (other_gate, other_up, swap_core(held))
    hidden, *sent = call(
        attend_kernel,
        [shaped(rows, width)] + [shaped(2 * CAP, width)] * NZ,
        [q_all, res, table, *carried, y_2, far_2],
        "attend",
        [pltpu.VMEM((heads * rows, HEAD_DIM), f32)],
    )

    arrived = [sent[0]] + turned([sent[s] for s in SHIFTS], "zh", Z_ORDER)
    arrived, other = lax.optimization_barrier((arrived, other))
    rows_a = shaped(NZ * CAP, width)
    a, away = call(merge_kernel, [rows_a] * 2, arrived, "merge")
    b = cross(away)
    b_far = swap_y(b)
    *a_turned, b_far = together(turned([a] * 3, "x", X_ORDER) + [b_far], (2, 1, 0, 3))
    a_own = jnp.stack([a] + a_turned)
    b_pair = jnp.stack((b, b_far))
    *b_turned, a_far = together(turned([b_pair] * 3, "x", X_ORDER) + [swap_y(a_own)], (2, 1, 0, 3))
    gain = norm_gain.reshape(NX, 1, width)
    a_own = experts(where, gain, [a_own], [], own, other, "experts_own")[0]
    a_far, *b_all = experts(where, gain, [a_far], [b_pair] + b_turned, own, other, "experts")

    *b_turned, a_far = lax.optimization_barrier(
        [turn(v, "x", s) for v, s in zip(b_all[1:], SHIFTS)] + [swap_y(a_far)]
    )
    *a_sums, b_own, b_far = call(
        first_sum_kernel, [rows_a] * (NX + 2), [a_own, a_far, b_all[0], *b_turned], "first_sum"
    )
    b_sum = (b_own.astype(f32) + swap_y(b_far).astype(f32)).astype(bf16)
    moved = lax.optimization_barrier(
        [turn(v, "x", s) for v, s in zip(a_sums[1:], SHIFTS)] + [cross(b_sum)]
    )
    result = call(
        last_sum_kernel,
        [shaped(2 * CAP, width)] * NZ,
        [a_sums[0], *moved],
        "last_sum",
    )
    back = turned([result[NZ - s] for s in SHIFTS], "zh", Z_ORDER)
    back = [result[0]] + back
    return call(
        mix_kernel,
        shaped(rows, width),
        [weight, hidden, *back],
        "mix",
        [pltpu.VMEM((EXPERTS * PAD, width), f32)],
    )


def solution(mesh):
    fine = Mesh(mesh.devices.reshape(2, 4, 2, 2, 2, 4), ("dp", "zh", "yh", "yl", "core", "x"))
    ctx = ("zh", "yh", "yl", "core")
    tok = P(("dp",) + ctx, "x")
    in_specs = (
        tok, tok, tok, tok, tok, tok,
        P(),
        P(None, ctx + ("x",)),
        P(None, ctx + ("x",)),
        P(ctx + ("x",), None),
        P(("dp",) + ctx, None),
        P(("dp",) + ctx, None),
    )
    return jax.shard_map(per_device, mesh=fine, in_specs=in_specs, out_specs=tok, check_vma=False)
```

```python
import math

import jax
import jax.numpy as jnp
from jax import lax
from jax.experimental import pallas as pl
from jax.experimental.pallas import tpu as pltpu
from jax.sharding import Mesh, PartitionSpec as P

HEADS = 24
KV_HEADS = 4
HEAD_DIM = 128
EXPERTS = 8
TOP = 2
CAP = 36
PAD = 40
EPS = 1e-05
NZ, NY, NX, NC = 4, 4, 4, 2
SHIFTS = (1, 3, 2)
KV_ORDER, Z_ORDER, X_ORDER = (0, 1, 2), (0, 1, 2), (2, 1, 0)
MB = 1024 * 1024
LIMIT = 20

bf16 = jnp.bfloat16
f32 = jnp.float32
VM = pl.BlockSpec(memory_space=pltpu.VMEM)
SM = pl.BlockSpec(memory_space=pltpu.SMEM)
HBM = pl.BlockSpec(memory_space=pltpu.HBM)


def call(body, out_shape, args, name, scratch=(), limit=16, scalars=0, hbm=0):
    many = isinstance(out_shape, list)
    return pl.pallas_call(
        body,
        out_shape=out_shape,
        in_specs=[SM] * scalars + [VM] * (len(args) - scalars - hbm) + [HBM] * hbm,
        out_specs=[VM] * len(out_shape) if many else VM,
        scratch_shapes=list(scratch),
        compiler_params=pltpu.CompilerParams(vmem_limit_bytes=limit * MB),
        name=name,
    )(*args)


def group_expert(z, yh, g):
    return lax.rem(z + g // 2, NZ) * 2 + lax.rem(yh + g % 2, 2)


def pick_table(z, yh, ids_ref):
    n = ids_ref.shape[1]
    first, second = ids_ref[0:1, :], ids_ref[1:2, :]
    line = lax.broadcasted_iota(jnp.int32, (EXPERTS, n), 0)
    expert = jnp.zeros((EXPERTS, n), jnp.int32)
    for g in range(EXPERTS):
        expert = jnp.where(line == g, group_expert(z, yh, g), expert)
    named = (first == expert) | (second == expert)
    earlier = (
        lax.broadcasted_iota(jnp.int32, (n, n), 0) < lax.broadcasted_iota(jnp.int32, (n, n), 1)
    ).astype(bf16)
    rank = jnp.dot(named.astype(bf16), earlier, preferred_element_type=f32).astype(jnp.int32)
    rank = jnp.where(named, rank, -1)
    row = lax.broadcasted_iota(jnp.int32, (PAD, n), 0)
    return [rank[g : g + 1, :] == row for g in range(EXPERTS)]


def prep_kernel(where_ref, ids_ref, gates_ref, q_ref, res_ref, q_all, res_out, table, weight):
    rows = q_ref.shape[0]
    for h in range(q_ref.shape[1] // HEAD_DIM):
        q_all[h * rows : (h + 1) * rows, :] = q_ref[:, h * HEAD_DIM : (h + 1) * HEAD_DIM]
    res_out[...] = res_ref[...]
    z, yh = where_ref[0], lax.div(where_ref[1], 2)
    picks = pick_table(z, yh, ids_ref)
    table[...] = jnp.concatenate([t.astype(f32) for t in picks], axis=0).astype(bf16)
    for g, pick in enumerate(picks):
        e = group_expert(z, yh, g)
        gate = jnp.where(ids_ref[0:1, :] == e, gates_ref[0:1, :], 0.0)
        gate = gate + jnp.where(ids_ref[1:2, :] == e, gates_ref[1:2, :], 0.0)
        weight[g * PAD : (g + 1) * PAD, :] = jnp.where(pick, gate, 0.0)


def pack_kv_kernel(where_ref, tract, cache, *refs):
    from_z, outs = refs[: NZ - 1], refs[NZ - 1 :]
    n = tract.shape[1]
    y, core = where_ref[1], where_ref[2]
    later = [y + s < NY for s in SHIFTS] + [core == 0]
    for out, is_later in zip(outs, later):
        out[:, 0:n] = jnp.where(is_later, tract[...], cache[...])
        for i, ref in enumerate(from_z):
            out[:, (i + 1) * n : (i + 2) * n] = ref[...]


SCALE = math.log2(math.e) / math.sqrt(HEAD_DIM)
BY_ROWS = (((1,), (1,)), ((), ()))


def attend_piece(q, k, v, m, l, acc):
    s = lax.dot_general(q, k, BY_ROWS, preferred_element_type=f32) * SCALE
    m_new = jnp.maximum(m, jnp.max(s, axis=1, keepdims=True))
    fade = jnp.exp2(m - m_new)
    p = jnp.exp2(s - m_new)
    l = l * fade + jnp.sum(p, axis=1, keepdims=True)
    acc = acc * fade + jnp.dot(p.astype(bf16), v, preferred_element_type=f32)
    return m_new, l, acc


def attend_own_kernel(q_all, tract_ref, cache_ref, *refs):
    kv_refs, (m_ref, l_ref, acc_ref) = refs[:-3], refs[-3:]
    rows = tract_ref.shape[1]
    tile = 2 * rows
    row_at = lax.rem(lax.broadcasted_iota(jnp.int32, (tile, rows), 0), rows)
    col_at = lax.broadcasted_iota(jnp.int32, (tile, rows), 1)
    tract = col_at <= row_at

    def group(g, carry):
        at = pl.ds(pl.multiple_of(g * tile, tile), tile)
        q = q_all[at, :]
        s_tract = lax.dot_general(q, tract_ref[0], BY_ROWS, preferred_element_type=f32)
        s_cache = lax.dot_general(q, cache_ref[0], BY_ROWS, preferred_element_type=f32)
        s = jnp.where(tract, s_tract, s_cache) * SCALE
        m = jnp.max(s, axis=1, keepdims=True)
        p = jnp.exp2(s - m)
        l = jnp.sum(p, axis=1, keepdims=True)
        low = p.astype(bf16)
        zero = jnp.zeros_like(low)
        acc = jnp.dot(jnp.where(tract, low, zero), tract_ref[1], preferred_element_type=f32)
        acc += jnp.dot(jnp.where(tract, zero, low), cache_ref[1], preferred_element_type=f32)
        for i, ref in enumerate(kv_refs):
            keys = slice(0 if i else rows, ref.shape[1])
            m, l, acc = attend_piece(q, ref[0, keys], ref[1, keys], m, l, acc)
        m_ref[at, :] = jnp.broadcast_to(m, acc.shape)
        l_ref[at, :] = jnp.broadcast_to(l, acc.shape)
        acc_ref[at, :] = acc
        return carry

    lax.fori_loop(0, q_all.shape[0] // tile, group, 0)


def attend_more_kernel(q_all, m_ref, l_ref, acc_ref, *refs):
    kv_refs, (m_out, l_out, acc_out) = refs[:-3], refs[-3:]
    tile = 256

    def group(g, carry):
        at = pl.ds(pl.multiple_of(g * tile, tile), tile)
        q = q_all[at, :]
        m, l, acc = m_ref[at, :][:, :1], l_ref[at, :][:, :1], acc_ref[at, :]
        for ref in kv_refs:
            m, l, acc = attend_piece(q, ref[0], ref[1], m, l, acc)
        m_out[at, :] = jnp.broadcast_to(m, acc.shape)
        l_out[at, :] = jnp.broadcast_to(l, acc.shape)
        acc_out[at, :] = acc
        return carry

    lax.fori_loop(0, q_all.shape[0] // tile, group, 0)


def attend_kernel(q_all, res_ref, table, m_ref, l_ref, acc_ref, *refs):
    kv_refs, hid_ref, z_refs, o_all = refs[:NC], refs[NC], refs[NC + 1 : -1], refs[-1]
    rows, width = res_ref.shape
    heads = width // HEAD_DIM
    tile = 2 * rows

    def group(g, carry):
        at = pl.ds(pl.multiple_of(g * tile, tile), tile)
        q = q_all[at, :]
        m, l, acc = m_ref[at, :][:, :1], l_ref[at, :][:, :1], acc_ref[at, :]
        for ref in kv_refs:
            m, l, acc = attend_piece(q, ref[0], ref[1], m, l, acc)
        o_all[at, :] = acc / l
        return carry

    lax.fori_loop(0, heads * rows // tile, group, 0)
    for h in range(heads):
        cols = slice(h * HEAD_DIM, (h + 1) * HEAD_DIM)
        attended = o_all[h * rows : (h + 1) * rows, :]
        hid_ref[:, cols] = (res_ref[:, cols].astype(f32) + attended).astype(bf16)
    routed = jnp.dot(table[...], hid_ref[...], preferred_element_type=f32).astype(bf16)
    for g in range(EXPERTS):
        z_refs[g // 2][(g % 2) * CAP : (g % 2 + 1) * CAP, :] = routed[g * PAD : g * PAD + CAP]


def merge_kernel(*refs):
    keep, away = refs[NZ:]
    for d, ref in zip((0,) + SHIFTS, refs[:NZ]):
        keep[d * CAP : (d + 1) * CAP, :] = ref[:CAP]
        away[d * CAP : (d + 1) * CAP, :] = ref[CAP:]


def expert_kernel(stacks, pairs, where_ref, gain_ref, *refs):
    refs = list(refs)
    take = lambda n: [refs.pop(0) for _ in range(n)]
    stack_in, pair_in, weights = take(stacks), take(NX * pairs), take(6)
    stack_out, pair_out = take(stacks), take(NX * pairs)
    normed, act = refs
    total, ff = weights[0].shape
    width = total // NX
    rows = normed.shape[0] // (stacks + 2 * pairs)
    x = where_ref[3]
    order = (0,) + SHIFTS

    def place(r, shift, v, inverse):
        src = lax.rem(x - shift + NX, NX)
        cols = pl.ds(pl.multiple_of(src * width, width), width)
        v = v.astype(f32) * inverse * gain_ref[src]
        normed[r * rows : (r + 1) * rows, cols] = v.astype(bf16)

    def square(v, sq):
        v = v.astype(f32)
        return sq + jnp.sum(v * v, axis=1, keepdims=True)

    for r, ref in enumerate(stack_in):
        sq = lax.fori_loop(0, NX, lambda i, sq: square(ref[i], sq), jnp.zeros((rows, 1), f32))
        inverse = lax.rsqrt(sq * (1.0 / total) + EPS)

        def put(i, carry):
            place(r, i ^ (i >> 1), ref[i], inverse)
            return carry

        lax.fori_loop(0, NX, put, 0)
    for r in range(2 * pairs):
        sq = jnp.zeros((rows, 1), f32)
        for ref in pair_in:
            sq = square(ref[r], sq)
        inverse = lax.rsqrt(sq * (1.0 / total) + EPS)
        for shift, ref in zip(order, pair_in):
            place(stacks + r, shift, ref[r], inverse)

    tile = 256
    for half in range(2):
        w_gate, w_up, _ = weights[3 * half : 3 * half + 3]

        def units(j, carry):
            cols = pl.ds(pl.multiple_of(j * tile, tile), tile)
            gate = jnp.dot(normed[...], w_gate[:, cols], preferred_element_type=f32)
            up = jnp.dot(normed[...], w_up[:, cols], preferred_element_type=f32)
            at = pl.ds(pl.multiple_of(half * ff + j * tile, tile), tile)
            act[:, at] = (gate / (1.0 + jnp.exp(-gate)) * up).astype(bf16)
            return carry

        lax.fori_loop(0, ff // tile, units, 0)
    for i, shift in enumerate(order):
        start = lax.rem(x + shift, NX) * width

        def down(j, carry):
            cols = pl.ds(pl.multiple_of(start + j * tile, tile), tile)
            out = jnp.dot(act[:, :ff], weights[2][:, cols], preferred_element_type=f32)
            out += jnp.dot(act[:, ff:], weights[5][:, cols], preferred_element_type=f32)
            out = out.astype(bf16)
            at = pl.ds(pl.multiple_of(j * tile, tile), tile)
            for r, ref in enumerate(stack_out):
                ref[i, :, at] = out[r * rows : (r + 1) * rows]
            for r in range(2 * pairs):
                first = (stacks + r) * rows
                pair_out[i][r, :, at] = out[first : first + rows]
            return carry

        lax.fori_loop(0, width // tile, down, 0)


def experts(where, gain, stacks, pairs, weights, name):
    rows, width = stacks[0].shape[1:]
    total, ff = weights[0].shape
    groups = 1 if pairs else 0
    n = rows * (len(stacks) + 2 * groups)

    def body(*refs):
        expert_kernel(len(stacks), groups, *refs)

    return call(
        body,
        [jax.ShapeDtypeStruct(v.shape, bf16) for v in (*stacks, *pairs)],
        [where, gain, *stacks, *pairs, *weights],
        name,
        [pltpu.VMEM((n, total), bf16), pltpu.VMEM((n, 2 * ff), bf16)],
        limit=LIMIT,
        scalars=1,
    )


def first_sum_kernel(*refs):
    a_own, a_got, b_own, b_got = refs[0], refs[1], refs[2], refs[3 : 2 + NX]
    a_out, b_out = refs[2 + NX : 2 + 2 * NX], refs[2 + 2 * NX :]
    for i, out in enumerate(a_out):
        out[...] = (a_own[i].astype(f32) + a_got[i].astype(f32)).astype(bf16)
    for r in range(2):
        total = b_own[r].astype(f32)
        for got in b_got:
            total = total + got[r].astype(f32)
        b_out[r][...] = total.astype(bf16)


def last_sum_kernel(*refs):
    parts, back, outs = refs[:NX], refs[NX], refs[NX + 1 :]
    total = parts[0][...].astype(f32)
    for ref in parts[1:]:
        total = total + ref[...].astype(f32)
    total = total.astype(bf16)
    for d, out in enumerate(outs):
        out[:CAP] = total[d * CAP : (d + 1) * CAP]
        out[CAP:] = back[d * CAP : (d + 1) * CAP, :]


def mix_kernel(weight_ref, hid_ref, *refs):
    part_refs, out_ref, held = refs[:NZ], refs[NZ], refs[NZ + 1]
    held[...] = jnp.zeros_like(held)
    for g in range(EXPERTS):
        part = part_refs[(0, 3, 1, 2).index(g // 2)][(g % 2) * CAP : (g % 2 + 1) * CAP, :]
        held[g * PAD : g * PAD + CAP, :] = part.astype(f32)
    mixture = lax.dot_general(
        weight_ref[...],
        held[...],
        (((0,), (0,)), ((), ())),
        precision=lax.Precision.HIGHEST,
        preferred_element_type=f32,
    )
    out_ref[...] = (hid_ref[...].astype(f32) + mixture).astype(bf16)


SWAP = [(0, 1), (1, 0)]


def turn(v, axis, shift):
    n = 4
    return lax.ppermute(v, axis, [(i, (i + shift) % n) for i in range(n)])


def turned(parts, axis, order):
    got = {i: turn(parts[i], axis, SHIFTS[i]) for i in order}
    return [got[i] for i in range(len(parts))]


def together(parts, order):
    got = dict(zip(order, lax.optimization_barrier([parts[i] for i in order])))
    return [got[i] for i in range(len(parts))]


def cross(v):
    return lax.ppermute(v, ("yh", "yl"), [(i, NY - 1 - i) for i in range(NY)])


def swap_y(v):
    return lax.ppermute(v, "yl", SWAP)


def swap_core(v):
    return lax.ppermute(v, "core", SWAP)


def per_device(
    queries, keys, values, cache_keys, cache_values, residual, norm_gain, w_gate, w_up, w_down, expert_ids, gate_weights
):
    rows, width = queries.shape
    heads = width // HEAD_DIM
    z = lax.axis_index("zh")
    y = lax.axis_index(("yh", "yl"))
    where = jnp.stack((z, y, lax.axis_index("core"), lax.axis_index("x"))).astype(jnp.int32)
    ids, gates = expert_ids.T, gate_weights.T
    shaped = lambda *dims: jax.ShapeDtypeStruct(dims, bf16)

    near, past = jnp.stack((keys, values)), jnp.stack((cache_keys, cache_values))
    from_z = turned([jnp.where(z + s < NZ, near, past) for s in SHIFTS], "zh", KV_ORDER)
    slots = EXPERTS * PAD
    q_all, res, table, weight = call(
        prep_kernel,
        [
            shaped(heads * rows, HEAD_DIM),
            shaped(rows, width),
            shaped(slots, rows),
            jax.ShapeDtypeStruct((slots, rows), f32),
        ],
        [where, ids, gates, queries, residual],
        "prep",
        scalars=1,
    )
    packed = call(
        pack_kv_kernel,
        [shaped(2, NZ * rows, HEAD_DIM)] * 4,
        [where, near, past, *[from_z[i] for i in (1, 2, 0)]],
        "pack_kv",
        scalars=1,
    )
    packed, other_gate = lax.optimization_barrier((packed, swap_core(w_gate)))
    held = lax.optimization_barrier((w_up, packed[0]))[0]
    partner = swap_core(packed[3])
    y_1, y_3 = turn(packed[0], ("yh", "yl"), 1), turn(packed[1], ("yh", "yl"), 3)
    state = [jax.ShapeDtypeStruct((heads * rows, HEAD_DIM), f32)] * 3
    carried = call(attend_own_kernel, state, [q_all, near, past, packed[3], partner], "attend_own")
    carried, y_1, y_3, last, other_up = lax.optimization_barrier(
        (carried, y_1, y_3, packed[2], swap_core(held))
    )
    y_2 = turn(last, ("yh", "yl"), 2)
    far_1, far_3 = swap_core(y_1), swap_core(y_3)
    carried = call(attend_more_kernel, state, [q_all, *carried, y_1, y_3, far_1, far_3], "attend_more")
    carried, y_2 = lax.optimization_barrier((carried, y_2))
    far_2 = swap_core(y_2)
    held = lax.optimization_barrier((w_down, far_2))[0]
    own, other = (w_gate, w_up, w_down), (other_gate, other_up, swap_core(held))
    hidden, *sent = call(
        attend_kernel,
        [shaped(rows, width)] + [shaped(2 * CAP, width)] * NZ,
        [q_all, res, table, *carried, y_2, far_2],
        "attend",
        [pltpu.VMEM((heads * rows, HEAD_DIM), f32)],
    )

    arrived = [sent[0]] + turned([sent[s] for s in SHIFTS], "zh", Z_ORDER)
    arrived, other = lax.optimization_barrier((arrived, other))
    rows_a = shaped(NZ * CAP, width)
    a, away = call(merge_kernel, [rows_a] * 2, arrived, "merge")
    b = cross(away)
    b_far = swap_y(b)
    *a_turned, b_far = together(turned([a] * 3, "x", X_ORDER) + [b_far], (2, 1, 0, 3))
    a_own = jnp.stack([a] + a_turned)
    b_pair = jnp.stack((b, b_far))
    *b_turned, a_far = together(turned([b_pair] * 3, "x", X_ORDER) + [swap_y(a_own)], (2, 1, 0, 3))
    gain = norm_gain.reshape(NX, 1, width)
    weights = (*own, *other)
    a_own = experts(where, gain, [a_own], [], weights, "experts_own")[0]
    a_far, *b_all = experts(where, gain, [a_far], [b_pair] + b_turned, weights, "experts")

    *b_turned, a_far = lax.optimization_barrier(
        [turn(v, "x", s) for v, s in zip(b_all[1:], SHIFTS)] + [swap_y(a_far)]
    )
    *a_sums, b_own, b_far = call(
        first_sum_kernel, [rows_a] * (NX + 2), [a_own, a_far, b_all[0], *b_turned], "first_sum"
    )
    b_sum = (b_own.astype(f32) + swap_y(b_far).astype(f32)).astype(bf16)
    moved = lax.optimization_barrier(
        [turn(v, "x", s) for v, s in zip(a_sums[1:], SHIFTS)] + [cross(b_sum)]
    )
    result = call(
        last_sum_kernel,
        [shaped(2 * CAP, width)] * NZ,
        [a_sums[0], *moved],
        "last_sum",
    )
    back = turned([result[NZ - s] for s in SHIFTS], "zh", Z_ORDER)
    back = [result[0]] + back
    return call(
        mix_kernel,
        shaped(rows, width),
        [weight, hidden, *back],
        "mix",
        [pltpu.VMEM((EXPERTS * PAD, width), f32)],
    )


def solution(mesh):
    fine = Mesh(mesh.devices.reshape(2, 4, 2, 2, 2, 4), ("dp", "zh", "yh", "yl", "core", "x"))
    ctx = ("zh", "yh", "yl", "core")
    tok = P(("dp",) + ctx, "x")
    in_specs = (
        tok, tok, tok, tok, tok, tok,
        P(),
        P(None, ctx + ("x",)),
        P(None, ctx + ("x",)),
        P(ctx + ("x",), None),
        P(("dp",) + ctx, None),
        P(("dp",) + ctx, None),
    )
    return jax.shard_map(per_device, mesh=fine, in_specs=in_specs, out_specs=tok, check_vma=False)
```

```python
import math

import jax
import jax.numpy as jnp
from jax import lax
from jax.experimental import pallas as pl
from jax.experimental.pallas import tpu as pltpu
from jax.sharding import Mesh, PartitionSpec as P

HEADS = 24
KV_HEADS = 4
HEAD_DIM = 128
EXPERTS = 8
TOP = 2
CAP = 36
PAD = 40
EPS = 1e-05
NZ, NY, NX, NC = 4, 4, 4, 2
SHIFTS = (1, 3, 2)
KV_ORDER, Z_ORDER, X_ORDER = (0, 1, 2), (0, 1, 2), (2, 1, 0)
MB = 1024 * 1024
LIMIT = 13

bf16 = jnp.bfloat16
f32 = jnp.float32
VM = pl.BlockSpec(memory_space=pltpu.VMEM)
SM = pl.BlockSpec(memory_space=pltpu.SMEM)
HBM = pl.BlockSpec(memory_space=pltpu.HBM)


def call(body, out_shape, args, name, scratch=(), limit=16, scalars=0, hbm=0):
    many = isinstance(out_shape, list)
    return pl.pallas_call(
        body,
        out_shape=out_shape,
        in_specs=[SM] * scalars + [VM] * (len(args) - scalars - hbm) + [HBM] * hbm,
        out_specs=[VM] * len(out_shape) if many else VM,
        scratch_shapes=list(scratch),
        compiler_params=pltpu.CompilerParams(vmem_limit_bytes=limit * MB),
        name=name,
    )(*args)


def group_expert(z, yh, g):
    return lax.rem(z + g // 2, NZ) * 2 + lax.rem(yh + g % 2, 2)


def pick_table(z, yh, ids_ref):
    n = ids_ref.shape[1]
    first, second = ids_ref[0:1, :], ids_ref[1:2, :]
    line = lax.broadcasted_iota(jnp.int32, (EXPERTS, n), 0)
    expert = jnp.zeros((EXPERTS, n), jnp.int32)
    for g in range(EXPERTS):
        expert = jnp.where(line == g, group_expert(z, yh, g), expert)
    named = (first == expert) | (second == expert)
    earlier = (
        lax.broadcasted_iota(jnp.int32, (n, n), 0) < lax.broadcasted_iota(jnp.int32, (n, n), 1)
    ).astype(bf16)
    rank = jnp.dot(named.astype(bf16), earlier, preferred_element_type=f32).astype(jnp.int32)
    rank = jnp.where(named, rank, -1)
    row = lax.broadcasted_iota(jnp.int32, (PAD, n), 0)
    return [rank[g : g + 1, :] == row for g in range(EXPERTS)]


def prep_kernel(where_ref, ids_ref, gates_ref, q_ref, res_ref, q_all, res_out, table, weight):
    rows = q_ref.shape[0]
    for h in range(q_ref.shape[1] // HEAD_DIM):
        q_all[h * rows : (h + 1) * rows, :] = q_ref[:, h * HEAD_DIM : (h + 1) * HEAD_DIM]
    res_out[...] = res_ref[...]
    z, yh = where_ref[0], lax.div(where_ref[1], 2)
    picks = pick_table(z, yh, ids_ref)
    table[...] = jnp.concatenate([t.astype(f32) for t in picks], axis=0).astype(bf16)
    for g, pick in enumerate(picks):
        e = group_expert(z, yh, g)
        gate = jnp.where(ids_ref[0:1, :] == e, gates_ref[0:1, :], 0.0)
        gate = gate + jnp.where(ids_ref[1:2, :] == e, gates_ref[1:2, :], 0.0)
        weight[g * PAD : (g + 1) * PAD, :] = jnp.where(pick, gate, 0.0)


def pack_kv_kernel(where_ref, tract, cache, *refs):
    from_z, outs = refs[: NZ - 1], refs[NZ - 1 :]
    n = tract.shape[1]
    y, core = where_ref[1], where_ref[2]
    later = [y + s < NY for s in SHIFTS] + [core == 0]
    for out, is_later in zip(outs, later):
        out[:, 0:n] = jnp.where(is_later, tract[...], cache[...])
        for i, ref in enumerate(from_z):
            out[:, (i + 1) * n : (i + 2) * n] = ref[...]


SCALE = math.log2(math.e) / math.sqrt(HEAD_DIM)
BY_ROWS = (((1,), (1,)), ((), ()))


def attend_piece(q, k, v, m, l, acc):
    s = lax.dot_general(q, k, BY_ROWS, preferred_element_type=f32) * SCALE
    m_new = jnp.maximum(m, jnp.max(s, axis=1, keepdims=True))
    fade = jnp.exp2(m - m_new)
    p = jnp.exp2(s - m_new)
    l = l * fade + jnp.sum(p, axis=1, keepdims=True)
    acc = acc * fade + jnp.dot(p.astype(bf16), v, preferred_element_type=f32)
    return m_new, l, acc


def attend_own_kernel(q_all, tract_ref, cache_ref, *refs):
    kv_refs, (m_ref, l_ref, acc_ref) = refs[:-3], refs[-3:]
    rows = tract_ref.shape[1]
    tile = 2 * rows
    row_at = lax.rem(lax.broadcasted_iota(jnp.int32, (tile, rows), 0), rows)
    col_at = lax.broadcasted_iota(jnp.int32, (tile, rows), 1)
    tract = col_at <= row_at

    def group(g, carry):
        at = pl.ds(pl.multiple_of(g * tile, tile), tile)
        q = q_all[at, :]
        s_tract = lax.dot_general(q, tract_ref[0], BY_ROWS, preferred_element_type=f32)
        s_cache = lax.dot_general(q, cache_ref[0], BY_ROWS, preferred_element_type=f32)
        s = jnp.where(tract, s_tract, s_cache) * SCALE
        m = jnp.max(s, axis=1, keepdims=True)
        p = jnp.exp2(s - m)
        l = jnp.sum(p, axis=1, keepdims=True)
        low = p.astype(bf16)
        zero = jnp.zeros_like(low)
        acc = jnp.dot(jnp.where(tract, low, zero), tract_ref[1], preferred_element_type=f32)
        acc += jnp.dot(jnp.where(tract, zero, low), cache_ref[1], preferred_element_type=f32)
        for i, ref in enumerate(kv_refs):
            keys = slice(0 if i else rows, ref.shape[1])
            m, l, acc = attend_piece(q, ref[0, keys], ref[1, keys], m, l, acc)
        m_ref[at, :] = jnp.broadcast_to(m, acc.shape)
        l_ref[at, :] = jnp.broadcast_to(l, acc.shape)
        acc_ref[at, :] = acc
        return carry

    lax.fori_loop(0, q_all.shape[0] // tile, group, 0)


def attend_more_kernel(q_all, m_ref, l_ref, acc_ref, *refs):
    kv_refs, (m_out, l_out, acc_out) = refs[:-3], refs[-3:]
    tile = 256

    def group(g, carry):
        at = pl.ds(pl.multiple_of(g * tile, tile), tile)
        q = q_all[at, :]
        m, l, acc = m_ref[at, :][:, :1], l_ref[at, :][:, :1], acc_ref[at, :]
        for ref in kv_refs:
            m, l, acc = attend_piece(q, ref[0], ref[1], m, l, acc)
        m_out[at, :] = jnp.broadcast_to(m, acc.shape)
        l_out[at, :] = jnp.broadcast_to(l, acc.shape)
        acc_out[at, :] = acc
        return carry

    lax.fori_loop(0, q_all.shape[0] // tile, group, 0)


def attend_kernel(q_all, res_ref, table, m_ref, l_ref, acc_ref, *refs):
    kv_refs, hid_ref, z_refs, o_all = refs[:NC], refs[NC], refs[NC + 1 : -1], refs[-1]
    rows, width = res_ref.shape
    heads = width // HEAD_DIM
    tile = 2 * rows

    def group(g, carry):
        at = pl.ds(pl.multiple_of(g * tile, tile), tile)
        q = q_all[at, :]
        m, l, acc = m_ref[at, :][:, :1], l_ref[at, :][:, :1], acc_ref[at, :]
        for ref in kv_refs:
            m, l, acc = attend_piece(q, ref[0], ref[1], m, l, acc)
        o_all[at, :] = acc / l
        return carry

    lax.fori_loop(0, heads * rows // tile, group, 0)
    for h in range(heads):
        cols = slice(h * HEAD_DIM, (h + 1) * HEAD_DIM)
        attended = o_all[h * rows : (h + 1) * rows, :]
        hid_ref[:, cols] = (res_ref[:, cols].astype(f32) + attended).astype(bf16)
    routed = jnp.dot(table[...], hid_ref[...], preferred_element_type=f32).astype(bf16)
    for g in range(EXPERTS):
        z_refs[g // 2][(g % 2) * CAP : (g % 2 + 1) * CAP, :] = routed[g * PAD : g * PAD + CAP]


def merge_kernel(*refs):
    keep, away = refs[NZ:]
    for d, ref in zip((0,) + SHIFTS, refs[:NZ]):
        keep[d * CAP : (d + 1) * CAP, :] = ref[:CAP]
        away[d * CAP : (d + 1) * CAP, :] = ref[CAP:]


def expert_kernel(stacks, pairs, loading, where_ref, gain_ref, *refs):
    refs = list(refs)
    take = lambda n: [refs.pop(0) for _ in range(n)]
    stack_in, pair_in = take(stacks), take(NX * pairs)
    weights = take(6 if loading else 3)
    stack_out, pair_out = take(stacks), take(NX * pairs)
    gate_v, up_v, down_v = take(3) if loading else weights
    normed, act = take(2)
    _, total, ff = gate_v.shape
    width = total // NX
    rows = normed.shape[0] // (stacks + 2 * pairs)
    down_loads = []
    if loading:
        sems = refs[0]
        gate_loads, up_loads, down_loads = [
            [pltpu.make_async_copy(weights[3 * h + j], place(h), sems.at[h, j]) for h in range(2)]
            for j, place in enumerate(
                (
                    lambda h: gate_v.at[h],
                    lambda h: up_v.at[h],
                    lambda h: down_v.at[pl.ds(h * ff, ff)],
                )
            )
        ]
        for c in (gate_loads[0], up_loads[0], gate_loads[1], up_loads[1], *down_loads):
            c.start()
    x = where_ref[3]
    order = (0,) + SHIFTS

    def place(r, shift, v, inverse):
        src = lax.rem(x - shift + NX, NX)
        cols = pl.ds(pl.multiple_of(src * width, width), width)
        v = v.astype(f32) * inverse * gain_ref[src]
        normed[r * rows : (r + 1) * rows, cols] = v.astype(bf16)

    def square(v, sq):
        v = v.astype(f32)
        return sq + jnp.sum(v * v, axis=1, keepdims=True)

    for r, ref in enumerate(stack_in):
        sq = lax.fori_loop(0, NX, lambda i, sq: square(ref[i], sq), jnp.zeros((rows, 1), f32))
        inverse = lax.rsqrt(sq * (1.0 / total) + EPS)

        def put(i, carry):
            place(r, i ^ (i >> 1), ref[i], inverse)
            return carry

        lax.fori_loop(0, NX, put, 0)
    for r in range(2 * pairs):
        sq = jnp.zeros((rows, 1), f32)
        for ref in pair_in:
            sq = square(ref[r], sq)
        inverse = lax.rsqrt(sq * (1.0 / total) + EPS)
        for shift, ref in zip(order, pair_in):
            place(stacks + r, shift, ref[r], inverse)

    def hidden_units(half, carry):
        for j, v in enumerate((gate_v, up_v) if loading else ()):
            pltpu.make_async_copy(v.at[half], v.at[half], sems.at[half, j]).wait()
        gate = jnp.dot(normed[...], gate_v[half], preferred_element_type=f32)
        up = jnp.dot(normed[...], up_v[half], preferred_element_type=f32)
        low = (gate / (1.0 + jnp.exp(-gate)) * up).astype(bf16)
        act[:, pl.ds(pl.multiple_of(half * ff, ff), ff)] = low
        return carry

    lax.fori_loop(0, 2, hidden_units, 0)
    for c in down_loads:
        c.wait()
    for i, shift in enumerate(order):
        cols = pl.ds(pl.multiple_of(lax.rem(x + shift, NX) * width, width), width)
        out = jnp.dot(act[...], down_v[:, cols], preferred_element_type=f32).astype(bf16)
        for r, ref in enumerate(stack_out):
            ref[i] = out[r * rows : (r + 1) * rows]
        for r in range(2 * pairs):
            at = (stacks + r) * rows
            pair_out[i][r] = out[at : at + rows]


def experts(where, gain, stacks, pairs, weights, name):
    rows, width = stacks[0].shape[1:]
    loading = len(weights) == 6
    total = width * NX
    ff = weights[0].shape[-1]
    groups = 1 if pairs else 0
    n = rows * (len(stacks) + 2 * groups)

    def body(*refs):
        expert_kernel(len(stacks), groups, loading, *refs)

    shapes = [v.shape for v in (*stacks, *pairs)]
    if loading:
        shapes += [(2, total, ff), (2, total, ff), (2 * ff, total)]
    return call(
        body,
        [jax.ShapeDtypeStruct(v, bf16) for v in shapes],
        [where, gain, *stacks, *pairs, *weights],
        name,
        [pltpu.VMEM((n, total), bf16), pltpu.VMEM((n, 2 * ff), bf16)]
        + [pltpu.SemaphoreType.DMA((2, 3))] * loading,
        limit=LIMIT,
        scalars=1,
        hbm=6 * loading,
    )


def first_sum_kernel(*refs):
    a_own, a_got, b_own, b_got = refs[0], refs[1], refs[2], refs[3 : 2 + NX]
    a_out, b_out = refs[2 + NX : 2 + 2 * NX], refs[2 + 2 * NX :]
    for i, out in enumerate(a_out):
        out[...] = (a_own[i].astype(f32) + a_got[i].astype(f32)).astype(bf16)
    for r in range(2):
        total = b_own[r].astype(f32)
        for got in b_got:
            total = total + got[r].astype(f32)
        b_out[r][...] = total.astype(bf16)


def last_sum_kernel(*refs):
    parts, back, outs = refs[:NX], refs[NX], refs[NX + 1 :]
    total = parts[0][...].astype(f32)
    for ref in parts[1:]:
        total = total + ref[...].astype(f32)
    total = total.astype(bf16)
    for d, out in enumerate(outs):
        out[:CAP] = total[d * CAP : (d + 1) * CAP]
        out[CAP:] = back[d * CAP : (d + 1) * CAP, :]


def mix_kernel(weight_ref, hid_ref, *refs):
    part_refs, out_ref, held = refs[:NZ], refs[NZ], refs[NZ + 1]
    held[...] = jnp.zeros_like(held)
    for g in range(EXPERTS):
        part = part_refs[(0, 3, 1, 2).index(g // 2)][(g % 2) * CAP : (g % 2 + 1) * CAP, :]
        held[g * PAD : g * PAD + CAP, :] = part.astype(f32)
    mixture = lax.dot_general(
        weight_ref[...],
        held[...],
        (((0,), (0,)), ((), ())),
        precision=lax.Precision.HIGHEST,
        preferred_element_type=f32,
    )
    out_ref[...] = (hid_ref[...].astype(f32) + mixture).astype(bf16)


SWAP = [(0, 1), (1, 0)]


def turn(v, axis, shift):
    n = 4
    return lax.ppermute(v, axis, [(i, (i + shift) % n) for i in range(n)])


def turned(parts, axis, order):
    got = {i: turn(parts[i], axis, SHIFTS[i]) for i in order}
    return [got[i] for i in range(len(parts))]


def together(parts, order):
    got = dict(zip(order, lax.optimization_barrier([parts[i] for i in order])))
    return [got[i] for i in range(len(parts))]


def cross(v):
    return lax.ppermute(v, ("yh", "yl"), [(i, NY - 1 - i) for i in range(NY)])


def swap_y(v):
    return lax.ppermute(v, "yl", SWAP)


def swap_core(v):
    return lax.ppermute(v, "core", SWAP)


def per_device(
    queries, keys, values, cache_keys, cache_values, residual, norm_gain, w_gate, w_up, w_down, expert_ids, gate_weights
):
    rows, width = queries.shape
    heads = width // HEAD_DIM
    z = lax.axis_index("zh")
    y = lax.axis_index(("yh", "yl"))
    where = jnp.stack((z, y, lax.axis_index("core"), lax.axis_index("x"))).astype(jnp.int32)
    ids, gates = expert_ids.T, gate_weights.T
    shaped = lambda *dims: jax.ShapeDtypeStruct(dims, bf16)

    near, past = jnp.stack((keys, values)), jnp.stack((cache_keys, cache_values))
    from_z = turned([jnp.where(z + s < NZ, near, past) for s in SHIFTS], "zh", KV_ORDER)
    slots = EXPERTS * PAD
    q_all, res, table, weight = call(
        prep_kernel,
        [
            shaped(heads * rows, HEAD_DIM),
            shaped(rows, width),
            shaped(slots, rows),
            jax.ShapeDtypeStruct((slots, rows), f32),
        ],
        [where, ids, gates, queries, residual],
        "prep",
        scalars=1,
    )
    packed = call(
        pack_kv_kernel,
        [shaped(2, NZ * rows, HEAD_DIM)] * 4,
        [where, near, past, *[from_z[i] for i in (0, 1, 2)]],
        "pack_kv",
        scalars=1,
    )
    packed, other_gate = lax.optimization_barrier((packed, swap_core(w_gate)))
    held = lax.optimization_barrier((w_up, packed[0]))[0]
    partner = swap_core(packed[3])
    y_1, y_3 = turn(packed[0], ("yh", "yl"), 1), turn(packed[1], ("yh", "yl"), 3)
    state = [jax.ShapeDtypeStruct((heads * rows, HEAD_DIM), f32)] * 3
    carried = call(attend_own_kernel, state, [q_all, near, past, packed[3], partner], "attend_own")
    carried, y_1, y_3, last, other_up = lax.optimization_barrier(
        (carried, y_1, y_3, packed[2], swap_core(held))
    )
    y_2 = turn(last, ("yh", "yl"), 2)
    far_1, far_3 = swap_core(y_1), swap_core(y_3)
    carried = call(attend_more_kernel, state, [q_all, *carried, y_1, y_3, far_1, far_3], "attend_more")
    carried, y_2 = lax.optimization_barrier((carried, y_2))
    far_2 = swap_core(y_2)
    held = lax.optimization_barrier((w_down, far_2))[0]
    own, other = (w_gate, w_up, w_down), (other_gate, other_up, swap_core(held))
    hidden, *sent = call(
        attend_kernel,
        [shaped(rows, width)] + [shaped(2 * CAP, width)] * NZ,
        [q_all, res, table, *carried, y_2, far_2],
        "attend",
        [pltpu.VMEM((heads * rows, HEAD_DIM), f32)],
    )

    arrived = [sent[0]] + turned([sent[s] for s in SHIFTS], "zh", Z_ORDER)
    arrived, other = lax.optimization_barrier((arrived, other))
    rows_a = shaped(NZ * CAP, width)
    a, away = call(merge_kernel, [rows_a] * 2, arrived, "merge")
    b = cross(away)
    b_far = swap_y(b)
    *a_turned, b_far = together(turned([a] * 3, "x", X_ORDER) + [b_far], (0, 1, 2, 3))
    a_own = jnp.stack([a] + a_turned)
    b_pair = jnp.stack((b, b_far))
    *b_turned, a_far = together(turned([b_pair] * 3, "x", X_ORDER) + [swap_y(a_own)], (0, 1, 2, 3))
    gain = norm_gain.reshape(NX, 1, width)
    a_own, *weights = experts(where, gain, [a_own], [], [*own, *other], "experts_own")
    a_far, *b_all = experts(where, gain, [a_far], [b_pair] + b_turned, weights, "experts")

    *b_turned, a_far = lax.optimization_barrier(
        [turn(v, "x", s) for v, s in zip(b_all[1:], SHIFTS)] + [swap_y(a_far)]
    )
    *a_sums, b_own, b_far = call(
        first_sum_kernel, [rows_a] * (NX + 2), [a_own, a_far, b_all[0], *b_turned], "first_sum"
    )
    b_sum = (b_own.astype(f32) + swap_y(b_far).astype(f32)).astype(bf16)
    moved = lax.optimization_barrier(
        [turn(v, "x", s) for v, s in zip(a_sums[1:], SHIFTS)] + [cross(b_sum)]
    )
    result = call(
        last_sum_kernel,
        [shaped(2 * CAP, width)] * NZ,
        [a_sums[0], *moved],
        "last_sum",
    )
    back = turned([result[NZ - s] for s in SHIFTS], "zh", Z_ORDER)
    back = [result[0]] + back
    return call(
        mix_kernel,
        shaped(rows, width),
        [weight, hidden, *back],
        "mix",
        [pltpu.VMEM((EXPERTS * PAD, width), f32)],
    )


def solution(mesh):
    fine = Mesh(mesh.devices.reshape(2, 4, 2, 2, 2, 4), ("dp", "zh", "yh", "yl", "core", "x"))
    ctx = ("zh", "yh", "yl", "core")
    tok = P(("dp",) + ctx, "x")
    in_specs = (
        tok, tok, tok, tok, tok, tok,
        P(),
        P(None, ctx + ("x",)),
        P(None, ctx + ("x",)),
        P(ctx + ("x",), None),
        P(("dp",) + ctx, None),
        P(("dp",) + ctx, None),
    )
    return jax.shard_map(per_device, mesh=fine, in_specs=in_specs, out_specs=tok, check_vma=False)
```

```python
import math

import jax
import jax.numpy as jnp
from jax import lax
from jax.experimental import pallas as pl
from jax.experimental.pallas import tpu as pltpu
from jax.sharding import Mesh, PartitionSpec as P

HEADS = 24
KV_HEADS = 4
HEAD_DIM = 128
EXPERTS = 8
TOP = 2
CAP = 36
PAD = 40
EPS = 1e-05
NZ, NY, NX, NC = 4, 4, 4, 2
SHIFTS = (1, 3, 2)
KV_ORDER, Z_ORDER, X_ORDER = (0, 1, 2), (0, 1, 2), (2, 1, 0)
MB = 1024 * 1024
LIMIT = 13

bf16 = jnp.bfloat16
f32 = jnp.float32
VM = pl.BlockSpec(memory_space=pltpu.VMEM)
SM = pl.BlockSpec(memory_space=pltpu.SMEM)
HBM = pl.BlockSpec(memory_space=pltpu.HBM)


def call(body, out_shape, args, name, scratch=(), limit=16, scalars=0, hbm=0):
    many = isinstance(out_shape, list)
    return pl.pallas_call(
        body,
        out_shape=out_shape,
        in_specs=[SM] * scalars + [VM] * (len(args) - scalars - hbm) + [HBM] * hbm,
        out_specs=[VM] * len(out_shape) if many else VM,
        scratch_shapes=list(scratch),
        compiler_params=pltpu.CompilerParams(vmem_limit_bytes=limit * MB),
        name=name,
    )(*args)


def group_expert(z, yh, g):
    return lax.rem(z + g // 2, NZ) * 2 + lax.rem(yh + g % 2, 2)


def pick_table(z, yh, ids_ref):
    n = ids_ref.shape[1]
    first, second = ids_ref[0:1, :], ids_ref[1:2, :]
    line = lax.broadcasted_iota(jnp.int32, (EXPERTS, n), 0)
    expert = jnp.zeros((EXPERTS, n), jnp.int32)
    for g in range(EXPERTS):
        expert = jnp.where(line == g, group_expert(z, yh, g), expert)
    named = (first == expert) | (second == expert)
    earlier = (
        lax.broadcasted_iota(jnp.int32, (n, n), 0) < lax.broadcasted_iota(jnp.int32, (n, n), 1)
    ).astype(bf16)
    rank = jnp.dot(named.astype(bf16), earlier, preferred_element_type=f32).astype(jnp.int32)
    rank = jnp.where(named, rank, -1)
    row = lax.broadcasted_iota(jnp.int32, (PAD, n), 0)
    return [rank[g : g + 1, :] == row for g in range(EXPERTS)]


def prep_kernel(where_ref, ids_ref, gates_ref, q_ref, res_ref, q_all, res_out, table, weight):
    rows = q_ref.shape[0]
    for h in range(q_ref.shape[1] // HEAD_DIM):
        q_all[h * rows : (h + 1) * rows, :] = q_ref[:, h * HEAD_DIM : (h + 1) * HEAD_DIM]
    res_out[...] = res_ref[...]
    z, yh = where_ref[0], lax.div(where_ref[1], 2)
    picks = pick_table(z, yh, ids_ref)
    table[...] = jnp.concatenate([t.astype(f32) for t in picks], axis=0).astype(bf16)
    for g, pick in enumerate(picks):
        e = group_expert(z, yh, g)
        gate = jnp.where(ids_ref[0:1, :] == e, gates_ref[0:1, :], 0.0)
        gate = gate + jnp.where(ids_ref[1:2, :] == e, gates_ref[1:2, :], 0.0)
        weight[g * PAD : (g + 1) * PAD, :] = jnp.where(pick, gate, 0.0)


def pack_kv_kernel(where_ref, tract, cache, *refs):
    from_z, outs = refs[: NZ - 1], refs[NZ - 1 :]
    n = tract.shape[1]
    y, core = where_ref[1], where_ref[2]
    later = [y + s < NY for s in SHIFTS] + [core == 0]
    for out, is_later in zip(outs, later):
        out[:, 0:n] = jnp.where(is_later, tract[...], cache[...])
        for i, ref in enumerate(from_z):
            out[:, (i + 1) * n : (i + 2) * n] = ref[...]


SCALE = math.log2(math.e) / math.sqrt(HEAD_DIM)
BY_ROWS = (((1,), (1,)), ((), ()))


def attend_piece(q, k, v, m, l, acc):
    s = lax.dot_general(q, k, BY_ROWS, preferred_element_type=f32) * SCALE
    m_new = jnp.maximum(m, jnp.max(s, axis=1, keepdims=True))
    fade = jnp.exp2(m - m_new)
    p = jnp.exp2(s - m_new)
    l = l * fade + jnp.sum(p, axis=1, keepdims=True)
    acc = acc * fade + jnp.dot(p.astype(bf16), v, preferred_element_type=f32)
    return m_new, l, acc


def attend_own_kernel(q_all, tract_ref, cache_ref, *refs):
    kv_refs, (m_ref, l_ref, acc_ref) = refs[:-3], refs[-3:]
    rows = tract_ref.shape[1]
    tile = 2 * rows
    row_at = lax.rem(lax.broadcasted_iota(jnp.int32, (tile, rows), 0), rows)
    col_at = lax.broadcasted_iota(jnp.int32, (tile, rows), 1)
    tract = col_at <= row_at

    def group(g, carry):
        at = pl.ds(pl.multiple_of(g * tile, tile), tile)
        q = q_all[at, :]
        s_tract = lax.dot_general(q, tract_ref[0], BY_ROWS, preferred_element_type=f32)
        s_cache = lax.dot_general(q, cache_ref[0], BY_ROWS, preferred_element_type=f32)
        s = jnp.where(tract, s_tract, s_cache) * SCALE
        m = jnp.max(s, axis=1, keepdims=True)
        p = jnp.exp2(s - m)
        l = jnp.sum(p, axis=1, keepdims=True)
        low = p.astype(bf16)
        zero = jnp.zeros_like(low)
        acc = jnp.dot(jnp.where(tract, low, zero), tract_ref[1], preferred_element_type=f32)
        acc += jnp.dot(jnp.where(tract, zero, low), cache_ref[1], preferred_element_type=f32)
        for i, ref in enumerate(kv_refs):
            keys = slice(0 if i else rows, ref.shape[1])
            m, l, acc = attend_piece(q, ref[0, keys], ref[1, keys], m, l, acc)
        m_ref[at, :] = jnp.broadcast_to(m, acc.shape)
        l_ref[at, :] = jnp.broadcast_to(l, acc.shape)
        acc_ref[at, :] = acc
        return carry

    lax.fori_loop(0, q_all.shape[0] // tile, group, 0)


def attend_more_kernel(q_all, m_ref, l_ref, acc_ref, *refs):
    kv_refs, (m_out, l_out, acc_out) = refs[:-3], refs[-3:]
    tile = 256

    def group(g, carry):
        at = pl.ds(pl.multiple_of(g * tile, tile), tile)
        q = q_all[at, :]
        m, l, acc = m_ref[at, :][:, :1], l_ref[at, :][:, :1], acc_ref[at, :]
        for ref in kv_refs:
            m, l, acc = attend_piece(q, ref[0], ref[1], m, l, acc)
        m_out[at, :] = jnp.broadcast_to(m, acc.shape)
        l_out[at, :] = jnp.broadcast_to(l, acc.shape)
        acc_out[at, :] = acc
        return carry

    lax.fori_loop(0, q_all.shape[0] // tile, group, 0)


def attend_kernel(q_all, res_ref, table, m_ref, l_ref, acc_ref, *refs):
    kv_refs, hid_ref, z_refs, o_all = refs[:NC], refs[NC], refs[NC + 1 : -1], refs[-1]
    rows, width = res_ref.shape
    heads = width // HEAD_DIM
    tile = 2 * rows

    def group(g, carry):
        at = pl.ds(pl.multiple_of(g * tile, tile), tile)
        q = q_all[at, :]
        m, l, acc = m_ref[at, :][:, :1], l_ref[at, :][:, :1], acc_ref[at, :]
        for ref in kv_refs:
            m, l, acc = attend_piece(q, ref[0], ref[1], m, l, acc)
        o_all[at, :] = acc / l
        return carry

    lax.fori_loop(0, heads * rows // tile, group, 0)
    for h in range(heads):
        cols = slice(h * HEAD_DIM, (h + 1) * HEAD_DIM)
        attended = o_all[h * rows : (h + 1) * rows, :]
        hid_ref[:, cols] = (res_ref[:, cols].astype(f32) + attended).astype(bf16)
    routed = jnp.dot(table[...], hid_ref[...], preferred_element_type=f32).astype(bf16)
    for g in range(EXPERTS):
        z_refs[g // 2][(g % 2) * CAP : (g % 2 + 1) * CAP, :] = routed[g * PAD : g * PAD + CAP]


def merge_kernel(*refs):
    keep, away = refs[NZ:]
    for d, ref in zip((0,) + SHIFTS, refs[:NZ]):
        keep[d * CAP : (d + 1) * CAP, :] = ref[:CAP]
        away[d * CAP : (d + 1) * CAP, :] = ref[CAP:]


def expert_kernel(stacks, pairs, loading, where_ref, gain_ref, *refs):
    refs = list(refs)
    take = lambda n: [refs.pop(0) for _ in range(n)]
    stack_in, pair_in = take(stacks), take(NX * pairs)
    weights = take(6 if loading else 3)
    stack_out, pair_out = take(stacks), take(NX * pairs)
    gate_v, up_v, down_v = take(3) if loading else weights
    normed, act = take(2)
    _, total, ff = gate_v.shape
    width = total // NX
    rows = normed.shape[0] // (stacks + 2 * pairs)
    down_loads = []
    if loading:
        sems = refs[0]
        gate_loads, up_loads, down_loads = [
            [pltpu.make_async_copy(weights[3 * h + j], place(h), sems.at[h, j]) for h in range(2)]
            for j, place in enumerate(
                (
                    lambda h: gate_v.at[h],
                    lambda h: up_v.at[h],
                    lambda h: down_v.at[pl.ds(h * ff, ff)],
                )
            )
        ]
        for c in (gate_loads[0], up_loads[0], gate_loads[1], up_loads[1], *down_loads):
            c.start()
    x = where_ref[3]
    order = (0,) + SHIFTS

    def place(r, shift, v, inverse):
        src = lax.rem(x - shift + NX, NX)
        cols = pl.ds(pl.multiple_of(src * width, width), width)
        v = v.astype(f32) * inverse * gain_ref[src]
        normed[r * rows : (r + 1) * rows, cols] = v.astype(bf16)

    def square(v, sq):
        v = v.astype(f32)
        return sq + jnp.sum(v * v, axis=1, keepdims=True)

    for r, ref in enumerate(stack_in):
        sq = lax.fori_loop(0, NX, lambda i, sq: square(ref[i], sq), jnp.zeros((rows, 1), f32))
        inverse = lax.rsqrt(sq * (1.0 / total) + EPS)

        def put(i, carry):
            place(r, i ^ (i >> 1), ref[i], inverse)
            return carry

        lax.fori_loop(0, NX, put, 0)
    for r in range(2 * pairs):
        sq = jnp.zeros((rows, 1), f32)
        for ref in pair_in:
            sq = square(ref[r], sq)
        inverse = lax.rsqrt(sq * (1.0 / total) + EPS)
        for shift, ref in zip(order, pair_in):
            place(stacks + r, shift, ref[r], inverse)

    def hidden_units(half, carry):
        for j, v in enumerate((gate_v, up_v) if loading else ()):
            pltpu.make_async_copy(v.at[half], v.at[half], sems.at[half, j]).wait()
        gate = jnp.dot(normed[...], gate_v[half], preferred_element_type=f32)
        up = jnp.dot(normed[...], up_v[half], preferred_element_type=f32)
        low = (gate / (1.0 + jnp.exp(-gate)) * up).astype(bf16)
        act[:, pl.ds(pl.multiple_of(half * ff, ff), ff)] = low
        return carry

    lax.fori_loop(0, 2, hidden_units, 0)
    for c in down_loads:
        c.wait()
    for i, shift in enumerate(order):
        cols = pl.ds(pl.multiple_of(lax.rem(x + shift, NX) * width, width), width)
        out = jnp.dot(act[...], down_v[:, cols], preferred_element_type=f32).astype(bf16)
        for r, ref in enumerate(stack_out):
            ref[i] = out[r * rows : (r + 1) * rows]
        for r in range(2 * pairs):
            at = (stacks + r) * rows
            pair_out[i][r] = out[at : at + rows]


def experts(where, gain, stacks, pairs, weights, name):
    rows, width = stacks[0].shape[1:]
    loading = len(weights) == 6
    total = width * NX
    ff = weights[0].shape[-1]
    groups = 1 if pairs else 0
    n = rows * (len(stacks) + 2 * groups)

    def body(*refs):
        expert_kernel(len(stacks), groups, loading, *refs)

    shapes = [v.shape for v in (*stacks, *pairs)]
    if loading:
        shapes += [(2, total, ff), (2, total, ff), (2 * ff, total)]
    return call(
        body,
        [jax.ShapeDtypeStruct(v, bf16) for v in shapes],
        [where, gain, *stacks, *pairs, *weights],
        name,
        [pltpu.VMEM((n, total), bf16), pltpu.VMEM((n, 2 * ff), bf16)]
        + [pltpu.SemaphoreType.DMA((2, 3))] * loading,
        limit=LIMIT,
        scalars=1,
        hbm=6 * loading,
    )


def first_sum_kernel(*refs):
    a_own, a_got, b_own, b_got = refs[0], refs[1], refs[2], refs[3 : 2 + NX]
    a_out, b_out = refs[2 + NX : 2 + 2 * NX], refs[2 + 2 * NX :]
    for i, out in enumerate(a_out):
        out[...] = (a_own[i].astype(f32) + a_got[i].astype(f32)).astype(bf16)
    for r in range(2):
        total = b_own[r].astype(f32)
        for got in b_got:
            total = total + got[r].astype(f32)
        b_out[r][...] = total.astype(bf16)


def last_sum_kernel(*refs):
    parts, (back, far), outs = refs[:NX], refs[NX : NX + 2], refs[NX + 2 :]
    total = parts[0][...].astype(f32)
    for ref in parts[1:]:
        total = total + ref[...].astype(f32)
    total = total.astype(bf16)
    crossed = (back[...].astype(f32) + far[...].astype(f32)).astype(bf16)
    for d, out in enumerate(outs):
        out[:CAP] = total[d * CAP : (d + 1) * CAP]
        out[CAP:] = crossed[d * CAP : (d + 1) * CAP]


def mix_kernel(weight_ref, hid_ref, *refs):
    part_refs, out_ref, held = refs[:NZ], refs[NZ], refs[NZ + 1]
    held[...] = jnp.zeros_like(held)
    for g in range(EXPERTS):
        part = part_refs[(0, 3, 1, 2).index(g // 2)][(g % 2) * CAP : (g % 2 + 1) * CAP, :]
        held[g * PAD : g * PAD + CAP, :] = part.astype(f32)
    mixture = lax.dot_general(
        weight_ref[...],
        held[...],
        (((0,), (0,)), ((), ())),
        precision=lax.Precision.HIGHEST,
        preferred_element_type=f32,
    )
    out_ref[...] = (hid_ref[...].astype(f32) + mixture).astype(bf16)


SWAP = [(0, 1), (1, 0)]


def turn(v, axis, shift):
    n = 4
    return lax.ppermute(v, axis, [(i, (i + shift) % n) for i in range(n)])


def turned(parts, axis, order):
    got = {i: turn(parts[i], axis, SHIFTS[i]) for i in order}
    return [got[i] for i in range(len(parts))]


def together(parts, order):
    got = dict(zip(order, lax.optimization_barrier([parts[i] for i in order])))
    return [got[i] for i in range(len(parts))]


def cross(v):
    return lax.ppermute(v, ("yh", "yl"), [(i, NY - 1 - i) for i in range(NY)])


def swap_y(v):
    return lax.ppermute(v, "yl", SWAP)


def swap_core(v):
    return lax.ppermute(v, "core", SWAP)


def per_device(
    queries, keys, values, cache_keys, cache_values, residual, norm_gain, w_gate, w_up, w_down, expert_ids, gate_weights
):
    rows, width = queries.shape
    heads = width // HEAD_DIM
    z = lax.axis_index("zh")
    y = lax.axis_index(("yh", "yl"))
    where = jnp.stack((z, y, lax.axis_index("core"), lax.axis_index("x"))).astype(jnp.int32)
    ids, gates = expert_ids.T, gate_weights.T
    shaped = lambda *dims: jax.ShapeDtypeStruct(dims, bf16)

    near, past = jnp.stack((keys, values)), jnp.stack((cache_keys, cache_values))
    from_z = turned([jnp.where(z + s < NZ, near, past) for s in SHIFTS], "zh", KV_ORDER)
    slots = EXPERTS * PAD
    (keys, values), (cache_keys, cache_values) = lax.optimization_barrier(
        ((keys, values), (cache_keys, cache_values))
    )
    near, past = jnp.stack((keys, values)), jnp.stack((cache_keys, cache_values))
    q_all, res, table, weight = call(
        prep_kernel,
        [
            shaped(heads * rows, HEAD_DIM),
            shaped(rows, width),
            shaped(slots, rows),
            jax.ShapeDtypeStruct((slots, rows), f32),
        ],
        [where, ids, gates, queries, residual],
        "prep",
        scalars=1,
    )
    packed = call(
        pack_kv_kernel,
        [shaped(2, NZ * rows, HEAD_DIM)] * 4,
        [where, near, past, *[from_z[i] for i in (0, 1, 2)]],
        "pack_kv",
        scalars=1,
    )
    packed, other_gate = lax.optimization_barrier((packed, swap_core(w_gate)))
    held = lax.optimization_barrier((w_up, packed[0]))[0]
    partner = swap_core(packed[3])
    y_1, y_3 = turn(packed[0], ("yh", "yl"), 1), turn(packed[1], ("yh", "yl"), 3)
    state = [jax.ShapeDtypeStruct((heads * rows, HEAD_DIM), f32)] * 3
    carried = call(attend_own_kernel, state, [q_all, near, past, packed[3], partner], "attend_own")
    carried, y_1, y_3, last, other_up = lax.optimization_barrier(
        (carried, y_1, y_3, packed[2], swap_core(held))
    )
    y_2 = turn(last, ("yh", "yl"), 2)
    far_1, far_3 = swap_core(y_1), swap_core(y_3)
    carried = call(attend_more_kernel, state, [q_all, *carried, y_1, y_3, far_1, far_3], "attend_more")
    carried, y_2 = lax.optimization_barrier((carried, y_2))
    far_2 = swap_core(y_2)
    held = lax.optimization_barrier((w_down, far_2))[0]
    own, other = (w_gate, w_up, w_down), (other_gate, other_up, swap_core(held))
    hidden, *sent = call(
        attend_kernel,
        [shaped(rows, width)] + [shaped(2 * CAP, width)] * NZ,
        [q_all, res, table, *carried, y_2, far_2],
        "attend",
        [pltpu.VMEM((heads * rows, HEAD_DIM), f32)],
    )

    arrived = [sent[0]] + turned([sent[s] for s in SHIFTS], "zh", Z_ORDER)
    arrived, other = lax.optimization_barrier((arrived, other))
    rows_a = shaped(NZ * CAP, width)
    a, away = call(merge_kernel, [rows_a] * 2, arrived, "merge")
    b = cross(away)
    b_far = swap_y(b)
    *a_turned, b_far = together(turned([a] * 3, "x", X_ORDER) + [b_far], (0, 1, 2, 3))
    a_own = jnp.stack([a] + a_turned)
    b_pair = jnp.stack((b, b_far))
    *b_turned, a_far = together(turned([b_pair] * 3, "x", X_ORDER) + [swap_y(a_own)], (0, 1, 2, 3))
    gain = norm_gain.reshape(NX, 1, width)
    a_own, *weights = experts(where, gain, [a_own], [], [*own, *other], "experts_own")
    a_far, *b_all = experts(where, gain, [a_far], [b_pair] + b_turned, weights, "experts")

    *b_turned, a_far = lax.optimization_barrier(
        [turn(v, "x", s) for v, s in zip(b_all[1:], SHIFTS)] + [swap_y(a_far)]
    )
    *a_sums, b_own, b_far = call(
        first_sum_kernel, [rows_a] * (NX + 2), [a_own, a_far, b_all[0], *b_turned], "first_sum"
    )
    moved = lax.optimization_barrier(
        [turn(v, "x", s) for v, s in zip(a_sums[1:], SHIFTS)]
        + [cross(b_own), turn(b_far, ("yh", "yl"), 2)]
    )
    result = call(
        last_sum_kernel,
        [shaped(2 * CAP, width)] * NZ,
        [a_sums[0], *moved],
        "last_sum",
    )
    back = turned([result[NZ - s] for s in SHIFTS], "zh", Z_ORDER)
    back = [result[0]] + back
    return call(
        mix_kernel,
        shaped(rows, width),
        [weight, hidden, *back],
        "mix",
        [pltpu.VMEM((EXPERTS * PAD, width), f32)],
    )


def solution(mesh):
    fine = Mesh(mesh.devices.reshape(2, 4, 2, 2, 2, 4), ("dp", "zh", "yh", "yl", "core", "x"))
    ctx = ("zh", "yh", "yl", "core")
    tok = P(("dp",) + ctx, "x")
    in_specs = (
        tok, tok, tok, tok, tok, tok,
        P(),
        P(None, ctx + ("x",)),
        P(None, ctx + ("x",)),
        P(ctx + ("x",), None),
        P(("dp",) + ctx, None),
        P(("dp",) + ctx, None),
    )
    return jax.shard_map(per_device, mesh=fine, in_specs=in_specs, out_specs=tok, check_vma=False)
```

```python
import math

import jax
import jax.numpy as jnp
from jax import lax
from jax.experimental import pallas as pl
from jax.experimental.pallas import tpu as pltpu
from jax.sharding import Mesh, PartitionSpec as P

HEADS = 24
KV_HEADS = 4
HEAD_DIM = 128
EXPERTS = 8
TOP = 2
CAP = 36
PAD = 40
EPS = 1e-05
NZ, NY, NX, NC = 4, 4, 4, 2
SHIFTS = (1, 3, 2)
KV_ORDER, Z_ORDER, X_ORDER = (0, 1, 2), (0, 1, 2), (2, 1, 0)
MB = 1024 * 1024
LIMIT = 13

bf16 = jnp.bfloat16
f32 = jnp.float32
VM = pl.BlockSpec(memory_space=pltpu.VMEM)
SM = pl.BlockSpec(memory_space=pltpu.SMEM)
HBM = pl.BlockSpec(memory_space=pltpu.HBM)


def call(body, out_shape, args, name, scratch=(), limit=16, scalars=0, hbm=0):
    many = isinstance(out_shape, list)
    return pl.pallas_call(
        body,
        out_shape=out_shape,
        in_specs=[SM] * scalars + [VM] * (len(args) - scalars - hbm) + [HBM] * hbm,
        out_specs=[VM] * len(out_shape) if many else VM,
        scratch_shapes=list(scratch),
        compiler_params=pltpu.CompilerParams(vmem_limit_bytes=limit * MB),
        name=name,
    )(*args)


def group_expert(z, yh, g):
    return lax.rem(z + g // 2, NZ) * 2 + lax.rem(yh + g % 2, 2)


def pick_table(z, yh, ids_ref):
    n = ids_ref.shape[1]
    first, second = ids_ref[0:1, :], ids_ref[1:2, :]
    line = lax.broadcasted_iota(jnp.int32, (EXPERTS, n), 0)
    expert = jnp.zeros((EXPERTS, n), jnp.int32)
    for g in range(EXPERTS):
        expert = jnp.where(line == g, group_expert(z, yh, g), expert)
    named = (first == expert) | (second == expert)
    earlier = (
        lax.broadcasted_iota(jnp.int32, (n, n), 0) < lax.broadcasted_iota(jnp.int32, (n, n), 1)
    ).astype(bf16)
    rank = jnp.dot(named.astype(bf16), earlier, preferred_element_type=f32).astype(jnp.int32)
    rank = jnp.where(named, rank, -1)
    row = lax.broadcasted_iota(jnp.int32, (PAD, n), 0)
    return [rank[g : g + 1, :] == row for g in range(EXPERTS)]


def prep_kernel(where_ref, ids_ref, gates_ref, q_ref, res_ref, q_all, res_out, table, weight):
    rows = q_ref.shape[0]
    for h in range(q_ref.shape[1] // HEAD_DIM):
        q_all[h * rows : (h + 1) * rows, :] = q_ref[:, h * HEAD_DIM : (h + 1) * HEAD_DIM]
    res_out[...] = res_ref[...]
    z, yh = where_ref[0], lax.div(where_ref[1], 2)
    picks = pick_table(z, yh, ids_ref)
    table[...] = jnp.concatenate([t.astype(f32) for t in picks], axis=0).astype(bf16)
    for g, pick in enumerate(picks):
        e = group_expert(z, yh, g)
        gate = jnp.where(ids_ref[0:1, :] == e, gates_ref[0:1, :], 0.0)
        gate = gate + jnp.where(ids_ref[1:2, :] == e, gates_ref[1:2, :], 0.0)
        weight[g * PAD : (g + 1) * PAD, :] = jnp.where(pick, gate, 0.0)


def pack_kv_kernel(where_ref, tract, cache, *refs):
    from_z, outs = refs[: NZ - 1], refs[NZ - 1 :]
    n = tract.shape[1]
    y, core = where_ref[1], where_ref[2]
    later = [y + s < NY for s in SHIFTS] + [core == 0]
    for out, is_later in zip(outs, later):
        out[:, 0:n] = jnp.where(is_later, tract[...], cache[...])
        for i, ref in enumerate(from_z):
            out[:, (i + 1) * n : (i + 2) * n] = ref[...]


SCALE = math.log2(math.e) / math.sqrt(HEAD_DIM)
BY_ROWS = (((1,), (1,)), ((), ()))


def attend_piece(q, k, v, m, l, acc):
    s = lax.dot_general(q, k, BY_ROWS, preferred_element_type=f32) * SCALE
    m_new = jnp.maximum(m, jnp.max(s, axis=1, keepdims=True))
    fade = jnp.exp2(m - m_new)
    p = jnp.exp2(s - m_new)
    l = l * fade + jnp.sum(p, axis=1, keepdims=True)
    acc = acc * fade + jnp.dot(p.astype(bf16), v, preferred_element_type=f32)
    return m_new, l, acc


def attend_own_kernel(q_all, tract_ref, cache_ref, *refs):
    kv_refs, (m_ref, l_ref, acc_ref) = refs[:-3], refs[-3:]
    rows = tract_ref.shape[1]
    tile = 2 * rows
    row_at = lax.rem(lax.broadcasted_iota(jnp.int32, (tile, rows), 0), rows)
    col_at = lax.broadcasted_iota(jnp.int32, (tile, rows), 1)
    tract = col_at <= row_at

    def group(g, carry):
        at = pl.ds(pl.multiple_of(g * tile, tile), tile)
        q = q_all[at, :]
        s_tract = lax.dot_general(q, tract_ref[0], BY_ROWS, preferred_element_type=f32)
        s_cache = lax.dot_general(q, cache_ref[0], BY_ROWS, preferred_element_type=f32)
        s = jnp.where(tract, s_tract, s_cache) * SCALE
        m = jnp.max(s, axis=1, keepdims=True)
        p = jnp.exp2(s - m)
        l = jnp.sum(p, axis=1, keepdims=True)
        low = p.astype(bf16)
        zero = jnp.zeros_like(low)
        acc = jnp.dot(jnp.where(tract, low, zero), tract_ref[1], preferred_element_type=f32)
        acc += jnp.dot(jnp.where(tract, zero, low), cache_ref[1], preferred_element_type=f32)
        for i, ref in enumerate(kv_refs):
            keys = slice(0 if i else rows, ref.shape[1])
            m, l, acc = attend_piece(q, ref[0, keys], ref[1, keys], m, l, acc)
        m_ref[at, :] = jnp.broadcast_to(m, acc.shape)
        l_ref[at, :] = jnp.broadcast_to(l, acc.shape)
        acc_ref[at, :] = acc
        return carry

    lax.fori_loop(0, q_all.shape[0] // tile, group, 0)


def attend_more_kernel(q_all, m_ref, l_ref, acc_ref, *refs):
    kv_refs, (m_out, l_out, acc_out) = refs[:-3], refs[-3:]
    tile = 256

    def group(g, carry):
        at = pl.ds(pl.multiple_of(g * tile, tile), tile)
        q = q_all[at, :]
        m, l, acc = m_ref[at, :][:, :1], l_ref[at, :][:, :1], acc_ref[at, :]
        for ref in kv_refs:
            m, l, acc = attend_piece(q, ref[0], ref[1], m, l, acc)
        m_out[at, :] = jnp.broadcast_to(m, acc.shape)
        l_out[at, :] = jnp.broadcast_to(l, acc.shape)
        acc_out[at, :] = acc
        return carry

    lax.fori_loop(0, q_all.shape[0] // tile, group, 0)


def attend_kernel(q_all, res_ref, table, m_ref, l_ref, acc_ref, *refs):
    kv_refs, hid_ref, z_refs, o_all = refs[:NC], refs[NC], refs[NC + 1 : -1], refs[-1]
    rows, width = res_ref.shape
    heads = width // HEAD_DIM
    tile = 2 * rows

    def group(g, carry):
        at = pl.ds(pl.multiple_of(g * tile, tile), tile)
        q = q_all[at, :]
        m, l, acc = m_ref[at, :][:, :1], l_ref[at, :][:, :1], acc_ref[at, :]
        for ref in kv_refs:
            m, l, acc = attend_piece(q, ref[0], ref[1], m, l, acc)
        o_all[at, :] = acc / l
        return carry

    lax.fori_loop(0, heads * rows // tile, group, 0)
    for h in range(heads):
        cols = slice(h * HEAD_DIM, (h + 1) * HEAD_DIM)
        attended = o_all[h * rows : (h + 1) * rows, :]
        hid_ref[:, cols] = (res_ref[:, cols].astype(f32) + attended).astype(bf16)
    routed = jnp.dot(table[...], hid_ref[...], preferred_element_type=f32).astype(bf16)
    for g in range(EXPERTS):
        z_refs[g // 2][(g % 2) * CAP : (g % 2 + 1) * CAP, :] = routed[g * PAD : g * PAD + CAP]


def merge_kernel(*refs):
    keep, away = refs[NZ:]
    for d, ref in zip((0,) + SHIFTS, refs[:NZ]):
        keep[d * CAP : (d + 1) * CAP, :] = ref[:CAP]
        away[d * CAP : (d + 1) * CAP, :] = ref[CAP:]


def expert_kernel(stacks, pairs, loading, where_ref, gain_ref, *refs):
    refs = list(refs)
    take = lambda n: [refs.pop(0) for _ in range(n)]
    stack_in, pair_in = take(stacks), take(NX * pairs)
    weights = take(6 if loading else 3)
    stack_out, pair_out = take(stacks), take(NX * pairs)
    gate_v, up_v, down_v = take(3) if loading else weights
    normed, act = take(2)
    _, total, ff = gate_v.shape
    width = total // NX
    rows = normed.shape[0] // (stacks + 2 * pairs)
    down_loads = []
    if loading:
        sems = refs[0]
        gate_loads, up_loads, down_loads = [
            [pltpu.make_async_copy(weights[3 * h + j], place(h), sems.at[h, j]) for h in range(2)]
            for j, place in enumerate(
                (
                    lambda h: gate_v.at[h],
                    lambda h: up_v.at[h],
                    lambda h: down_v.at[pl.ds(h * ff, ff)],
                )
            )
        ]
        for c in (gate_loads[0], up_loads[0], gate_loads[1], up_loads[1], *down_loads):
            c.start()
    x = where_ref[3]
    order = (0,) + SHIFTS

    def place(r, shift, v, inverse):
        src = lax.rem(x - shift + NX, NX)
        cols = pl.ds(pl.multiple_of(src * width, width), width)
        v = v.astype(f32) * inverse * gain_ref[src]
        normed[r * rows : (r + 1) * rows, cols] = v.astype(bf16)

    def square(v, sq):
        v = v.astype(f32)
        return sq + jnp.sum(v * v, axis=1, keepdims=True)

    for r, ref in enumerate(stack_in):
        sq = lax.fori_loop(0, NX, lambda i, sq: square(ref[i], sq), jnp.zeros((rows, 1), f32))
        inverse = lax.rsqrt(sq * (1.0 / total) + EPS)

        def put(i, carry):
            place(r, i ^ (i >> 1), ref[i], inverse)
            return carry

        lax.fori_loop(0, NX, put, 0)
    for r in range(2 * pairs):
        sq = jnp.zeros((rows, 1), f32)
        for ref in pair_in:
            sq = square(ref[r], sq)
        inverse = lax.rsqrt(sq * (1.0 / total) + EPS)
        for shift, ref in zip(order, pair_in):
            place(stacks + r, shift, ref[r], inverse)

    def hidden_units(half, carry):
        for j, v in enumerate((gate_v, up_v) if loading else ()):
            pltpu.make_async_copy(v.at[half], v.at[half], sems.at[half, j]).wait()
        gate = jnp.dot(normed[...], gate_v[half], preferred_element_type=f32)
        up = jnp.dot(normed[...], up_v[half], preferred_element_type=f32)
        low = (gate / (1.0 + jnp.exp(-gate)) * up).astype(bf16)
        act[:, pl.ds(pl.multiple_of(half * ff, ff), ff)] = low
        return carry

    lax.fori_loop(0, 2, hidden_units, 0)
    for c in down_loads:
        c.wait()
    for i, shift in enumerate(order):
        cols = pl.ds(pl.multiple_of(lax.rem(x + shift, NX) * width, width), width)
        out = jnp.dot(act[...], down_v[:, cols], preferred_element_type=f32).astype(bf16)
        for r, ref in enumerate(stack_out):
            ref[i] = out[r * rows : (r + 1) * rows]
        for r in range(2 * pairs):
            at = (stacks + r) * rows
            pair_out[i][r] = out[at : at + rows]


def experts(where, gain, stacks, pairs, weights, name):
    rows, width = stacks[0].shape[1:]
    loading = len(weights) == 6
    total = width * NX
    ff = weights[0].shape[-1]
    groups = 1 if pairs else 0
    n = rows * (len(stacks) + 2 * groups)

    def body(*refs):
        expert_kernel(len(stacks), groups, loading, *refs)

    shapes = [v.shape for v in (*stacks, *pairs)]
    if loading:
        shapes += [(2, total, ff), (2, total, ff), (2 * ff, total)]
    return call(
        body,
        [jax.ShapeDtypeStruct(v, bf16) for v in shapes],
        [where, gain, *stacks, *pairs, *weights],
        name,
        [pltpu.VMEM((n, total), bf16), pltpu.VMEM((n, 2 * ff), bf16)]
        + [pltpu.SemaphoreType.DMA((2, 3))] * loading,
        limit=LIMIT,
        scalars=1,
        hbm=6 * loading,
    )


def first_sum_kernel(*refs):
    a_own, a_got, b_own, b_got = refs[0], refs[1], refs[2], refs[3 : 2 + NX]
    a_out, b_out = refs[2 + NX : 2 + 2 * NX], refs[2 + 2 * NX :]
    for i, out in enumerate(a_out):
        out[...] = (a_own[i].astype(f32) + a_got[i].astype(f32)).astype(bf16)
    for r in range(2):
        total = b_own[r].astype(f32)
        for got in b_got:
            total = total + got[r].astype(f32)
        b_out[r][...] = total.astype(bf16)


def last_sum_kernel(*refs):
    parts, back, outs = refs[:NX], refs[NX], refs[NX + 1 :]
    total = parts[0][...].astype(f32)
    for ref in parts[1:]:
        total = total + ref[...].astype(f32)
    total = total.astype(bf16)
    for d, out in enumerate(outs):
        out[:CAP] = total[d * CAP : (d + 1) * CAP]
        out[CAP:] = back[d * CAP : (d + 1) * CAP, :]


def mix_kernel(weight_ref, hid_ref, *refs):
    part_refs, out_ref, held = refs[:NZ], refs[NZ], refs[NZ + 1]
    held[...] = jnp.zeros_like(held)
    for g in range(EXPERTS):
        part = part_refs[(0, 3, 1, 2).index(g // 2)][(g % 2) * CAP : (g % 2 + 1) * CAP, :]
        held[g * PAD : g * PAD + CAP, :] = part.astype(f32)
    mixture = lax.dot_general(
        weight_ref[...],
        held[...],
        (((0,), (0,)), ((), ())),
        precision=lax.Precision.HIGHEST,
        preferred_element_type=f32,
    )
    out_ref[...] = (hid_ref[...].astype(f32) + mixture).astype(bf16)


SWAP = [(0, 1), (1, 0)]


def turn(v, axis, shift):
    n = 4
    return lax.ppermute(v, axis, [(i, (i + shift) % n) for i in range(n)])


def turned(parts, axis, order):
    got = {i: turn(parts[i], axis, SHIFTS[i]) for i in order}
    return [got[i] for i in range(len(parts))]


def together(parts, order):
    got = dict(zip(order, lax.optimization_barrier([parts[i] for i in order])))
    return [got[i] for i in range(len(parts))]


def cross(v):
    return lax.ppermute(v, ("yh", "yl"), [(i, NY - 1 - i) for i in range(NY)])


def swap_y(v):
    return lax.ppermute(v, "yl", SWAP)


def swap_core(v):
    return lax.ppermute(v, "core", SWAP)


def per_device(
    queries, keys, values, cache_keys, cache_values, residual, norm_gain, w_gate, w_up, w_down, expert_ids, gate_weights
):
    rows, width = queries.shape
    heads = width // HEAD_DIM
    z = lax.axis_index("zh")
    y = lax.axis_index(("yh", "yl"))
    where = jnp.stack((z, y, lax.axis_index("core"), lax.axis_index("x"))).astype(jnp.int32)
    ids, gates = expert_ids.T, gate_weights.T
    shaped = lambda *dims: jax.ShapeDtypeStruct(dims, bf16)

    near, past = jnp.stack((keys, values)), jnp.stack((cache_keys, cache_values))
    from_z = turned([jnp.where(z + s < NZ, near, past) for s in SHIFTS], "zh", KV_ORDER)
    slots = EXPERTS * PAD
    (keys, values), (cache_keys, cache_values) = lax.optimization_barrier(
        ((keys, values), (cache_keys, cache_values))
    )
    near, past = jnp.stack((keys, values)), jnp.stack((cache_keys, cache_values))
    q_all, res, table, weight = call(
        prep_kernel,
        [
            shaped(heads * rows, HEAD_DIM),
            shaped(rows, width),
            shaped(slots, rows),
            jax.ShapeDtypeStruct((slots, rows), f32),
        ],
        [where, ids, gates, queries, residual],
        "prep",
        scalars=1,
    )
    packed = call(
        pack_kv_kernel,
        [shaped(2, NZ * rows, HEAD_DIM)] * 4,
        [where, near, past, *[from_z[i] for i in (0, 1, 2)]],
        "pack_kv",
        scalars=1,
    )
    packed, other_gate = lax.optimization_barrier((packed, swap_core(w_gate)))
    held = lax.optimization_barrier((w_up, packed[0]))[0]
    partner = swap_core(packed[3])
    y_1, y_3 = turn(packed[0], ("yh", "yl"), 1), turn(packed[1], ("yh", "yl"), 3)
    state = [jax.ShapeDtypeStruct((heads * rows, HEAD_DIM), f32)] * 3
    carried = call(attend_own_kernel, state, [q_all, near, past, packed[3], partner], "attend_own")
    carried, y_1, y_3, last, other_up = lax.optimization_barrier(
        (carried, y_1, y_3, packed[2], swap_core(held))
    )
    y_2 = turn(last, ("yh", "yl"), 2)
    far_1, far_3 = swap_core(y_1), swap_core(y_3)
    carried = call(attend_more_kernel, state, [q_all, *carried, y_1, y_3, far_1, far_3], "attend_more")
    carried, y_2 = lax.optimization_barrier((carried, y_2))
    far_2 = swap_core(y_2)
    held = lax.optimization_barrier((w_down, far_2))[0]
    own, other = (w_gate, w_up, w_down), (other_gate, other_up, swap_core(held))
    hidden, *sent = call(
        attend_kernel,
        [shaped(rows, width)] + [shaped(2 * CAP, width)] * NZ,
        [q_all, res, table, *carried, y_2, far_2],
        "attend",
        [pltpu.VMEM((heads * rows, HEAD_DIM), f32)],
    )

    arrived = [sent[0]] + turned([sent[s] for s in SHIFTS], "zh", Z_ORDER)
    arrived, other = lax.optimization_barrier((arrived, other))
    rows_a = shaped(NZ * CAP, width)
    a, away = call(merge_kernel, [rows_a] * 2, arrived, "merge")
    b = cross(away)
    b_far = swap_y(b)
    *a_turned, b_far = together(turned([a] * 3, "x", X_ORDER) + [b_far], (0, 1, 2, 3))
    a_own = jnp.stack([a] + a_turned)
    b_pair = jnp.stack((b, b_far))
    *b_turned, a_far = together(turned([b_pair] * 3, "x", X_ORDER) + [swap_y(a_own)], (0, 1, 2, 3))
    gain = norm_gain.reshape(NX, 1, width)
    a_own, *weights = experts(where, gain, [a_own], [], [*own, *other], "experts_own")
    a_far, *b_all = experts(where, gain, [a_far], [b_pair] + b_turned, weights, "experts")

    *b_turned, a_far = lax.optimization_barrier(
        [turn(v, "x", s) for v, s in zip(b_all[1:], SHIFTS)] + [swap_y(a_far)]
    )
    *a_sums, b_own, b_far = call(
        first_sum_kernel, [rows_a] * (NX + 2), [a_own, a_far, b_all[0], *b_turned], "first_sum"
    )
    b_sum = (b_own.astype(f32) + swap_y(b_far).astype(f32)).astype(bf16)
    moved = lax.optimization_barrier(
        [turn(v, "x", s) for v, s in zip(a_sums[1:], SHIFTS)] + [cross(b_sum)]
    )
    result = call(
        last_sum_kernel,
        [shaped(2 * CAP, width)] * NZ,
        [a_sums[0], *moved],
        "last_sum",
    )
    back = turned([result[NZ - s] for s in SHIFTS], "zh", Z_ORDER)
    back = [result[0]] + back
    return call(
        mix_kernel,
        shaped(rows, width),
        [weight, hidden, *back],
        "mix",
        [pltpu.VMEM((EXPERTS * PAD, width), f32)],
    )


def solution(mesh):
    fine = Mesh(mesh.devices.reshape(2, 4, 2, 2, 2, 4), ("dp", "zh", "yh", "yl", "core", "x"))
    ctx = ("zh", "yh", "yl", "core")
    tok = P(("dp",) + ctx, "x")
    in_specs = (
        tok, tok, tok, tok, tok, tok,
        P(),
        P(None, ctx + ("x",)),
        P(None, ctx + ("x",)),
        P(ctx + ("x",), None),
        P(("dp",) + ctx, None),
        P(("dp",) + ctx, None),
    )
    return jax.shard_map(per_device, mesh=fine, in_specs=in_specs, out_specs=tok, check_vma=False)
```
